256 devices in a mesh: req: 32 (over z, y), mdl: 8 (over x, core).
Axes of the slice: x: 4, y: 4, z: 8, core: 2. Of those that a mesh axis runs over, the one named last changes fastest.
Arguments:
- stream: bfloat16 [24576, 1792], P('req'), may hold values from -6 to 6
- attention_projection_weight: bfloat16 [3, 1792, 1792], P(None, 'mdl'), may hold values from -0.125 to 0.125
- head_output_weight: bfloat16 [1792, 1792], P('mdl'), may hold values from -0.125 to 0.125
- adapter_down_maps: bfloat16 [64, 1792, 16], P('mdl'), may hold values from -0.125 to 0.125
- adapter_up_maps: bfloat16 [2, 1792, 1024], P(None, 'mdl'), may hold values from -1.5 to 1.5
- tenant_adapter_scale: float32 [4], replicated, may hold values from 0.5 to 2
- feedforward_norm_gain: bfloat16 [1792], replicated, may hold values from 0.099609375 to 1.8984375
- feedforward_weight: bfloat16 [3, 1792, 4864], P(None, 'req', 'mdl'), may hold values from -0.125 to 0.125
- prefix_cache_store: bfloat16 [1024, 2, 1792, 128], P('req', None, 'mdl'), may hold values from -140 to 140
- token_adapter_index: int32 [24576], P('req'), may hold values from 0 to 63
- request_token_lengths: int32 [32, 24], P('req'), may hold values from 1 to 192, 768 in all within a row
- request_tenant_index: int32 [768], P('req'), may hold values from 0 to 3
- last_page_holder: int32 [768, 1], replicated, may hold values from 0 to 31; in each aligned block of 24 rows (0 to 23, 24 to 47, ...) at most 2 rows name the same one
- holder_page_slot: int32 [768], replicated, may hold values from 0 to 31
- page_filled_rows: int32 [768], replicated, may hold values from 64 to 128
Outputs:
- layer_out: bfloat16 [24576, 1792], P(('req', 'mdl'))
The draws below stay inside these ranges and needn't reach their ends.
Inputs may be any that keep to these rules, and one draw needn't show every extreme that they name: `last_page_holder`: within the rows of one index of req (aligned blocks of 24 rows) no holder is named more than 2 times, and one holder exactly 2 times in some blocks. `request_token_lengths`: each row sums to 768; its longest request has exactly 192 tokens.
All inputs are finite; a program needn't handle non-finite values.
Results may differ from the reference program's by a relative error of at most 0.025.
Values may be sent and summed in bfloat16 or wider, within the bound.
A program may use at most 128 MiB of HBM per device.

```python
import math
import jax
import jax.numpy as jnp
import numpy as np
from jax import lax

MODEL_DIMENSION = 1792
ATTENTION_HEADS = 16
HEAD_SIZE = 112
FF = 4864
WINDOW = 64
PAGE = 128
ADAPTER_RANK = 16
ADAPTER_TOTAL = 64
TENANTS = 4
TOKEN_SLOTS = 768
REQ_DEV = 24
POOL_DEV = 32
MOST_LEN = 192
CAP = 2
TOKENS = 24576
REQS = 768
POOLS = 1024
N_REQ = 32
N_MDL = 8


def draw_prefix_cache_store(key, part):
    array_shape = (POOLS, 2, ATTENTION_HEADS * HEAD_SIZE, PAGE)
    return jax.random.truncated_normal(jax.random.fold_in(key, 73), -6.0, 6.0, array_shape, jnp.float32).astype(jnp.bfloat16)


def with_ends(entries, rng, low, high):
    shape = entries.shape
    spot = [jax.random.randint(jax.random.fold_in(rng, axis), (), 0, shape[axis]) for axis in range(len(shape))]
    entries = entries.at[tuple(spot)].set(low)
    longest = shape.index(max(shape))
    spot[longest] = (spot[longest] + 1) % shape[longest]
    return entries.at[tuple(spot)].set(high)


def block_scale(own_key, extent, shards, low, top_value):
    def one(axis_at, blocks):
        steps = jax.random.uniform(jax.random.fold_in(jax.random.fold_in(own_key, 6), axis_at), (blocks,), jnp.float32, low / len(shards), top_value / len(shards))
        return jnp.repeat(jnp.exp(steps), extent[axis_at] // blocks).reshape((-1,) + (1,) * (len(extent) - axis_at - 1))

    level = one(*shards[0])
    for cut in shards[1:]:
        level = level * one(*cut)
    return level


def profile(count, total, reach, slope):
    weights = [(1 << 20) // math.isqrt(standing ** slope) + 1 for standing in range(2, count + 1)]
    rest, counts = total - reach - (count - 1), [1] * (count - 1)
    while rest > 0:
        movable = [i for i in range(count - 1) if counts[i] < reach]
        mass, remaining = sum([weights[i] for i in movable]), rest
        for i in movable:
            addition = min(reach - counts[i], max(1, remaining * weights[i] // mass), rest)
            counts[i] = counts[i] + addition
            rest = rest - addition
    return np.array([reach] + counts)


def ragged_sizes(key, count, total, bound, slope):
    if count == 2:
        one = jax.random.randint(key, (), max(1, total - bound), min(bound, total - 1) + 1)
        return jnp.stack([one, total - one])
    tallies = jnp.asarray(profile(count, total, bound, slope), jnp.int32)
    twos = (count - 1) // 2
    donor, sink = tallies[1:1 + 2 * twos:2], tallies[2:2 + 2 * twos:2]
    slack = jnp.minimum(donor - 1, bound - sink)
    moved = jax.random.randint(jax.random.fold_in(key, 1), (twos,), 0, 1 << 20) % (slack + 1)
    tallies = tallies.at[1:1 + 2 * twos:2].set(donor - moved).at[2:2 + 2 * twos:2].set(sink + moved)
    return tallies[jax.random.permutation(jax.random.fold_in(key, 2), count)]


def deal_out(own_key, own, number, rows, number_of, top, bound, lean):
    sequence = jax.random.permutation(own_key, number_of)
    crowded, ordinary = shares(number_of, rows * top, bound, lean, True), shares(number_of, rows * top, bound, lean, False)
    places = jnp.arange(number_of)

    def named(lengths, rotation):
        used = int((lengths > 0).sum())
        fixed = max(1, used // 4)
        passed = fixed + (places - fixed + rotation * (used - fixed)) % max(1, number_of - fixed)
        return jnp.zeros((number_of,), jnp.int32).at[sequence[jnp.where(places < fixed, places, passed)]].set(jnp.asarray(lengths, jnp.int32))

    lengths = jnp.where(number % 4 == 0, named(crowded, number // 4), named(ordinary, number - number // 4 - 1))
    mixed = jax.random.permutation(jax.random.fold_in(own, 3), number_of)
    giver, receiver = mixed[0:number_of // 2 * 2:2], mixed[1:number_of // 2 * 2:2]
    slack = jnp.minimum(lengths[giver] - 1, bound - lengths[receiver]) // 2
    slack = jnp.where((giver == sequence[0]) | (receiver == sequence[0]) | (lengths[receiver] == 0), 0, jnp.maximum(slack, 0))
    passed = jax.random.randint(jax.random.fold_in(own, 4), (number_of // 2,), 0, 1 << 20) % (slack + 1)
    lengths = lengths.at[giver].add(-passed).at[receiver].add(passed)
    labels = jnp.searchsorted(jnp.cumsum(lengths), jnp.arange(rows * top), side="right").astype(jnp.int32)
    listing = labels.reshape(top, rows).T
    listing = listing[jax.random.permutation(jax.random.fold_in(own, 1), rows)]
    rotation = jax.random.randint(jax.random.fold_in(own, 2), (rows, 1), 0, top)
    return jnp.take_along_axis(listing, (jnp.arange(top)[None, :] + rotation) % top, axis=1)


def shares(number_of, total, bound, lean, full):
    loads = [(1 << 20) // math.isqrt(rank ** lean) + 1 for rank in range(1, number_of + 1)]
    largest = bound if full else min(bound, max(-(-total // number_of), total * loads[0] // sum(loads)))
    least = 1 if total - largest >= number_of - 1 else 0
    counts, rest = [largest] + [least] * (number_of - 1), total - largest - least * (number_of - 1)
    while rest > 0:
        free = [i for i in range(1, number_of) if counts[i] < largest] or [i for i in range(1, number_of) if counts[i] < bound]
        mass, remaining = sum([loads[i] for i in free]), rest
        for i in free:
            extra = min(bound - counts[i], max(1, remaining * loads[i] // mass), rest)
            counts[i] = counts[i] + extra
            rest = rest - extra
    return np.array(counts)


def centred(stream_key, extent, width, bound, cuts=(), kind=jnp.bfloat16):
    array = jax.random.normal(stream_key, extent, jnp.float32) * width
    if len(cuts) > 0:
        array = block_scale(stream_key, extent, cuts, -0.22, 0.18) * array
    return jnp.clip(array, min=-bound, max=bound).astype(kind)


def setup_inputs(seed: int = 0) -> dict:
    key_list = jax.random.split(jax.random.key(seed), 16)
    stream = centred(key_list[0], (TOKENS, MODEL_DIMENSION), 1.0, 6.0, ((0, 32),))
    attention_projection_weight = centred(key_list[1], (3, ATTENTION_HEADS * HEAD_SIZE, MODEL_DIMENSION), MODEL_DIMENSION ** -0.5, 0.125, ((1, 8),))
    head_output_weight = centred(key_list[2], (ATTENTION_HEADS * HEAD_SIZE, MODEL_DIMENSION), (ATTENTION_HEADS * HEAD_SIZE) ** -0.5, 0.125, ((0, 8),))
    adapter_down_maps = centred(key_list[3], (ADAPTER_TOTAL, MODEL_DIMENSION, ADAPTER_RANK), MODEL_DIMENSION ** -0.5, 0.125, ((0, 8),))
    adapter_up_maps = centred(key_list[4], (2, ATTENTION_HEADS * HEAD_SIZE, ADAPTER_TOTAL * ADAPTER_RANK), ADAPTER_RANK ** -0.5, 1.5, ((1, 8),))
    tenant_adapter_scale = jnp.clip(jnp.exp(jax.random.uniform(key_list[5], (TENANTS,), jnp.float32, math.log(0.5), math.log(2.0))), 0.5, 2.0)
    feedforward_norm_gain = jnp.clip(1.0 + 0.18 * jax.random.normal(key_list[6], (MODEL_DIMENSION,), jnp.float32), 0.099609375, 1.8984375).astype(jnp.bfloat16)
    feedforward_weight = centred(key_list[7], (3, MODEL_DIMENSION, FF), MODEL_DIMENSION ** -0.5, 0.125, ((1, 32), (2, 8)))
    prefix_cache_store = draw_prefix_cache_store(jax.random.fold_in(key_list[15], 71), 0)
    token_adapter_index = with_ends(jax.random.randint(key_list[9], (TOKENS,), 0, ADAPTER_TOTAL), jax.random.fold_in(key_list[9], 1), 0, ADAPTER_TOTAL - 1).astype(jnp.int32)
    request_token_lengths = jax.vmap(lambda own: ragged_sizes(own, REQ_DEV, TOKEN_SLOTS, MOST_LEN, 2))(jax.random.split(key_list[10], N_REQ)).reshape((N_REQ, REQ_DEV)).astype(jnp.int32)
    request_tenant_index = with_ends(jax.random.randint(key_list[11], (REQS,), 0, TENANTS), jax.random.fold_in(key_list[11], 1), 0, TENANTS - 1).astype(jnp.int32)
    last_page_holder_keys = jax.random.split(jax.random.fold_in(key_list[12], 1), REQS // REQ_DEV)
    last_page_holder_turns = jax.random.permutation(jax.random.fold_in(key_list[12], 3), REQS // REQ_DEV)
    last_page_holder = jax.vmap(lambda own, number: deal_out(jax.random.fold_in(key_list[12], 2), own, number, REQ_DEV, N_REQ, 1, CAP, 2))(last_page_holder_keys, last_page_holder_turns).reshape((REQS, 1))
    holder_page_slot = with_ends(jax.random.randint(key_list[13], (REQS,), 0, POOL_DEV), jax.random.fold_in(key_list[13], 1), 0, POOL_DEV - 1).astype(jnp.int32)
    page_filled_rows = with_ends(jax.random.randint(key_list[14], (REQS,), WINDOW, PAGE + 1), jax.random.fold_in(key_list[14], 1), WINDOW, PAGE).astype(jnp.int32)
    return dict(stream=stream, attention_projection_weight=attention_projection_weight, head_output_weight=head_output_weight, adapter_down_maps=adapter_down_maps, adapter_up_maps=adapter_up_maps, tenant_adapter_scale=tenant_adapter_scale, feedforward_norm_gain=feedforward_norm_gain, feedforward_weight=feedforward_weight, prefix_cache_store=prefix_cache_store, token_adapter_index=token_adapter_index, request_token_lengths=request_token_lengths, request_tenant_index=request_tenant_index, last_page_holder=last_page_holder, holder_page_slot=holder_page_slot, page_filled_rows=page_filled_rows)


def fetch_rows(prefix_cache_store, page_index, fill_rows):
    zero_index = jnp.zeros((), jnp.int32)
    block_rows = lax.dynamic_slice(prefix_cache_store, (page_index, zero_index, zero_index, fill_rows - WINDOW), (1, 2, ATTENTION_HEADS * HEAD_SIZE, WINDOW))
    return jnp.transpose(block_rows[0], (2, 0, 1))

def reference(stream, attention_projection_weight, head_output_weight, adapter_down_maps, adapter_up_maps, tenant_adapter_scale, feedforward_norm_gain, feedforward_weight, prefix_cache_store, token_adapter_index, request_token_lengths, request_tenant_index, last_page_holder, holder_page_slot, page_filled_rows):
    head_column_set = ATTENTION_HEADS * HEAD_SIZE
    owners = last_page_holder[:, 0].astype(jnp.int32)
    page_index = (owners * POOL_DEV + holder_page_slot).astype(jnp.int32)
    prefix_all = jax.vmap(lambda one_page, fill_rows: fetch_rows(prefix_cache_store, one_page, fill_rows))(page_index, page_filled_rows.astype(jnp.int32))
    down_flattened = jnp.transpose(adapter_down_maps, (1, 0, 2)).reshape(MODEL_DIMENSION, ADAPTER_TOTAL * ADAPTER_RANK)
    up_flattened = jnp.transpose(adapter_up_maps.reshape(2 * head_column_set, ADAPTER_TOTAL * ADAPTER_RANK))
    attn_f32 = attention_projection_weight.astype(jnp.float32)
    out_groups = head_output_weight.astype(jnp.float32).reshape(N_MDL, head_column_set // N_MDL, MODEL_DIMENSION)
    down_groups = feedforward_weight[2].astype(jnp.float32).reshape(MODEL_DIMENSION, N_MDL, FF // N_MDL)
    inv_scale = 1.0 / math.sqrt(HEAD_SIZE)

    def group_layer(group):
        first_row = group * TOKEN_SLOTS
        tokens = lax.dynamic_slice_in_dim(stream, first_row, TOKEN_SLOTS, 0)
        tok_adapters = lax.dynamic_slice_in_dim(token_adapter_index, first_row, TOKEN_SLOTS, 0)
        lengths_row = lax.dynamic_slice_in_dim(request_token_lengths, group, 1, 0)[0]
        tenants = lax.dynamic_slice_in_dim(request_tenant_index, group * REQ_DEV, REQ_DEV, 0)
        prefix = lax.dynamic_slice_in_dim(prefix_all, group * REQ_DEV, REQ_DEV, 0)
        projected_rows = jnp.einsum('td,kcd->ktc', tokens.astype(jnp.float32), attn_f32)
        onehot = tok_adapters[:, None] == jnp.arange(ADAPTER_TOTAL, dtype=jnp.int32)[None, :]
        rank_all = jnp.dot(tokens, down_flattened, preferred_element_type=jnp.float32).reshape(TOKEN_SLOTS, ADAPTER_TOTAL, ADAPTER_RANK)
        rank_feat = lax.optimization_barrier(jnp.sum(rank_all * onehot.astype(jnp.float32)[:, :, None], axis=1)).astype(jnp.bfloat16)
        broadcast_result = (onehot.astype(jnp.bfloat16)[:, :, None] * rank_feat[:, None, :]).reshape(TOKEN_SLOTS, ADAPTER_TOTAL * ADAPTER_RANK)
        adapter_column_set = jnp.dot(broadcast_result, up_flattened, preferred_element_type=jnp.float32).reshape(TOKEN_SLOTS, 2, head_column_set)
        positions = jnp.arange(TOKEN_SLOTS, dtype=jnp.int32)
        starts = jnp.cumsum(lengths_row) - lengths_row
        member = (positions[:, None] >= starts[None, :]) & (positions[:, None] < (starts + lengths_row)[None, :])
        member_int = member.astype(jnp.int32)
        request_of = lax.optimization_barrier(jnp.sum(member_int * jnp.arange(REQ_DEV, dtype=jnp.int32)[None, :], axis=1))
        relative = positions - lax.optimization_barrier(jnp.sum(member_int * starts[None, :], axis=1))
        request_scale = tenant_adapter_scale[tenants]
        per_token_scale = lax.optimization_barrier(jnp.sum(member.astype(jnp.float32) * request_scale[None, :], axis=1))[:, None]
        query_rows = (projected_rows[0] + per_token_scale * adapter_column_set[:, 0]).astype(jnp.bfloat16)
        key_rows = projected_rows[1].astype(jnp.bfloat16)
        value_row_block = (projected_rows[2] + per_token_scale * adapter_column_set[:, 1]).astype(jnp.bfloat16)
        key_all = jnp.concatenate([key_rows, prefix[:, :, 0].reshape(REQ_DEV * WINDOW, head_column_set)], axis=0)
        value_all = jnp.concatenate([value_row_block, prefix[:, :, 1].reshape(REQ_DEV * WINDOW, head_column_set)], axis=0)
        distance = positions[:, None] - positions[None, :]
        local_ok = (request_of[:, None] == request_of[None, :]) & (distance >= 0) & (distance <= WINDOW)
        key_request = jnp.repeat(jnp.arange(REQ_DEV, dtype=jnp.int32), WINDOW)
        key_offset = jnp.tile(jnp.arange(WINDOW, dtype=jnp.int32), REQ_DEV)
        prefix_ok = (request_of[:, None] == key_request[None, :]) & (key_offset[None, :] >= relative[:, None])
        allowed = jnp.concatenate([local_ok, prefix_ok], axis=1)
        query_heads = query_rows.astype(jnp.float32).reshape(TOKEN_SLOTS, ATTENTION_HEADS, HEAD_SIZE)
        key_heads = key_all.astype(jnp.float32).reshape(-1, ATTENTION_HEADS, HEAD_SIZE)
        value_heads = value_all.astype(jnp.float32).reshape(-1, ATTENTION_HEADS, HEAD_SIZE)
        scores = jnp.einsum('thd,shd->hts', query_heads, key_heads) * inv_scale
        masked = jnp.where(allowed[None], scores, -1e+30)
        row_max = lax.optimization_barrier(jnp.max(masked, axis=-1, keepdims=True))
        exp_scores = jnp.exp(masked - row_max)
        weights = (exp_scores / lax.optimization_barrier(jnp.sum(exp_scores, axis=-1, keepdims=True))).astype(jnp.bfloat16)
        mixed = jnp.einsum('hts,shd->thd', weights.astype(jnp.float32), value_heads).astype(jnp.bfloat16)
        mixed_groups = mixed.reshape(TOKEN_SLOTS, N_MDL, head_column_set // N_MDL).astype(jnp.float32)
        attn_parts = jnp.einsum('tgc,gcd->gtd', mixed_groups, out_groups).astype(jnp.bfloat16)
        attn = lax.optimization_barrier(jnp.sum(attn_parts.astype(jnp.float32), axis=0))
        resid = (tokens.astype(jnp.float32) + attn).astype(jnp.bfloat16)
        resid32 = resid.astype(jnp.float32)
        mean_sq = lax.optimization_barrier(jnp.mean(resid32 * resid32, axis=1, keepdims=True))
        normed = (resid32 * lax.rsqrt(mean_sq + 1e-06) * feedforward_norm_gain.astype(jnp.float32)[None, :]).astype(jnp.bfloat16)
        gate_part = jnp.dot(normed, feedforward_weight[0], preferred_element_type=jnp.float32)
        up_part = jnp.dot(normed, feedforward_weight[1], preferred_element_type=jnp.float32)
        hidden = (jax.nn.silu(gate_part) * up_part).astype(jnp.bfloat16)
        hidden_groups = hidden.reshape(TOKEN_SLOTS, N_MDL, FF // N_MDL).astype(jnp.float32)
        mlp_parts = jnp.einsum('tgf,dgf->gtd', hidden_groups, down_groups).astype(jnp.bfloat16)
        mlp_sum = lax.optimization_barrier(jnp.sum(mlp_parts.astype(jnp.float32), axis=0))
        return (resid32 + mlp_sum).astype(jnp.bfloat16)
    outputs = lax.map(group_layer, jnp.arange(N_REQ, dtype=jnp.int32))
    return outputs.reshape(N_REQ * TOKEN_SLOTS, MODEL_DIMENSION)
```

```python
import math

import jax
import jax.numpy as jnp
from jax import lax
from jax.sharding import PartitionSpec as P

HEAD_SIZE = 112
WINDOW = 64


def per_device(
    stream,
    attention_projection_weight,
    head_output_weight,
    adapter_down_maps,
    adapter_up_maps,
    tenant_adapter_scale,
    feedforward_norm_gain,
    feedforward_weight,
    prefix_cache_store,
    token_adapter_index,
    request_token_lengths,
    request_tenant_index,
    last_page_holder,
    holder_page_slot,
    page_filled_rows,
):
    tok_count, model_width = stream.shape
    head_column_set = attention_projection_weight.shape[1]
    head_local = head_column_set // HEAD_SIZE
    req_per_dev = request_token_lengths.shape[1]
    rank_total_width = adapter_down_maps.shape[2]
    adapter_number = adapter_up_maps.shape[2] // rank_total_width
    req_devices = lax.axis_size("req")
    req_index = lax.axis_index("req")
    mdl_index = lax.axis_index("mdl")
    row_share = tok_count // lax.axis_size("mdl")
    cap_slots = max(2, (req_per_dev + req_devices - 1) // req_devices + 1)
    projected_rows = jnp.einsum(
        "td,kcd->ktc", stream, attention_projection_weight, preferred_element_type=jnp.float32
    )
    all_onehot = (
        token_adapter_index[:, None] == jnp.arange(adapter_number, dtype=jnp.int32)[None, :]
    )
    holder_count = adapter_down_maps.shape[0]
    holder_rank_rows = jnp.einsum(
        "qf,kfn->qkn", stream, adapter_down_maps, preferred_element_type=jnp.float32
    )
    held_onehot = (
        token_adapter_index[:, None]
        == (mdl_index * holder_count + jnp.arange(holder_count, dtype=jnp.int32))[None, :]
    )
    rank_part = jnp.sum(holder_rank_rows * held_onehot.astype(jnp.float32)[:, :, None], axis=1)
    rank_feat = lax.psum(rank_part.astype(jnp.bfloat16), "mdl")
    broadcast_result = (
        all_onehot.astype(jnp.bfloat16)[:, :, None] * rank_feat[:, None, :]
    ).reshape(tok_count, adapter_number * rank_total_width)
    adapter_column_set = jnp.einsum(
        "iu,pdu->ipd", broadcast_result, adapter_up_maps, preferred_element_type=jnp.float32
    )
    positions = jnp.arange(tok_count, dtype=jnp.int32)
    lengths_row = request_token_lengths[0]
    starts = jnp.cumsum(lengths_row) - lengths_row
    member = (positions[:, None] >= starts[None, :]) & (
        positions[:, None] < (starts + lengths_row)[None, :]
    )
    member_int = member.astype(jnp.int32)
    request_of = jnp.sum(member_int * jnp.arange(req_per_dev, dtype=jnp.int32)[None, :], axis=1)
    relative = positions - jnp.sum(member_int * starts[None, :], axis=1)
    tenant_hot = (
        request_tenant_index[:, None]
        == jnp.arange(tenant_adapter_scale.shape[0], dtype=jnp.int32)[None, :]
    ).astype(jnp.float32)
    request_scale = jnp.sum(tenant_hot * tenant_adapter_scale[None, :], axis=1)
    per_token_scale = jnp.sum(member.astype(jnp.float32) * request_scale[None, :], axis=1)[:, None]
    query_rows = (projected_rows[0] + per_token_scale * adapter_column_set[:, 0]).astype(
        jnp.bfloat16
    )
    key_rows = projected_rows[1].astype(jnp.bfloat16)
    value_row_block = (projected_rows[2] + per_token_scale * adapter_column_set[:, 1]).astype(
        jnp.bfloat16
    )
    owner_column = last_page_holder[:, 0]
    owner_table = owner_column.reshape(req_devices, req_per_dev)
    slot_table = holder_page_slot.reshape(req_devices, req_per_dev)
    owned = (owner_table == req_index).astype(jnp.int32)
    owned_rank = jnp.cumsum(owned, axis=1) - 1
    picked = owned[:, None, :] * (
        owned_rank[:, None, :] == jnp.arange(cap_slots, dtype=jnp.int32)[None, :, None]
    ).astype(jnp.int32)
    send_slot = jnp.sum(picked * slot_table[:, None, :], axis=2)
    fill_table = page_filled_rows.reshape(req_devices, req_per_dev)
    send_fill = jnp.sum(picked * fill_table[:, None, :], axis=2)
    my_owner = lax.dynamic_slice_in_dim(owner_column, req_index * req_per_dev, req_per_dev, 0)
    order_ids = jnp.arange(req_per_dev, dtype=jnp.int32)
    earlier = (my_owner[:, None] == my_owner[None, :]) & (order_ids[:, None] > order_ids[None, :])
    flat_pick = my_owner * cap_slots + jnp.sum(earlier.astype(jnp.int32), axis=1)
    page_inner = prefix_cache_store.shape[1:3]

    def cut_window(slot, fill):
        return lax.dynamic_slice(
            prefix_cache_store, (slot, 0, 0, fill - WINDOW), (1,) + page_inner + (WINDOW,)
        )[0]

    source_pages = jax.vmap(cut_window)(send_slot.reshape(-1), send_fill.reshape(-1))
    source_pages = source_pages.reshape((req_devices, cap_slots) + page_inner + (WINDOW,))
    arrived = lax.all_to_all(source_pages, "req", split_axis=0, concat_axis=0, tiled=True)
    chosen = jnp.take(
        arrived.reshape((req_devices * cap_slots,) + page_inner + (WINDOW,)),
        flat_pick,
        axis=0,
        mode="clip",
    )
    prefix = jnp.transpose(chosen, (0, 3, 1, 2))
    key_all = jnp.concatenate(
        [key_rows, prefix[:, :, 0].reshape(req_per_dev * WINDOW, head_column_set)], axis=0
    )
    value_all = jnp.concatenate(
        [value_row_block, prefix[:, :, 1].reshape(req_per_dev * WINDOW, head_column_set)], axis=0
    )
    distance = positions[:, None] - positions[None, :]
    local_ok = (request_of[:, None] == request_of[None, :]) & (distance >= 0) & (distance <= WINDOW)
    key_request = jnp.repeat(jnp.arange(req_per_dev, dtype=jnp.int32), WINDOW)
    key_offset = jnp.tile(jnp.arange(WINDOW, dtype=jnp.int32), req_per_dev)
    prefix_ok = (request_of[:, None] == key_request[None, :]) & (
        key_offset[None, :] >= relative[:, None]
    )
    allowed = jnp.concatenate([local_ok, prefix_ok], axis=1)
    query_heads = query_rows.reshape(tok_count, head_local, HEAD_SIZE)
    key_heads = key_all.reshape(-1, head_local, HEAD_SIZE)
    value_heads = value_all.reshape(-1, head_local, HEAD_SIZE)
    scores = jnp.einsum(
        "thd,shd->hts", query_heads, key_heads, preferred_element_type=jnp.float32
    ) * (1.0 / math.sqrt(HEAD_SIZE))
    masked = jnp.where(allowed[None], scores, -1e30)
    row_max = jnp.max(masked, axis=-1, keepdims=True)
    exp_scores = jnp.exp(masked - row_max)
    weights = (exp_scores / jnp.sum(exp_scores, axis=-1, keepdims=True)).astype(jnp.bfloat16)
    mixed = (
        jnp.einsum("hts,shd->thd", weights, value_heads, preferred_element_type=jnp.float32)
        .astype(jnp.bfloat16)
        .reshape(tok_count, head_column_set)
    )
    attn_part = (
        jnp.dot(mixed, head_output_weight, preferred_element_type=jnp.float32)
        .astype(jnp.bfloat16)
        .astype(jnp.float32)
    )
    gain_wide = feedforward_norm_gain.astype(jnp.float32)[None, :]
    attn_full = lax.psum(attn_part.astype(jnp.bfloat16), "mdl").astype(jnp.float32)
    resid_full = (stream.astype(jnp.float32) + attn_full).astype(jnp.bfloat16)
    resid_wide = resid_full.astype(jnp.float32)
    mean_sq = jnp.mean(resid_wide * resid_wide, axis=1, keepdims=True)
    normed = (resid_wide * lax.rsqrt(mean_sq + 1e-06) * gain_wide).astype(jnp.bfloat16)
    resid_mine = lax.dynamic_slice_in_dim(resid_full, mdl_index * row_share, row_share, 0)
    full_mlp = lax.all_gather(feedforward_weight, "req", axis=1, tiled=True)
    gate_part = jnp.dot(normed, full_mlp[0], preferred_element_type=jnp.float32)
    up_part = jnp.dot(normed, full_mlp[1], preferred_element_type=jnp.float32)
    hidden = (jax.nn.silu(gate_part) * up_part).astype(jnp.bfloat16)
    mlp_part = (
        jnp.einsum("tf,df->td", hidden, full_mlp[2], preferred_element_type=jnp.float32)
        .astype(jnp.bfloat16)
        .astype(jnp.float32)
    )
    mlp_mine = lax.psum_scatter(
        mlp_part.astype(jnp.bfloat16), "mdl", scatter_dimension=0, tiled=True
    ).astype(jnp.float32)
    return (resid_mine.astype(jnp.float32) + mlp_mine).astype(jnp.bfloat16)


def solution(mesh):
    return jax.shard_map(
        per_device,
        mesh=mesh,
        in_specs=(
            P("req", None),
            P(None, "mdl", None),
            P("mdl", None),
            P("mdl", None, None),
            P(None, "mdl", None),
            P(),
            P(),
            P(None, "req", "mdl"),
            P("req", None, "mdl", None),
            P("req"),
            P("req", None),
            P("req"),
            P(),
            P(),
            P(),
        ),
        out_specs=P(("req", "mdl"), None),
        check_vma=False,
    )
```

```python
import math

import jax
import jax.numpy as jnp
from jax import lax
from jax.sharding import PartitionSpec as P

HEAD_SIZE = 112
WINDOW = 64


def per_device(
    stream,
    attention_projection_weight,
    head_output_weight,
    adapter_down_maps,
    adapter_up_maps,
    tenant_adapter_scale,
    feedforward_norm_gain,
    feedforward_weight,
    prefix_cache_store,
    token_adapter_index,
    request_token_lengths,
    request_tenant_index,
    last_page_holder,
    holder_page_slot,
    page_filled_rows,
):
    tok_count, model_width = stream.shape
    head_column_set = attention_projection_weight.shape[1]
    head_local = head_column_set // HEAD_SIZE
    req_per_dev = request_token_lengths.shape[1]
    rank_total_width = adapter_down_maps.shape[2]
    adapter_number = adapter_up_maps.shape[2] // rank_total_width
    req_devices = lax.axis_size("req")
    req_index = lax.axis_index("req")
    mdl_index = lax.axis_index("mdl")
    row_share = tok_count // lax.axis_size("mdl")
    cap_slots = max(2, (req_per_dev + req_devices - 1) // req_devices + 1)
    projected_rows = jnp.einsum(
        "td,kcd->ktc", stream, attention_projection_weight, preferred_element_type=jnp.float32
    )
    all_onehot = (
        token_adapter_index[:, None] == jnp.arange(adapter_number, dtype=jnp.int32)[None, :]
    )
    holder_count = adapter_down_maps.shape[0]
    holder_rank_rows = jnp.einsum(
        "qf,kfn->qkn", stream, adapter_down_maps, preferred_element_type=jnp.float32
    )
    held_onehot = (
        token_adapter_index[:, None]
        == (mdl_index * holder_count + jnp.arange(holder_count, dtype=jnp.int32))[None, :]
    )
    rank_part = jnp.sum(holder_rank_rows * held_onehot.astype(jnp.float32)[:, :, None], axis=1)
    rank_feat = lax.psum(rank_part.astype(jnp.bfloat16), "mdl")
    broadcast_result = (
        all_onehot.astype(jnp.bfloat16)[:, :, None] * rank_feat[:, None, :]
    ).reshape(tok_count, adapter_number * rank_total_width)
    adapter_column_set = jnp.einsum(
        "iu,pdu->ipd", broadcast_result, adapter_up_maps, preferred_element_type=jnp.float32
    )
    positions = jnp.arange(tok_count, dtype=jnp.int32)
    lengths_row = request_token_lengths[0]
    starts = jnp.cumsum(lengths_row) - lengths_row
    member = (positions[:, None] >= starts[None, :]) & (
        positions[:, None] < (starts + lengths_row)[None, :]
    )
    member_int = member.astype(jnp.int32)
    request_of = jnp.sum(member_int * jnp.arange(req_per_dev, dtype=jnp.int32)[None, :], axis=1)
    relative = positions - jnp.sum(member_int * starts[None, :], axis=1)
    tenant_hot = (
        request_tenant_index[:, None]
        == jnp.arange(tenant_adapter_scale.shape[0], dtype=jnp.int32)[None, :]
    ).astype(jnp.float32)
    request_scale = jnp.sum(tenant_hot * tenant_adapter_scale[None, :], axis=1)
    per_token_scale = jnp.sum(member.astype(jnp.float32) * request_scale[None, :], axis=1)[:, None]
    query_rows = (projected_rows[0] + per_token_scale * adapter_column_set[:, 0]).astype(
        jnp.bfloat16
    )
    key_rows = projected_rows[1].astype(jnp.bfloat16)
    value_row_block = (projected_rows[2] + per_token_scale * adapter_column_set[:, 1]).astype(
        jnp.bfloat16
    )
    owner_column = last_page_holder[:, 0]
    owner_table = owner_column.reshape(req_devices, req_per_dev)
    slot_table = holder_page_slot.reshape(req_devices, req_per_dev)
    owned = (owner_table == req_index).astype(jnp.int32)
    owned_rank = jnp.cumsum(owned, axis=1) - 1
    picked = owned[:, None, :] * (
        owned_rank[:, None, :] == jnp.arange(cap_slots, dtype=jnp.int32)[None, :, None]
    ).astype(jnp.int32)
    send_slot = jnp.sum(picked * slot_table[:, None, :], axis=2)
    fill_table = page_filled_rows.reshape(req_devices, req_per_dev)
    send_fill = jnp.sum(picked * fill_table[:, None, :], axis=2)
    my_owner = lax.dynamic_slice_in_dim(owner_column, req_index * req_per_dev, req_per_dev, 0)
    order_ids = jnp.arange(req_per_dev, dtype=jnp.int32)
    earlier = (my_owner[:, None] == my_owner[None, :]) & (order_ids[:, None] > order_ids[None, :])
    flat_pick = my_owner * cap_slots + jnp.sum(earlier.astype(jnp.int32), axis=1)
    page_inner = prefix_cache_store.shape[1:3]

    def cut_window(slot, fill):
        return lax.dynamic_slice(
            prefix_cache_store, (slot, 0, 0, fill - WINDOW), (1,) + page_inner + (WINDOW,)
        )[0]

    source_pages = jax.vmap(cut_window)(send_slot.reshape(-1), send_fill.reshape(-1))
    source_pages = source_pages.reshape((req_devices, cap_slots) + page_inner + (WINDOW,))
    arrived = lax.all_to_all(source_pages, "req", split_axis=0, concat_axis=0, tiled=True)
    full_mlp = lax.all_gather(feedforward_weight, "req", axis=1, tiled=True)
    full_mlp, arrived = lax.optimization_barrier((full_mlp, arrived))
    chosen = jnp.take(
        arrived.reshape((req_devices * cap_slots,) + page_inner + (WINDOW,)),
        flat_pick,
        axis=0,
        mode="clip",
    )
    prefix = jnp.transpose(chosen, (0, 3, 1, 2))
    key_all = jnp.concatenate(
        [key_rows, prefix[:, :, 0].reshape(req_per_dev * WINDOW, head_column_set)], axis=0
    )
    value_all = jnp.concatenate(
        [value_row_block, prefix[:, :, 1].reshape(req_per_dev * WINDOW, head_column_set)], axis=0
    )
    distance = positions[:, None] - positions[None, :]
    local_ok = (request_of[:, None] == request_of[None, :]) & (distance >= 0) & (distance <= WINDOW)
    key_request = jnp.repeat(jnp.arange(req_per_dev, dtype=jnp.int32), WINDOW)
    key_offset = jnp.tile(jnp.arange(WINDOW, dtype=jnp.int32), req_per_dev)
    prefix_ok = (request_of[:, None] == key_request[None, :]) & (
        key_offset[None, :] >= relative[:, None]
    )
    allowed = jnp.concatenate([local_ok, prefix_ok], axis=1)
    query_heads = query_rows.reshape(tok_count, head_local, HEAD_SIZE)
    key_heads = key_all.reshape(-1, head_local, HEAD_SIZE)
    value_heads = value_all.reshape(-1, head_local, HEAD_SIZE)
    scores = jnp.einsum(
        "thd,shd->hts", query_heads, key_heads, preferred_element_type=jnp.float32
    ) * (1.0 / math.sqrt(HEAD_SIZE))
    masked = jnp.where(allowed[None], scores, -1e30)
    row_max = jnp.max(masked, axis=-1, keepdims=True)
    exp_scores = jnp.exp(masked - row_max)
    weights = (exp_scores / jnp.sum(exp_scores, axis=-1, keepdims=True)).astype(jnp.bfloat16)
    mixed = (
        jnp.einsum("hts,shd->thd", weights, value_heads, preferred_element_type=jnp.float32)
        .astype(jnp.bfloat16)
        .reshape(tok_count, head_column_set)
    )
    attn_part = (
        jnp.dot(mixed, head_output_weight, preferred_element_type=jnp.float32)
        .astype(jnp.bfloat16)
        .astype(jnp.float32)
    )
    gain_wide = feedforward_norm_gain.astype(jnp.float32)[None, :]
    attn_full = lax.psum(attn_part.astype(jnp.bfloat16), "mdl").astype(jnp.float32)
    resid_full = (stream.astype(jnp.float32) + attn_full).astype(jnp.bfloat16)
    resid_wide = resid_full.astype(jnp.float32)
    mean_sq = jnp.mean(resid_wide * resid_wide, axis=1, keepdims=True)
    normed = (resid_wide * lax.rsqrt(mean_sq + 1e-06) * gain_wide).astype(jnp.bfloat16)
    resid_mine = lax.dynamic_slice_in_dim(resid_full, mdl_index * row_share, row_share, 0)
    gate_part = jnp.dot(normed, full_mlp[0], preferred_element_type=jnp.float32)
    up_part = jnp.dot(normed, full_mlp[1], preferred_element_type=jnp.float32)
    hidden = (jax.nn.silu(gate_part) * up_part).astype(jnp.bfloat16)
    mlp_part = (
        jnp.einsum("tf,df->td", hidden, full_mlp[2], preferred_element_type=jnp.float32)
        .astype(jnp.bfloat16)
        .astype(jnp.float32)
    )
    mlp_mine = lax.psum_scatter(
        mlp_part.astype(jnp.bfloat16), "mdl", scatter_dimension=0, tiled=True
    ).astype(jnp.float32)
    return (resid_mine.astype(jnp.float32) + mlp_mine).astype(jnp.bfloat16)


def solution(mesh):
    return jax.shard_map(
        per_device,
        mesh=mesh,
        in_specs=(
            P("req", None),
            P(None, "mdl", None),
            P("mdl", None),
            P("mdl", None, None),
            P(None, "mdl", None),
            P(),
            P(),
            P(None, "req", "mdl"),
            P("req", None, "mdl", None),
            P("req"),
            P("req", None),
            P("req"),
            P(),
            P(),
            P(),
        ),
        out_specs=P(("req", "mdl"), None),
        check_vma=False,
    )
```

```python
import math

import jax
import jax.numpy as jnp
from jax import lax
from jax.sharding import PartitionSpec as P

HEAD_SIZE = 112
WINDOW = 64


def per_device(
    stream,
    attention_projection_weight,
    head_output_weight,
    adapter_down_maps,
    adapter_up_maps,
    tenant_adapter_scale,
    feedforward_norm_gain,
    feedforward_weight,
    prefix_cache_store,
    token_adapter_index,
    request_token_lengths,
    request_tenant_index,
    last_page_holder,
    holder_page_slot,
    page_filled_rows,
):
    tok_count, model_width = stream.shape
    head_column_set = attention_projection_weight.shape[1]
    head_local = head_column_set // HEAD_SIZE
    req_per_dev = request_token_lengths.shape[1]
    rank_total_width = adapter_down_maps.shape[2]
    adapter_number = adapter_up_maps.shape[2] // rank_total_width
    req_devices = lax.axis_size("req")
    req_index = lax.axis_index("req")
    mdl_index = lax.axis_index("mdl")
    row_share = tok_count // lax.axis_size("mdl")
    cap_slots = max(2, (req_per_dev + req_devices - 1) // req_devices + 1)
    projected_rows = jnp.einsum(
        "td,kcd->ktc", stream, attention_projection_weight, preferred_element_type=jnp.float32
    )
    all_onehot = (
        token_adapter_index[:, None] == jnp.arange(adapter_number, dtype=jnp.int32)[None, :]
    )
    holder_count = adapter_down_maps.shape[0]
    holder_rank_rows = jnp.einsum(
        "qf,kfn->qkn", stream, adapter_down_maps, preferred_element_type=jnp.float32
    )
    held_onehot = (
        token_adapter_index[:, None]
        == (mdl_index * holder_count + jnp.arange(holder_count, dtype=jnp.int32))[None, :]
    )
    rank_part = jnp.sum(holder_rank_rows * held_onehot.astype(jnp.float32)[:, :, None], axis=1)
    rank_feat = lax.psum(rank_part.astype(jnp.bfloat16), "mdl")
    broadcast_result = (
        all_onehot.astype(jnp.bfloat16)[:, :, None] * rank_feat[:, None, :]
    ).reshape(tok_count, adapter_number * rank_total_width)
    adapter_column_set = jnp.einsum(
        "iu,pdu->ipd", broadcast_result, adapter_up_maps, preferred_element_type=jnp.float32
    )
    positions = jnp.arange(tok_count, dtype=jnp.int32)
    lengths_row = request_token_lengths[0]
    starts = jnp.cumsum(lengths_row) - lengths_row
    member = (positions[:, None] >= starts[None, :]) & (
        positions[:, None] < (starts + lengths_row)[None, :]
    )
    member_int = member.astype(jnp.int32)
    request_of = jnp.sum(member_int * jnp.arange(req_per_dev, dtype=jnp.int32)[None, :], axis=1)
    relative = positions - jnp.sum(member_int * starts[None, :], axis=1)
    tenant_hot = (
        request_tenant_index[:, None]
        == jnp.arange(tenant_adapter_scale.shape[0], dtype=jnp.int32)[None, :]
    ).astype(jnp.float32)
    request_scale = jnp.sum(tenant_hot * tenant_adapter_scale[None, :], axis=1)
    per_token_scale = jnp.sum(member.astype(jnp.float32) * request_scale[None, :], axis=1)[:, None]
    query_rows = (projected_rows[0] + per_token_scale * adapter_column_set[:, 0]).astype(
        jnp.bfloat16
    )
    key_rows = projected_rows[1].astype(jnp.bfloat16)
    value_row_block = (projected_rows[2] + per_token_scale * adapter_column_set[:, 1]).astype(
        jnp.bfloat16
    )
    owner_column = last_page_holder[:, 0]
    owner_table = owner_column.reshape(req_devices, req_per_dev)
    slot_table = holder_page_slot.reshape(req_devices, req_per_dev)
    owned = (owner_table == req_index).astype(jnp.int32)
    owned_rank = jnp.cumsum(owned, axis=1) - 1
    picked = owned[:, None, :] * (
        owned_rank[:, None, :] == jnp.arange(cap_slots, dtype=jnp.int32)[None, :, None]
    ).astype(jnp.int32)
    send_slot = jnp.sum(picked * slot_table[:, None, :], axis=2)
    fill_table = page_filled_rows.reshape(req_devices, req_per_dev)
    send_fill = jnp.sum(picked * fill_table[:, None, :], axis=2)
    my_owner = lax.dynamic_slice_in_dim(owner_column, req_index * req_per_dev, req_per_dev, 0)
    order_ids = jnp.arange(req_per_dev, dtype=jnp.int32)
    earlier = (my_owner[:, None] == my_owner[None, :]) & (order_ids[:, None] > order_ids[None, :])
    flat_pick = my_owner * cap_slots + jnp.sum(earlier.astype(jnp.int32), axis=1)
    page_inner = prefix_cache_store.shape[1:3]
    page_rows = prefix_cache_store.shape[3]
    pages = jnp.take(prefix_cache_store, send_slot.reshape(-1), axis=0, mode="clip")
    window_pick = (
        jnp.arange(page_rows, dtype=jnp.int32)[None, :, None]
        == (send_fill.reshape(-1)[:, None, None] - WINDOW)
        + jnp.arange(WINDOW, dtype=jnp.int32)[None, None, :]
    ).astype(jnp.bfloat16)
    source_pages = jnp.einsum(
        "skcr,srj->sjkc", pages, window_pick, preferred_element_type=jnp.float32
    ).astype(jnp.bfloat16)
    source_pages = source_pages.reshape((req_devices, cap_slots, WINDOW) + page_inner)
    arrived = lax.all_to_all(source_pages, "req", split_axis=0, concat_axis=0, tiled=True)
    prefix = jnp.take(
        arrived.reshape((req_devices * cap_slots, WINDOW) + page_inner),
        flat_pick,
        axis=0,
        mode="clip",
    )
    key_all = jnp.concatenate(
        [key_rows, prefix[:, :, 0].reshape(req_per_dev * WINDOW, head_column_set)], axis=0
    )
    value_all = jnp.concatenate(
        [value_row_block, prefix[:, :, 1].reshape(req_per_dev * WINDOW, head_column_set)], axis=0
    )
    distance = positions[:, None] - positions[None, :]
    local_ok = (request_of[:, None] == request_of[None, :]) & (distance >= 0) & (distance <= WINDOW)
    key_request = jnp.repeat(jnp.arange(req_per_dev, dtype=jnp.int32), WINDOW)
    key_offset = jnp.tile(jnp.arange(WINDOW, dtype=jnp.int32), req_per_dev)
    prefix_ok = (request_of[:, None] == key_request[None, :]) & (
        key_offset[None, :] >= relative[:, None]
    )
    allowed = jnp.concatenate([local_ok, prefix_ok], axis=1)
    query_heads = query_rows.reshape(tok_count, head_local, HEAD_SIZE)
    key_heads = key_all.reshape(-1, head_local, HEAD_SIZE)
    value_heads = value_all.reshape(-1, head_local, HEAD_SIZE)
    scores = jnp.einsum(
        "thd,shd->hts", query_heads, key_heads, preferred_element_type=jnp.float32
    ) * (1.0 / math.sqrt(HEAD_SIZE))
    masked = jnp.where(allowed[None], scores, -1e30)
    row_max = jnp.max(masked, axis=-1, keepdims=True)
    exp_scores = jnp.exp(masked - row_max)
    weights = (exp_scores / jnp.sum(exp_scores, axis=-1, keepdims=True)).astype(jnp.bfloat16)
    mixed = (
        jnp.einsum("hts,shd->thd", weights, value_heads, preferred_element_type=jnp.float32)
        .astype(jnp.bfloat16)
        .reshape(tok_count, head_column_set)
    )
    attn_part = (
        jnp.dot(mixed, head_output_weight, preferred_element_type=jnp.float32)
        .astype(jnp.bfloat16)
        .astype(jnp.float32)
    )
    gain_wide = feedforward_norm_gain.astype(jnp.float32)[None, :]
    attn_full = lax.psum(attn_part.astype(jnp.bfloat16), "mdl").astype(jnp.float32)
    resid_full = (stream.astype(jnp.float32) + attn_full).astype(jnp.bfloat16)
    resid_wide = resid_full.astype(jnp.float32)
    mean_sq = jnp.mean(resid_wide * resid_wide, axis=1, keepdims=True)
    normed = (resid_wide * lax.rsqrt(mean_sq + 1e-06) * gain_wide).astype(jnp.bfloat16)
    resid_mine = lax.dynamic_slice_in_dim(resid_full, mdl_index * row_share, row_share, 0)
    full_mlp = lax.all_gather(feedforward_weight, "req", axis=1, tiled=True)
    gate_part = jnp.dot(normed, full_mlp[0], preferred_element_type=jnp.float32)
    up_part = jnp.dot(normed, full_mlp[1], preferred_element_type=jnp.float32)
    hidden = (jax.nn.silu(gate_part) * up_part).astype(jnp.bfloat16)
    mlp_part = (
        jnp.einsum("tf,df->td", hidden, full_mlp[2], preferred_element_type=jnp.float32)
        .astype(jnp.bfloat16)
        .astype(jnp.float32)
    )
    mlp_mine = lax.psum_scatter(
        mlp_part.astype(jnp.bfloat16), "mdl", scatter_dimension=0, tiled=True
    ).astype(jnp.float32)
    return (resid_mine.astype(jnp.float32) + mlp_mine).astype(jnp.bfloat16)


def solution(mesh):
    return jax.shard_map(
        per_device,
        mesh=mesh,
        in_specs=(
            P("req", None),
            P(None, "mdl", None),
            P("mdl", None),
            P("mdl", None, None),
            P(None, "mdl", None),
            P(),
            P(),
            P(None, "req", "mdl"),
            P("req", None, "mdl", None),
            P("req"),
            P("req", None),
            P("req"),
            P(),
            P(),
            P(),
        ),
        out_specs=P(("req", "mdl"), None),
        check_vma=False,
    )
```

```python
import math

import jax
import jax.numpy as jnp
from jax import lax
from jax.experimental import pallas as pl
from jax.experimental.pallas import tpu as pltpu
from jax.sharding import PartitionSpec as P

HEAD_SIZE = 112
WINDOW = 64


def window_kernel(slot_ref, fill_ref, page_ref, out_ref):
    start = fill_ref[pl.program_id(0)] - WINDOW
    page_rows = page_ref.shape[-1]
    page = page_ref[0].reshape(-1, page_rows)
    row_ids = lax.broadcasted_iota(jnp.int32, (WINDOW, page_rows), 1)
    out_ids = lax.broadcasted_iota(jnp.int32, (WINDOW, page_rows), 0)
    pick = (row_ids == out_ids + start).astype(page.dtype)
    picked = lax.dot_general(
        pick, page, (((1,), (1,)), ((), ())), preferred_element_type=jnp.float32
    )
    out_ref[0] = picked.astype(out_ref.dtype)


def cut_windows(store, slots, fills):
    count = slots.shape[0]
    inner = store.shape[1] * store.shape[2]
    return pl.pallas_call(
        window_kernel,
        grid_spec=pltpu.PrefetchScalarGridSpec(
            num_scalar_prefetch=2,
            grid=(count,),
            in_specs=[
                pl.BlockSpec(
                    (1,) + store.shape[1:], lambda i, slot_ref, fill_ref: (slot_ref[i], 0, 0, 0)
                )
            ],
            out_specs=pl.BlockSpec((1, WINDOW, inner), lambda i, slot_ref, fill_ref: (i, 0, 0)),
        ),
        out_shape=jax.ShapeDtypeStruct((count, WINDOW, inner), store.dtype),
    )(slots, fills, store)


def per_device(
    stream,
    attention_projection_weight,
    head_output_weight,
    adapter_down_maps,
    adapter_up_maps,
    tenant_adapter_scale,
    feedforward_norm_gain,
    feedforward_weight,
    prefix_cache_store,
    token_adapter_index,
    request_token_lengths,
    request_tenant_index,
    last_page_holder,
    holder_page_slot,
    page_filled_rows,
):
    tok_count, model_width = stream.shape
    head_column_set = attention_projection_weight.shape[1]
    head_local = head_column_set // HEAD_SIZE
    req_per_dev = request_token_lengths.shape[1]
    rank_total_width = adapter_down_maps.shape[2]
    adapter_number = adapter_up_maps.shape[2] // rank_total_width
    req_devices = lax.axis_size("req")
    req_index = lax.axis_index("req")
    mdl_index = lax.axis_index("mdl")
    row_share = tok_count // lax.axis_size("mdl")
    cap_slots = max(2, (req_per_dev + req_devices - 1) // req_devices + 1)
    projected_rows = jnp.einsum(
        "td,kcd->ktc", stream, attention_projection_weight, preferred_element_type=jnp.float32
    )
    all_onehot = (
        token_adapter_index[:, None] == jnp.arange(adapter_number, dtype=jnp.int32)[None, :]
    )
    holder_count = adapter_down_maps.shape[0]
    holder_rank_rows = jnp.einsum(
        "qf,kfn->qkn", stream, adapter_down_maps, preferred_element_type=jnp.float32
    )
    held_onehot = (
        token_adapter_index[:, None]
        == (mdl_index * holder_count + jnp.arange(holder_count, dtype=jnp.int32))[None, :]
    )
    rank_part = jnp.sum(holder_rank_rows * held_onehot.astype(jnp.float32)[:, :, None], axis=1)
    rank_feat = lax.psum(rank_part.astype(jnp.bfloat16), "mdl")
    broadcast_result = (
        all_onehot.astype(jnp.bfloat16)[:, :, None] * rank_feat[:, None, :]
    ).reshape(tok_count, adapter_number * rank_total_width)
    adapter_column_set = jnp.einsum(
        "iu,pdu->ipd", broadcast_result, adapter_up_maps, preferred_element_type=jnp.float32
    )
    positions = jnp.arange(tok_count, dtype=jnp.int32)
    lengths_row = request_token_lengths[0]
    starts = jnp.cumsum(lengths_row) - lengths_row
    member = (positions[:, None] >= starts[None, :]) & (
        positions[:, None] < (starts + lengths_row)[None, :]
    )
    member_int = member.astype(jnp.int32)
    request_of = jnp.sum(member_int * jnp.arange(req_per_dev, dtype=jnp.int32)[None, :], axis=1)
    relative = positions - jnp.sum(member_int * starts[None, :], axis=1)
    tenant_hot = (
        request_tenant_index[:, None]
        == jnp.arange(tenant_adapter_scale.shape[0], dtype=jnp.int32)[None, :]
    ).astype(jnp.float32)
    request_scale = jnp.sum(tenant_hot * tenant_adapter_scale[None, :], axis=1)
    per_token_scale = jnp.sum(member.astype(jnp.float32) * request_scale[None, :], axis=1)[:, None]
    query_rows = (projected_rows[0] + per_token_scale * adapter_column_set[:, 0]).astype(
        jnp.bfloat16
    )
    key_rows = projected_rows[1].astype(jnp.bfloat16)
    value_row_block = (projected_rows[2] + per_token_scale * adapter_column_set[:, 1]).astype(
        jnp.bfloat16
    )
    owner_column = last_page_holder[:, 0]
    owner_table = owner_column.reshape(req_devices, req_per_dev)
    slot_table = holder_page_slot.reshape(req_devices, req_per_dev)
    owned = (owner_table == req_index).astype(jnp.int32)
    owned_rank = jnp.cumsum(owned, axis=1) - 1
    picked = owned[:, None, :] * (
        owned_rank[:, None, :] == jnp.arange(cap_slots, dtype=jnp.int32)[None, :, None]
    ).astype(jnp.int32)
    send_slot = jnp.sum(picked * slot_table[:, None, :], axis=2)
    fill_table = page_filled_rows.reshape(req_devices, req_per_dev)
    send_fill = jnp.sum(picked * fill_table[:, None, :], axis=2)
    my_owner = lax.dynamic_slice_in_dim(owner_column, req_index * req_per_dev, req_per_dev, 0)
    order_ids = jnp.arange(req_per_dev, dtype=jnp.int32)
    earlier = (my_owner[:, None] == my_owner[None, :]) & (order_ids[:, None] > order_ids[None, :])
    flat_pick = my_owner * cap_slots + jnp.sum(earlier.astype(jnp.int32), axis=1)
    page_inner = prefix_cache_store.shape[1:3]
    page_rows = prefix_cache_store.shape[3]
    source_pages = cut_windows(
        prefix_cache_store,
        jnp.clip(send_slot.reshape(-1), 0, prefix_cache_store.shape[0] - 1),
        send_fill.reshape(-1),
    )
    source_pages = source_pages.reshape((req_devices, cap_slots, WINDOW) + page_inner)
    arrived = lax.all_to_all(source_pages, "req", split_axis=0, concat_axis=0, tiled=True)
    prefix = jnp.take(
        arrived.reshape((req_devices * cap_slots, WINDOW) + page_inner),
        flat_pick,
        axis=0,
        mode="clip",
    )
    key_all = jnp.concatenate(
        [key_rows, prefix[:, :, 0].reshape(req_per_dev * WINDOW, head_column_set)], axis=0
    )
    value_all = jnp.concatenate(
        [value_row_block, prefix[:, :, 1].reshape(req_per_dev * WINDOW, head_column_set)], axis=0
    )
    distance = positions[:, None] - positions[None, :]
    local_ok = (request_of[:, None] == request_of[None, :]) & (distance >= 0) & (distance <= WINDOW)
    key_request = jnp.repeat(jnp.arange(req_per_dev, dtype=jnp.int32), WINDOW)
    key_offset = jnp.tile(jnp.arange(WINDOW, dtype=jnp.int32), req_per_dev)
    prefix_ok = (request_of[:, None] == key_request[None, :]) & (
        key_offset[None, :] >= relative[:, None]
    )
    allowed = jnp.concatenate([local_ok, prefix_ok], axis=1)
    query_heads = query_rows.reshape(tok_count, head_local, HEAD_SIZE)
    key_heads = key_all.reshape(-1, head_local, HEAD_SIZE)
    value_heads = value_all.reshape(-1, head_local, HEAD_SIZE)
    scores = jnp.einsum(
        "thd,shd->hts", query_heads, key_heads, preferred_element_type=jnp.float32
    ) * (1.0 / math.sqrt(HEAD_SIZE))
    masked = jnp.where(allowed[None], scores, -1e30)
    row_max = jnp.max(masked, axis=-1, keepdims=True)
    exp_scores = jnp.exp(masked - row_max)
    weights = (exp_scores / jnp.sum(exp_scores, axis=-1, keepdims=True)).astype(jnp.bfloat16)
    mixed = (
        jnp.einsum("hts,shd->thd", weights, value_heads, preferred_element_type=jnp.float32)
        .astype(jnp.bfloat16)
        .reshape(tok_count, head_column_set)
    )
    attn_part = (
        jnp.dot(mixed, head_output_weight, preferred_element_type=jnp.float32)
        .astype(jnp.bfloat16)
        .astype(jnp.float32)
    )
    gain_wide = feedforward_norm_gain.astype(jnp.float32)[None, :]
    attn_full = lax.psum(attn_part.astype(jnp.bfloat16), "mdl").astype(jnp.float32)
    resid_full = (stream.astype(jnp.float32) + attn_full).astype(jnp.bfloat16)
    resid_wide = resid_full.astype(jnp.float32)
    mean_sq = jnp.mean(resid_wide * resid_wide, axis=1, keepdims=True)
    normed = (resid_wide * lax.rsqrt(mean_sq + 1e-06) * gain_wide).astype(jnp.bfloat16)
    resid_mine = lax.dynamic_slice_in_dim(resid_full, mdl_index * row_share, row_share, 0)
    full_mlp = lax.all_gather(feedforward_weight, "req", axis=1, tiled=True)
    gate_part = jnp.dot(normed, full_mlp[0], preferred_element_type=jnp.float32)
    up_part = jnp.dot(normed, full_mlp[1], preferred_element_type=jnp.float32)
    hidden = (jax.nn.silu(gate_part) * up_part).astype(jnp.bfloat16)
    mlp_part = (
        jnp.einsum("tf,df->td", hidden, full_mlp[2], preferred_element_type=jnp.float32)
        .astype(jnp.bfloat16)
        .astype(jnp.float32)
    )
    mlp_mine = lax.psum_scatter(
        mlp_part.astype(jnp.bfloat16), "mdl", scatter_dimension=0, tiled=True
    ).astype(jnp.float32)
    return (resid_mine.astype(jnp.float32) + mlp_mine).astype(jnp.bfloat16)


def solution(mesh):
    return jax.shard_map(
        per_device,
        mesh=mesh,
        in_specs=(
            P("req", None),
            P(None, "mdl", None),
            P("mdl", None),
            P("mdl", None, None),
            P(None, "mdl", None),
            P(),
            P(),
            P(None, "req", "mdl"),
            P("req", None, "mdl", None),
            P("req"),
            P("req", None),
            P("req"),
            P(),
            P(),
            P(),
        ),
        out_specs=P(("req", "mdl"), None),
        check_vma=False,
    )
```

```python
import math

import jax
import jax.numpy as jnp
from jax import lax
from jax.experimental import pallas as pl
from jax.experimental.pallas import tpu as pltpu
from jax.sharding import PartitionSpec as P

HEAD_SIZE = 112
WINDOW = 64


def window_kernel(slot_ref, fill_ref, store_ref, out_ref, held, sems):
    count = out_ref.shape[0]

    def fetch(i):
        return pltpu.make_async_copy(store_ref.at[slot_ref[i]], held.at[i], sems.at[i])

    def start(i, carry):
        fetch(i).start()
        return carry

    lax.fori_loop(0, count, start, 0)
    page_rows = held.shape[-1]
    row_ids = lax.broadcasted_iota(jnp.int32, (WINDOW, page_rows), 1)
    out_ids = lax.broadcasted_iota(jnp.int32, (WINDOW, page_rows), 0)

    def pick_rows(i, carry):
        fetch(i).wait()
        pick = (row_ids == out_ids + (fill_ref[i] - WINDOW)).astype(held.dtype)
        for part in range(held.shape[1]):
            out_ref[i, part] = lax.dot_general(
                pick, held[i, part], (((1,), (1,)), ((), ())), preferred_element_type=jnp.float32
            ).astype(out_ref.dtype)
        return carry

    lax.fori_loop(0, count, pick_rows, 0)


def cut_windows(store, slots, fills):
    count = slots.shape[0]
    parts, width, page_rows = store.shape[1:]
    return pl.pallas_call(
        window_kernel,
        grid_spec=pltpu.PrefetchScalarGridSpec(
            num_scalar_prefetch=2,
            grid=(1,),
            in_specs=[pl.BlockSpec(memory_space=pl.ANY)],
            out_specs=pl.BlockSpec(memory_space=pltpu.VMEM),
            scratch_shapes=[
                pltpu.VMEM((count, parts, width, page_rows), store.dtype),
                pltpu.SemaphoreType.DMA((count,)),
            ],
        ),
        out_shape=jax.ShapeDtypeStruct((count, parts, WINDOW, width), store.dtype),
    )(slots, fills, store)


def per_device(
    stream,
    attention_projection_weight,
    head_output_weight,
    adapter_down_maps,
    adapter_up_maps,
    tenant_adapter_scale,
    feedforward_norm_gain,
    feedforward_weight,
    prefix_cache_store,
    token_adapter_index,
    request_token_lengths,
    request_tenant_index,
    last_page_holder,
    holder_page_slot,
    page_filled_rows,
):
    tok_count, model_width = stream.shape
    head_column_set = attention_projection_weight.shape[1]
    head_local = head_column_set // HEAD_SIZE
    req_per_dev = request_token_lengths.shape[1]
    rank_total_width = adapter_down_maps.shape[2]
    adapter_number = adapter_up_maps.shape[2] // rank_total_width
    req_devices = lax.axis_size("req")
    req_index = lax.axis_index("req")
    mdl_index = lax.axis_index("mdl")
    row_share = tok_count // lax.axis_size("mdl")
    cap_slots = max(2, (req_per_dev + req_devices - 1) // req_devices + 1)
    projected_rows = jnp.einsum(
        "td,kcd->ktc", stream, attention_projection_weight, preferred_element_type=jnp.float32
    )
    all_onehot = (
        token_adapter_index[:, None] == jnp.arange(adapter_number, dtype=jnp.int32)[None, :]
    )
    holder_count = adapter_down_maps.shape[0]
    holder_rank_rows = jnp.einsum(
        "qf,kfn->qkn", stream, adapter_down_maps, preferred_element_type=jnp.float32
    )
    held_onehot = (
        token_adapter_index[:, None]
        == (mdl_index * holder_count + jnp.arange(holder_count, dtype=jnp.int32))[None, :]
    )
    rank_part = jnp.sum(holder_rank_rows * held_onehot.astype(jnp.float32)[:, :, None], axis=1)
    rank_feat = lax.psum(rank_part.astype(jnp.bfloat16), "mdl")
    broadcast_result = (
        all_onehot.astype(jnp.bfloat16)[:, :, None] * rank_feat[:, None, :]
    ).reshape(tok_count, adapter_number * rank_total_width)
    adapter_column_set = jnp.einsum(
        "iu,pdu->ipd", broadcast_result, adapter_up_maps, preferred_element_type=jnp.float32
    )
    positions = jnp.arange(tok_count, dtype=jnp.int32)
    lengths_row = request_token_lengths[0]
    starts = jnp.cumsum(lengths_row) - lengths_row
    member = (positions[:, None] >= starts[None, :]) & (
        positions[:, None] < (starts + lengths_row)[None, :]
    )
    member_int = member.astype(jnp.int32)
    request_of = jnp.sum(member_int * jnp.arange(req_per_dev, dtype=jnp.int32)[None, :], axis=1)
    relative = positions - jnp.sum(member_int * starts[None, :], axis=1)
    tenant_hot = (
        request_tenant_index[:, None]
        == jnp.arange(tenant_adapter_scale.shape[0], dtype=jnp.int32)[None, :]
    ).astype(jnp.float32)
    request_scale = jnp.sum(tenant_hot * tenant_adapter_scale[None, :], axis=1)
    per_token_scale = jnp.sum(member.astype(jnp.float32) * request_scale[None, :], axis=1)[:, None]
    query_rows = (projected_rows[0] + per_token_scale * adapter_column_set[:, 0]).astype(
        jnp.bfloat16
    )
    key_rows = projected_rows[1].astype(jnp.bfloat16)
    value_row_block = (projected_rows[2] + per_token_scale * adapter_column_set[:, 1]).astype(
        jnp.bfloat16
    )
    owner_column = last_page_holder[:, 0]
    owner_table = owner_column.reshape(req_devices, req_per_dev)
    slot_table = holder_page_slot.reshape(req_devices, req_per_dev)
    owned = (owner_table == req_index).astype(jnp.int32)
    owned_rank = jnp.cumsum(owned, axis=1) - 1
    picked = owned[:, None, :] * (
        owned_rank[:, None, :] == jnp.arange(cap_slots, dtype=jnp.int32)[None, :, None]
    ).astype(jnp.int32)
    send_slot = jnp.sum(picked * slot_table[:, None, :], axis=2)
    fill_table = page_filled_rows.reshape(req_devices, req_per_dev)
    send_fill = jnp.sum(picked * fill_table[:, None, :], axis=2)
    my_owner = lax.dynamic_slice_in_dim(owner_column, req_index * req_per_dev, req_per_dev, 0)
    order_ids = jnp.arange(req_per_dev, dtype=jnp.int32)
    earlier = (my_owner[:, None] == my_owner[None, :]) & (order_ids[:, None] > order_ids[None, :])
    flat_pick = my_owner * cap_slots + jnp.sum(earlier.astype(jnp.int32), axis=1)
    page_inner = prefix_cache_store.shape[1:3]
    page_rows = prefix_cache_store.shape[3]
    source_pages = cut_windows(
        prefix_cache_store,
        jnp.clip(send_slot.reshape(-1), 0, prefix_cache_store.shape[0] - 1),
        send_fill.reshape(-1),
    )
    source_pages = source_pages.reshape((req_devices, cap_slots, 2, WINDOW, head_column_set))
    arrived = lax.all_to_all(source_pages, "req", split_axis=0, concat_axis=0, tiled=True)
    prefix = jnp.take(
        arrived.reshape((req_devices * cap_slots, 2, WINDOW, head_column_set)),
        flat_pick,
        axis=0,
        mode="clip",
    )
    key_all = jnp.concatenate(
        [key_rows, prefix[:, 0].reshape(req_per_dev * WINDOW, head_column_set)], axis=0
    )
    value_all = jnp.concatenate(
        [value_row_block, prefix[:, 1].reshape(req_per_dev * WINDOW, head_column_set)], axis=0
    )
    distance = positions[:, None] - positions[None, :]
    local_ok = (request_of[:, None] == request_of[None, :]) & (distance >= 0) & (distance <= WINDOW)
    key_request = jnp.repeat(jnp.arange(req_per_dev, dtype=jnp.int32), WINDOW)
    key_offset = jnp.tile(jnp.arange(WINDOW, dtype=jnp.int32), req_per_dev)
    prefix_ok = (request_of[:, None] == key_request[None, :]) & (
        key_offset[None, :] >= relative[:, None]
    )
    allowed = jnp.concatenate([local_ok, prefix_ok], axis=1)
    query_heads = query_rows.reshape(tok_count, head_local, HEAD_SIZE)
    key_heads = key_all.reshape(-1, head_local, HEAD_SIZE)
    value_heads = value_all.reshape(-1, head_local, HEAD_SIZE)
    scores = jnp.einsum(
        "thd,shd->hts", query_heads, key_heads, preferred_element_type=jnp.float32
    ) * (1.0 / math.sqrt(HEAD_SIZE))
    masked = jnp.where(allowed[None], scores, -1e30)
    row_max = jnp.max(masked, axis=-1, keepdims=True)
    exp_scores = jnp.exp(masked - row_max)
    weights = (exp_scores / jnp.sum(exp_scores, axis=-1, keepdims=True)).astype(jnp.bfloat16)
    mixed = (
        jnp.einsum("hts,shd->thd", weights, value_heads, preferred_element_type=jnp.float32)
        .astype(jnp.bfloat16)
        .reshape(tok_count, head_column_set)
    )
    attn_part = (
        jnp.dot(mixed, head_output_weight, preferred_element_type=jnp.float32)
        .astype(jnp.bfloat16)
        .astype(jnp.float32)
    )
    gain_wide = feedforward_norm_gain.astype(jnp.float32)[None, :]
    attn_full = lax.psum(attn_part.astype(jnp.bfloat16), "mdl").astype(jnp.float32)
    resid_full = (stream.astype(jnp.float32) + attn_full).astype(jnp.bfloat16)
    resid_wide = resid_full.astype(jnp.float32)
    mean_sq = jnp.mean(resid_wide * resid_wide, axis=1, keepdims=True)
    normed = (resid_wide * lax.rsqrt(mean_sq + 1e-06) * gain_wide).astype(jnp.bfloat16)
    resid_mine = lax.dynamic_slice_in_dim(resid_full, mdl_index * row_share, row_share, 0)
    full_mlp = lax.all_gather(feedforward_weight, "req", axis=1, tiled=True)
    gate_part = jnp.dot(normed, full_mlp[0], preferred_element_type=jnp.float32)
    up_part = jnp.dot(normed, full_mlp[1], preferred_element_type=jnp.float32)
    hidden = (jax.nn.silu(gate_part) * up_part).astype(jnp.bfloat16)
    mlp_part = (
        jnp.einsum("tf,df->td", hidden, full_mlp[2], preferred_element_type=jnp.float32)
        .astype(jnp.bfloat16)
        .astype(jnp.float32)
    )
    mlp_mine = lax.psum_scatter(
        mlp_part.astype(jnp.bfloat16), "mdl", scatter_dimension=0, tiled=True
    ).astype(jnp.float32)
    return (resid_mine.astype(jnp.float32) + mlp_mine).astype(jnp.bfloat16)


def solution(mesh):
    return jax.shard_map(
        per_device,
        mesh=mesh,
        in_specs=(
            P("req", None),
            P(None, "mdl", None),
            P("mdl", None),
            P("mdl", None, None),
            P(None, "mdl", None),
            P(),
            P(),
            P(None, "req", "mdl"),
            P("req", None, "mdl", None),
            P("req"),
            P("req", None),
            P("req"),
            P(),
            P(),
            P(),
        ),
        out_specs=P(("req", "mdl"), None),
        check_vma=False,
    )
```

```python
import math

import jax
import jax.numpy as jnp
from jax import lax
from jax.experimental import pallas as pl
from jax.experimental.pallas import tpu as pltpu
from jax.sharding import PartitionSpec as P

HEAD_SIZE = 112
WINDOW = 64


def window_kernel(slot_ref, fill_ref, store_ref, out_ref, held, sems):
    count = out_ref.shape[0]

    def fetch(i):
        return pltpu.make_async_copy(store_ref.at[slot_ref[i]], held.at[i], sems.at[i])

    def start(i, carry):
        fetch(i).start()
        return carry

    lax.fori_loop(0, count, start, 0)
    page_rows = held.shape[-1]
    row_ids = lax.broadcasted_iota(jnp.int32, (WINDOW, page_rows), 1)
    out_ids = lax.broadcasted_iota(jnp.int32, (WINDOW, page_rows), 0)

    def pick_rows(i, carry):
        fetch(i).wait()
        pick = (row_ids == out_ids + (fill_ref[i] - WINDOW)).astype(held.dtype)
        for part in range(held.shape[1]):
            out_ref[i, part] = lax.dot_general(
                pick, held[i, part], (((1,), (1,)), ((), ())), preferred_element_type=jnp.float32
            ).astype(out_ref.dtype)
        return carry

    lax.fori_loop(0, count, pick_rows, 0)


def cut_windows(store, slots, fills):
    count = slots.shape[0]
    parts, width, page_rows = store.shape[1:]
    return pl.pallas_call(
        window_kernel,
        grid_spec=pltpu.PrefetchScalarGridSpec(
            num_scalar_prefetch=2,
            grid=(1,),
            in_specs=[pl.BlockSpec(memory_space=pl.ANY)],
            out_specs=pl.BlockSpec(memory_space=pltpu.VMEM),
            scratch_shapes=[
                pltpu.VMEM((count, parts, width, page_rows), store.dtype),
                pltpu.SemaphoreType.DMA((count,)),
            ],
        ),
        out_shape=jax.ShapeDtypeStruct((count, parts, WINDOW, width), store.dtype),
    )(slots, fills, store)


def exchange_kernel(sent, out_ref, got, send_sems, recv_sems):
    peers = lax.axis_size("req")
    cap = sent.shape[0] // peers
    me = lax.axis_index("req")
    mine = lax.axis_index("mdl")
    barrier = pltpu.get_barrier_semaphore()

    def greet(k, carry):
        peer = lax.rem(me + k, peers)
        pl.semaphore_signal(barrier, inc=1, device_id=(peer, mine), device_id_type=pl.DeviceIdType.MESH)
        return carry

    lax.fori_loop(1, peers, greet, 0)
    pl.semaphore_wait(barrier, peers - 1)

    def send(k):
        peer = lax.rem(me + k, peers)
        return pltpu.make_async_remote_copy(
            src_ref=sent.at[pl.ds(peer * cap, cap)],
            dst_ref=got.at[pl.ds(me * cap, cap)],
            send_sem=send_sems.at[k],
            recv_sem=recv_sems.at[k],
            device_id=(peer, mine),
            device_id_type=pl.DeviceIdType.MESH,
        )

    def start_send(k, carry):
        send(k).start()
        return carry

    lax.fori_loop(1, peers, start_send, 0)
    got[pl.ds(me * cap, cap)] = sent[pl.ds(me * cap, cap)]

    def finish(k, carry):
        send(k).wait()
        return carry

    lax.fori_loop(1, peers, finish, 0)
    out_ref[...] = got[...]


def exchange_windows(windows, peers):
    return pl.pallas_call(
        exchange_kernel,
        in_specs=[pl.BlockSpec(memory_space=pltpu.VMEM)],
        out_specs=pl.BlockSpec(memory_space=pltpu.VMEM),
        scratch_shapes=[
            pltpu.VMEM(windows.shape, windows.dtype),
            pltpu.SemaphoreType.DMA((peers,)),
            pltpu.SemaphoreType.DMA((peers,)),
        ],
        out_shape=jax.ShapeDtypeStruct(windows.shape, windows.dtype),
        compiler_params=pltpu.CompilerParams(collective_id=0, has_side_effects=True),
    )(windows)


def per_device(
    stream,
    attention_projection_weight,
    head_output_weight,
    adapter_down_maps,
    adapter_up_maps,
    tenant_adapter_scale,
    feedforward_norm_gain,
    feedforward_weight,
    prefix_cache_store,
    token_adapter_index,
    request_token_lengths,
    request_tenant_index,
    last_page_holder,
    holder_page_slot,
    page_filled_rows,
):
    tok_count, model_width = stream.shape
    head_column_set = attention_projection_weight.shape[1]
    head_local = head_column_set // HEAD_SIZE
    req_per_dev = request_token_lengths.shape[1]
    rank_total_width = adapter_down_maps.shape[2]
    adapter_number = adapter_up_maps.shape[2] // rank_total_width
    req_devices = lax.axis_size("req")
    req_index = lax.axis_index("req")
    mdl_index = lax.axis_index("mdl")
    row_share = tok_count // lax.axis_size("mdl")
    cap_slots = max(2, (req_per_dev + req_devices - 1) // req_devices + 1)
    projected_rows = jnp.einsum(
        "td,kcd->ktc", stream, attention_projection_weight, preferred_element_type=jnp.float32
    )
    all_onehot = (
        token_adapter_index[:, None] == jnp.arange(adapter_number, dtype=jnp.int32)[None, :]
    )
    holder_count = adapter_down_maps.shape[0]
    holder_rank_rows = jnp.einsum(
        "qf,kfn->qkn", stream, adapter_down_maps, preferred_element_type=jnp.float32
    )
    held_onehot = (
        token_adapter_index[:, None]
        == (mdl_index * holder_count + jnp.arange(holder_count, dtype=jnp.int32))[None, :]
    )
    rank_part = jnp.sum(holder_rank_rows * held_onehot.astype(jnp.float32)[:, :, None], axis=1)
    rank_feat = lax.psum(rank_part.astype(jnp.bfloat16), "mdl")
    broadcast_result = (
        all_onehot.astype(jnp.bfloat16)[:, :, None] * rank_feat[:, None, :]
    ).reshape(tok_count, adapter_number * rank_total_width)
    adapter_column_set = jnp.einsum(
        "iu,pdu->ipd", broadcast_result, adapter_up_maps, preferred_element_type=jnp.float32
    )
    positions = jnp.arange(tok_count, dtype=jnp.int32)
    lengths_row = request_token_lengths[0]
    starts = jnp.cumsum(lengths_row) - lengths_row
    member = (positions[:, None] >= starts[None, :]) & (
        positions[:, None] < (starts + lengths_row)[None, :]
    )
    member_int = member.astype(jnp.int32)
    request_of = jnp.sum(member_int * jnp.arange(req_per_dev, dtype=jnp.int32)[None, :], axis=1)
    relative = positions - jnp.sum(member_int * starts[None, :], axis=1)
    tenant_hot = (
        request_tenant_index[:, None]
        == jnp.arange(tenant_adapter_scale.shape[0], dtype=jnp.int32)[None, :]
    ).astype(jnp.float32)
    request_scale = jnp.sum(tenant_hot * tenant_adapter_scale[None, :], axis=1)
    per_token_scale = jnp.sum(member.astype(jnp.float32) * request_scale[None, :], axis=1)[:, None]
    query_rows = (projected_rows[0] + per_token_scale * adapter_column_set[:, 0]).astype(
        jnp.bfloat16
    )
    key_rows = projected_rows[1].astype(jnp.bfloat16)
    value_row_block = (projected_rows[2] + per_token_scale * adapter_column_set[:, 1]).astype(
        jnp.bfloat16
    )
    owner_column = last_page_holder[:, 0]
    owner_table = owner_column.reshape(req_devices, req_per_dev)
    slot_table = holder_page_slot.reshape(req_devices, req_per_dev)
    owned = (owner_table == req_index).astype(jnp.int32)
    owned_rank = jnp.cumsum(owned, axis=1) - 1
    picked = owned[:, None, :] * (
        owned_rank[:, None, :] == jnp.arange(cap_slots, dtype=jnp.int32)[None, :, None]
    ).astype(jnp.int32)
    send_slot = jnp.sum(picked * slot_table[:, None, :], axis=2)
    fill_table = page_filled_rows.reshape(req_devices, req_per_dev)
    send_fill = jnp.sum(picked * fill_table[:, None, :], axis=2)
    my_owner = lax.dynamic_slice_in_dim(owner_column, req_index * req_per_dev, req_per_dev, 0)
    order_ids = jnp.arange(req_per_dev, dtype=jnp.int32)
    earlier = (my_owner[:, None] == my_owner[None, :]) & (order_ids[:, None] > order_ids[None, :])
    flat_pick = my_owner * cap_slots + jnp.sum(earlier.astype(jnp.int32), axis=1)
    page_inner = prefix_cache_store.shape[1:3]
    page_rows = prefix_cache_store.shape[3]
    windows = cut_windows(
        prefix_cache_store,
        jnp.clip(send_slot.reshape(-1), 0, prefix_cache_store.shape[0] - 1),
        send_fill.reshape(-1),
    )
    arrived = exchange_windows(windows, req_devices)
    prefix = jnp.take(
        arrived.reshape((req_devices * cap_slots, 2, WINDOW, head_column_set)),
        flat_pick,
        axis=0,
        mode="clip",
    )
    key_all = jnp.concatenate(
        [key_rows, prefix[:, 0].reshape(req_per_dev * WINDOW, head_column_set)], axis=0
    )
    value_all = jnp.concatenate(
        [value_row_block, prefix[:, 1].reshape(req_per_dev * WINDOW, head_column_set)], axis=0
    )
    distance = positions[:, None] - positions[None, :]
    local_ok = (request_of[:, None] == request_of[None, :]) & (distance >= 0) & (distance <= WINDOW)
    key_request = jnp.repeat(jnp.arange(req_per_dev, dtype=jnp.int32), WINDOW)
    key_offset = jnp.tile(jnp.arange(WINDOW, dtype=jnp.int32), req_per_dev)
    prefix_ok = (request_of[:, None] == key_request[None, :]) & (
        key_offset[None, :] >= relative[:, None]
    )
    allowed = jnp.concatenate([local_ok, prefix_ok], axis=1)
    query_heads = query_rows.reshape(tok_count, head_local, HEAD_SIZE)
    key_heads = key_all.reshape(-1, head_local, HEAD_SIZE)
    value_heads = value_all.reshape(-1, head_local, HEAD_SIZE)
    scores = jnp.einsum(
        "thd,shd->hts", query_heads, key_heads, preferred_element_type=jnp.float32
    ) * (1.0 / math.sqrt(HEAD_SIZE))
    masked = jnp.where(allowed[None], scores, -1e30)
    row_max = jnp.max(masked, axis=-1, keepdims=True)
    exp_scores = jnp.exp(masked - row_max)
    weights = (exp_scores / jnp.sum(exp_scores, axis=-1, keepdims=True)).astype(jnp.bfloat16)
    mixed = (
        jnp.einsum("hts,shd->thd", weights, value_heads, preferred_element_type=jnp.float32)
        .astype(jnp.bfloat16)
        .reshape(tok_count, head_column_set)
    )
    attn_part = (
        jnp.dot(mixed, head_output_weight, preferred_element_type=jnp.float32)
        .astype(jnp.bfloat16)
        .astype(jnp.float32)
    )
    gain_wide = feedforward_norm_gain.astype(jnp.float32)[None, :]
    attn_full = lax.psum(attn_part.astype(jnp.bfloat16), "mdl").astype(jnp.float32)
    resid_full = (stream.astype(jnp.float32) + attn_full).astype(jnp.bfloat16)
    resid_wide = resid_full.astype(jnp.float32)
    mean_sq = jnp.mean(resid_wide * resid_wide, axis=1, keepdims=True)
    normed = (resid_wide * lax.rsqrt(mean_sq + 1e-06) * gain_wide).astype(jnp.bfloat16)
    resid_mine = lax.dynamic_slice_in_dim(resid_full, mdl_index * row_share, row_share, 0)
    full_mlp = lax.all_gather(feedforward_weight, "req", axis=1, tiled=True)
    gate_part = jnp.dot(normed, full_mlp[0], preferred_element_type=jnp.float32)
    up_part = jnp.dot(normed, full_mlp[1], preferred_element_type=jnp.float32)
    hidden = (jax.nn.silu(gate_part) * up_part).astype(jnp.bfloat16)
    mlp_part = (
        jnp.einsum("tf,df->td", hidden, full_mlp[2], preferred_element_type=jnp.float32)
        .astype(jnp.bfloat16)
        .astype(jnp.float32)
    )
    mlp_mine = lax.psum_scatter(
        mlp_part.astype(jnp.bfloat16), "mdl", scatter_dimension=0, tiled=True
    ).astype(jnp.float32)
    return (resid_mine.astype(jnp.float32) + mlp_mine).astype(jnp.bfloat16)


def solution(mesh):
    return jax.shard_map(
        per_device,
        mesh=mesh,
        in_specs=(
            P("req", None),
            P(None, "mdl", None),
            P("mdl", None),
            P("mdl", None, None),
            P(None, "mdl", None),
            P(),
            P(),
            P(None, "req", "mdl"),
            P("req", None, "mdl", None),
            P("req"),
            P("req", None),
            P("req"),
            P(),
            P(),
            P(),
        ),
        out_specs=P(("req", "mdl"), None),
        check_vma=False,
    )
```

```python
import math

import jax
import jax.numpy as jnp
from jax import lax
from jax.experimental import pallas as pl
from jax.experimental.pallas import tpu as pltpu
from jax.sharding import PartitionSpec as P

HEAD_SIZE = 112
WINDOW = 64


def window_kernel(slot_ref, fill_ref, store_ref, out_ref, held, sems):
    count = out_ref.shape[0]

    def fetch(i):
        return pltpu.make_async_copy(store_ref.at[slot_ref[i]], held.at[i], sems.at[i])

    def start(i, carry):
        fetch(i).start()
        return carry

    lax.fori_loop(0, count, start, 0)
    page_rows = held.shape[-1]
    row_ids = lax.broadcasted_iota(jnp.int32, (WINDOW, page_rows), 1)
    out_ids = lax.broadcasted_iota(jnp.int32, (WINDOW, page_rows), 0)

    def pick_rows(i, carry):
        fetch(i).wait()
        pick = (row_ids == out_ids + (fill_ref[i] - WINDOW)).astype(held.dtype)
        for part in range(held.shape[1]):
            out_ref[i, part] = lax.dot_general(
                pick, held[i, part], (((1,), (1,)), ((), ())), preferred_element_type=jnp.float32
            ).astype(out_ref.dtype)
        return carry

    lax.fori_loop(0, count, pick_rows, 0)


def cut_windows(store, slots, fills):
    count = slots.shape[0]
    parts, width, page_rows = store.shape[1:]
    return pl.pallas_call(
        window_kernel,
        grid_spec=pltpu.PrefetchScalarGridSpec(
            num_scalar_prefetch=2,
            grid=(1,),
            in_specs=[pl.BlockSpec(memory_space=pl.ANY)],
            out_specs=pl.BlockSpec(memory_space=pltpu.VMEM),
            scratch_shapes=[
                pltpu.VMEM((count, parts, width, page_rows), store.dtype),
                pltpu.SemaphoreType.DMA((count,)),
            ],
        ),
        out_shape=jax.ShapeDtypeStruct((count, parts, WINDOW, width), store.dtype),
    )(slots, fills, store)


def per_device(
    stream,
    attention_projection_weight,
    head_output_weight,
    adapter_down_maps,
    adapter_up_maps,
    tenant_adapter_scale,
    feedforward_norm_gain,
    feedforward_weight,
    prefix_cache_store,
    token_adapter_index,
    request_token_lengths,
    request_tenant_index,
    last_page_holder,
    holder_page_slot,
    page_filled_rows,
):
    tok_count, model_width = stream.shape
    head_column_set = attention_projection_weight.shape[1]
    head_local = head_column_set // HEAD_SIZE
    req_per_dev = request_token_lengths.shape[1]
    rank_total_width = adapter_down_maps.shape[2]
    adapter_number = adapter_up_maps.shape[2] // rank_total_width
    req_devices = lax.axis_size("req")
    req_index = lax.axis_index("req")
    mdl_index = lax.axis_index("mdl")
    row_share = tok_count // lax.axis_size("mdl")
    cap_slots = max(2, (req_per_dev + req_devices - 1) // req_devices + 1)
    projected_rows = jnp.einsum(
        "td,kcd->ktc", stream, attention_projection_weight, preferred_element_type=jnp.float32
    )
    all_onehot = (
        token_adapter_index[:, None] == jnp.arange(adapter_number, dtype=jnp.int32)[None, :]
    )
    holder_count = adapter_down_maps.shape[0]
    holder_rank_rows = jnp.einsum(
        "qf,kfn->qkn", stream, adapter_down_maps, preferred_element_type=jnp.float32
    )
    held_onehot = (
        token_adapter_index[:, None]
        == (mdl_index * holder_count + jnp.arange(holder_count, dtype=jnp.int32))[None, :]
    )
    rank_part = jnp.sum(holder_rank_rows * held_onehot.astype(jnp.float32)[:, :, None], axis=1)
    rank_feat = lax.psum(rank_part.astype(jnp.bfloat16), "mdl")
    broadcast_result = (
        all_onehot.astype(jnp.bfloat16)[:, :, None] * rank_feat[:, None, :]
    ).reshape(tok_count, adapter_number * rank_total_width)
    adapter_column_set = jnp.einsum(
        "iu,pdu->ipd", broadcast_result, adapter_up_maps, preferred_element_type=jnp.float32
    )
    positions = jnp.arange(tok_count, dtype=jnp.int32)
    lengths_row = request_token_lengths[0]
    starts = jnp.cumsum(lengths_row) - lengths_row
    member = (positions[:, None] >= starts[None, :]) & (
        positions[:, None] < (starts + lengths_row)[None, :]
    )
    member_int = member.astype(jnp.int32)
    request_of = jnp.sum(member_int * jnp.arange(req_per_dev, dtype=jnp.int32)[None, :], axis=1)
    relative = positions - jnp.sum(member_int * starts[None, :], axis=1)
    tenant_hot = (
        request_tenant_index[:, None]
        == jnp.arange(tenant_adapter_scale.shape[0], dtype=jnp.int32)[None, :]
    ).astype(jnp.float32)
    request_scale = jnp.sum(tenant_hot * tenant_adapter_scale[None, :], axis=1)
    per_token_scale = jnp.sum(member.astype(jnp.float32) * request_scale[None, :], axis=1)[:, None]
    query_rows = (projected_rows[0] + per_token_scale * adapter_column_set[:, 0]).astype(
        jnp.bfloat16
    )
    key_rows = projected_rows[1].astype(jnp.bfloat16)
    value_row_block = (projected_rows[2] + per_token_scale * adapter_column_set[:, 1]).astype(
        jnp.bfloat16
    )
    owner_column = last_page_holder[:, 0]
    owner_table = owner_column.reshape(req_devices, req_per_dev)
    slot_table = holder_page_slot.reshape(req_devices, req_per_dev)
    owned = (owner_table == req_index).astype(jnp.int32)
    owned_rank = jnp.cumsum(owned, axis=1) - 1
    picked = owned[:, None, :] * (
        owned_rank[:, None, :] == jnp.arange(cap_slots, dtype=jnp.int32)[None, :, None]
    ).astype(jnp.int32)
    send_slot = jnp.sum(picked * slot_table[:, None, :], axis=2)
    fill_table = page_filled_rows.reshape(req_devices, req_per_dev)
    send_fill = jnp.sum(picked * fill_table[:, None, :], axis=2)
    my_owner = lax.dynamic_slice_in_dim(owner_column, req_index * req_per_dev, req_per_dev, 0)
    order_ids = jnp.arange(req_per_dev, dtype=jnp.int32)
    earlier = (my_owner[:, None] == my_owner[None, :]) & (order_ids[:, None] > order_ids[None, :])
    flat_pick = my_owner * cap_slots + jnp.sum(earlier.astype(jnp.int32), axis=1)
    page_inner = prefix_cache_store.shape[1:3]
    page_rows = prefix_cache_store.shape[3]
    source_pages = cut_windows(
        prefix_cache_store,
        jnp.clip(send_slot.reshape(-1), 0, prefix_cache_store.shape[0] - 1),
        send_fill.reshape(-1),
    )
    source_pages = source_pages.reshape((req_devices, cap_slots, 2, WINDOW, head_column_set))
    arrived = lax.all_to_all(source_pages, "req", split_axis=0, concat_axis=0, tiled=True)
    prefix = jnp.take(
        arrived.reshape((req_devices * cap_slots, 2, WINDOW, head_column_set)),
        flat_pick,
        axis=0,
        mode="clip",
    )
    key_all = jnp.concatenate(
        [key_rows, prefix[:, 0].reshape(req_per_dev * WINDOW, head_column_set)], axis=0
    )
    value_all = jnp.concatenate(
        [value_row_block, prefix[:, 1].reshape(req_per_dev * WINDOW, head_column_set)], axis=0
    )
    distance = positions[:, None] - positions[None, :]
    local_ok = (request_of[:, None] == request_of[None, :]) & (distance >= 0) & (distance <= WINDOW)
    key_request = jnp.repeat(jnp.arange(req_per_dev, dtype=jnp.int32), WINDOW)
    key_offset = jnp.tile(jnp.arange(WINDOW, dtype=jnp.int32), req_per_dev)
    prefix_ok = (request_of[:, None] == key_request[None, :]) & (
        key_offset[None, :] >= relative[:, None]
    )
    allowed = jnp.concatenate([local_ok, prefix_ok], axis=1)
    query_heads = query_rows.reshape(tok_count, head_local, HEAD_SIZE)
    key_heads = key_all.reshape(-1, head_local, HEAD_SIZE)
    value_heads = value_all.reshape(-1, head_local, HEAD_SIZE)
    scores = jnp.einsum(
        "thd,shd->hts", query_heads, key_heads, preferred_element_type=jnp.float32
    ) * (1.0 / math.sqrt(HEAD_SIZE))
    masked = jnp.where(allowed[None], scores, -1e30)
    row_max = jnp.max(masked, axis=-1, keepdims=True)
    exp_scores = jnp.exp(masked - row_max)
    weights = (exp_scores / jnp.sum(exp_scores, axis=-1, keepdims=True)).astype(jnp.bfloat16)
    mixed = (
        jnp.einsum("hts,shd->thd", weights, value_heads, preferred_element_type=jnp.float32)
        .astype(jnp.bfloat16)
        .reshape(tok_count, head_column_set)
    )
    attn_part = (
        jnp.dot(mixed, head_output_weight, preferred_element_type=jnp.float32)
        .astype(jnp.bfloat16)
        .astype(jnp.float32)
    )
    gain_wide = feedforward_norm_gain.astype(jnp.float32)[None, :]
    attn_full = lax.psum(attn_part.astype(jnp.bfloat16), "mdl").astype(jnp.float32)
    resid_full = (stream.astype(jnp.float32) + attn_full).astype(jnp.bfloat16)
    resid_wide = resid_full.astype(jnp.float32)
    mean_sq = jnp.mean(resid_wide * resid_wide, axis=1, keepdims=True)
    normed = (resid_wide * lax.rsqrt(mean_sq + 1e-06) * gain_wide).astype(jnp.bfloat16)
    resid_mine = lax.dynamic_slice_in_dim(resid_full, mdl_index * row_share, row_share, 0)
    full_mlp = lax.all_gather(feedforward_weight, "req", axis=1, tiled=True)
    mdl_devices = lax.axis_size("mdl")
    halves = 2
    normed_split = normed.reshape(mdl_devices, halves, row_share // halves, model_width)
    resid_split = resid_mine.reshape(halves, row_share // halves, model_width)
    outputs = []
    for half in range(halves):
        normed_half = normed_split[:, half].reshape(-1, model_width)
        gate_part = jnp.dot(normed_half, full_mlp[0], preferred_element_type=jnp.float32)
        up_part = jnp.dot(normed_half, full_mlp[1], preferred_element_type=jnp.float32)
        hidden = (jax.nn.silu(gate_part) * up_part).astype(jnp.bfloat16)
        mlp_part = jnp.einsum(
            "tf,df->td", hidden, full_mlp[2], preferred_element_type=jnp.float32
        ).astype(jnp.bfloat16)
        mlp_mine = lax.psum_scatter(mlp_part, "mdl", scatter_dimension=0, tiled=True).astype(
            jnp.float32
        )
        outputs.append((resid_split[half].astype(jnp.float32) + mlp_mine).astype(jnp.bfloat16))
    return jnp.concatenate(outputs, axis=0)


def solution(mesh):
    return jax.shard_map(
        per_device,
        mesh=mesh,
        in_specs=(
            P("req", None),
            P(None, "mdl", None),
            P("mdl", None),
            P("mdl", None, None),
            P(None, "mdl", None),
            P(),
            P(),
            P(None, "req", "mdl"),
            P("req", None, "mdl", None),
            P("req"),
            P("req", None),
            P("req"),
            P(),
            P(),
            P(),
        ),
        out_specs=P(("req", "mdl"), None),
        check_vma=False,
    )
```

```python
import math

import jax
import jax.numpy as jnp
from jax import lax
from jax.experimental import pallas as pl
from jax.experimental.pallas import tpu as pltpu
from jax.sharding import PartitionSpec as P

HEAD_SIZE = 112
WINDOW = 64


def window_kernel(slot_ref, fill_ref, store_ref, out_ref, held, sems):
    count = out_ref.shape[0]

    def fetch(i):
        return pltpu.make_async_copy(store_ref.at[slot_ref[i]], held.at[i], sems.at[i])

    def start(i, carry):
        fetch(i).start()
        return carry

    lax.fori_loop(0, count, start, 0)
    page_rows = held.shape[-1]
    row_ids = lax.broadcasted_iota(jnp.int32, (WINDOW, page_rows), 1)
    out_ids = lax.broadcasted_iota(jnp.int32, (WINDOW, page_rows), 0)

    def pick_rows(i, carry):
        fetch(i).wait()
        pick = (row_ids == out_ids + (fill_ref[i] - WINDOW)).astype(held.dtype)
        for part in range(held.shape[1]):
            out_ref[i, part] = lax.dot_general(
                pick, held[i, part], (((1,), (1,)), ((), ())), preferred_element_type=jnp.float32
            ).astype(out_ref.dtype)
        return carry

    lax.fori_loop(0, count, pick_rows, 0)


def cut_windows(store, slots, fills):
    count = slots.shape[0]
    parts, width, page_rows = store.shape[1:]
    return pl.pallas_call(
        window_kernel,
        grid_spec=pltpu.PrefetchScalarGridSpec(
            num_scalar_prefetch=2,
            grid=(1,),
            in_specs=[pl.BlockSpec(memory_space=pl.ANY)],
            out_specs=pl.BlockSpec(memory_space=pltpu.VMEM),
            scratch_shapes=[
                pltpu.VMEM((count, parts, width, page_rows), store.dtype),
                pltpu.SemaphoreType.DMA((count,)),
            ],
        ),
        out_shape=jax.ShapeDtypeStruct((count, parts, WINDOW, width), store.dtype),
    )(slots, fills, store)


def scatter_sum_kernel(part_ref, out_ref, got, send_sems, recv_sems):
    peers = lax.axis_size("mdl")
    rows = out_ref.shape[0]
    me = lax.axis_index("mdl")
    group = lax.axis_index("req")
    got[me] = part_ref[pl.ds(me * rows, rows)]
    barrier = pltpu.get_barrier_semaphore()

    def greet(k, carry):
        peer = lax.rem(me + k, peers)
        pl.semaphore_signal(barrier, inc=1, device_id=(group, peer), device_id_type=pl.DeviceIdType.MESH)
        return carry

    lax.fori_loop(1, peers, greet, 0)
    pl.semaphore_wait(barrier, peers - 1)

    def send(k):
        peer = lax.rem(me + k, peers)
        return pltpu.make_async_remote_copy(
            src_ref=part_ref.at[pl.ds(peer * rows, rows)],
            dst_ref=got.at[me],
            send_sem=send_sems.at[k],
            recv_sem=recv_sems.at[k],
            device_id=(group, peer),
            device_id_type=pl.DeviceIdType.MESH,
        )

    def start_send(k, carry):
        send(k).start()
        return carry

    lax.fori_loop(1, peers, start_send, 0)

    def finish(k, carry):
        send(k).wait()
        return carry

    lax.fori_loop(1, peers, finish, 0)
    total = got[0].astype(jnp.float32)
    for source in range(1, peers):
        total = total + got[source].astype(jnp.float32)
    out_ref[...] = total


def scatter_sum(part, peers, collective):
    rows = part.shape[0] // peers
    return pl.pallas_call(
        scatter_sum_kernel,
        in_specs=[pl.BlockSpec(memory_space=pltpu.VMEM)],
        out_specs=pl.BlockSpec(memory_space=pltpu.VMEM),
        scratch_shapes=[
            pltpu.VMEM((peers, rows) + part.shape[1:], part.dtype),
            pltpu.SemaphoreType.DMA((peers,)),
            pltpu.SemaphoreType.DMA((peers,)),
        ],
        out_shape=jax.ShapeDtypeStruct((rows,) + part.shape[1:], jnp.float32),
        compiler_params=pltpu.CompilerParams(collective_id=collective, has_side_effects=True),
    )(part)


def per_device(
    stream,
    attention_projection_weight,
    head_output_weight,
    adapter_down_maps,
    adapter_up_maps,
    tenant_adapter_scale,
    feedforward_norm_gain,
    feedforward_weight,
    prefix_cache_store,
    token_adapter_index,
    request_token_lengths,
    request_tenant_index,
    last_page_holder,
    holder_page_slot,
    page_filled_rows,
):
    tok_count, model_width = stream.shape
    head_column_set = attention_projection_weight.shape[1]
    head_local = head_column_set // HEAD_SIZE
    req_per_dev = request_token_lengths.shape[1]
    rank_total_width = adapter_down_maps.shape[2]
    adapter_number = adapter_up_maps.shape[2] // rank_total_width
    req_devices = lax.axis_size("req")
    req_index = lax.axis_index("req")
    mdl_index = lax.axis_index("mdl")
    row_share = tok_count // lax.axis_size("mdl")
    cap_slots = max(2, (req_per_dev + req_devices - 1) // req_devices + 1)
    projected_rows = jnp.einsum(
        "td,kcd->ktc", stream, attention_projection_weight, preferred_element_type=jnp.float32
    )
    all_onehot = (
        token_adapter_index[:, None] == jnp.arange(adapter_number, dtype=jnp.int32)[None, :]
    )
    holder_count = adapter_down_maps.shape[0]
    holder_rank_rows = jnp.einsum(
        "qf,kfn->qkn", stream, adapter_down_maps, preferred_element_type=jnp.float32
    )
    held_onehot = (
        token_adapter_index[:, None]
        == (mdl_index * holder_count + jnp.arange(holder_count, dtype=jnp.int32))[None, :]
    )
    rank_part = jnp.sum(holder_rank_rows * held_onehot.astype(jnp.float32)[:, :, None], axis=1)
    rank_feat = lax.psum(rank_part.astype(jnp.bfloat16), "mdl")
    broadcast_result = (
        all_onehot.astype(jnp.bfloat16)[:, :, None] * rank_feat[:, None, :]
    ).reshape(tok_count, adapter_number * rank_total_width)
    adapter_column_set = jnp.einsum(
        "iu,pdu->ipd", broadcast_result, adapter_up_maps, preferred_element_type=jnp.float32
    )
    positions = jnp.arange(tok_count, dtype=jnp.int32)
    lengths_row = request_token_lengths[0]
    starts = jnp.cumsum(lengths_row) - lengths_row
    member = (positions[:, None] >= starts[None, :]) & (
        positions[:, None] < (starts + lengths_row)[None, :]
    )
    member_int = member.astype(jnp.int32)
    request_of = jnp.sum(member_int * jnp.arange(req_per_dev, dtype=jnp.int32)[None, :], axis=1)
    relative = positions - jnp.sum(member_int * starts[None, :], axis=1)
    tenant_hot = (
        request_tenant_index[:, None]
        == jnp.arange(tenant_adapter_scale.shape[0], dtype=jnp.int32)[None, :]
    ).astype(jnp.float32)
    request_scale = jnp.sum(tenant_hot * tenant_adapter_scale[None, :], axis=1)
    per_token_scale = jnp.sum(member.astype(jnp.float32) * request_scale[None, :], axis=1)[:, None]
    query_rows = (projected_rows[0] + per_token_scale * adapter_column_set[:, 0]).astype(
        jnp.bfloat16
    )
    key_rows = projected_rows[1].astype(jnp.bfloat16)
    value_row_block = (projected_rows[2] + per_token_scale * adapter_column_set[:, 1]).astype(
        jnp.bfloat16
    )
    owner_column = last_page_holder[:, 0]
    owner_table = owner_column.reshape(req_devices, req_per_dev)
    slot_table = holder_page_slot.reshape(req_devices, req_per_dev)
    owned = (owner_table == req_index).astype(jnp.int32)
    owned_rank = jnp.cumsum(owned, axis=1) - 1
    picked = owned[:, None, :] * (
        owned_rank[:, None, :] == jnp.arange(cap_slots, dtype=jnp.int32)[None, :, None]
    ).astype(jnp.int32)
    send_slot = jnp.sum(picked * slot_table[:, None, :], axis=2)
    fill_table = page_filled_rows.reshape(req_devices, req_per_dev)
    send_fill = jnp.sum(picked * fill_table[:, None, :], axis=2)
    my_owner = lax.dynamic_slice_in_dim(owner_column, req_index * req_per_dev, req_per_dev, 0)
    order_ids = jnp.arange(req_per_dev, dtype=jnp.int32)
    earlier = (my_owner[:, None] == my_owner[None, :]) & (order_ids[:, None] > order_ids[None, :])
    flat_pick = my_owner * cap_slots + jnp.sum(earlier.astype(jnp.int32), axis=1)
    page_inner = prefix_cache_store.shape[1:3]
    page_rows = prefix_cache_store.shape[3]
    source_pages = cut_windows(
        prefix_cache_store,
        jnp.clip(send_slot.reshape(-1), 0, prefix_cache_store.shape[0] - 1),
        send_fill.reshape(-1),
    )
    source_pages = source_pages.reshape((req_devices, cap_slots, 2, WINDOW, head_column_set))
    arrived = lax.all_to_all(source_pages, "req", split_axis=0, concat_axis=0, tiled=True)
    prefix = jnp.take(
        arrived.reshape((req_devices * cap_slots, 2, WINDOW, head_column_set)),
        flat_pick,
        axis=0,
        mode="clip",
    )
    key_all = jnp.concatenate(
        [key_rows, prefix[:, 0].reshape(req_per_dev * WINDOW, head_column_set)], axis=0
    )
    value_all = jnp.concatenate(
        [value_row_block, prefix[:, 1].reshape(req_per_dev * WINDOW, head_column_set)], axis=0
    )
    distance = positions[:, None] - positions[None, :]
    local_ok = (request_of[:, None] == request_of[None, :]) & (distance >= 0) & (distance <= WINDOW)
    key_request = jnp.repeat(jnp.arange(req_per_dev, dtype=jnp.int32), WINDOW)
    key_offset = jnp.tile(jnp.arange(WINDOW, dtype=jnp.int32), req_per_dev)
    prefix_ok = (request_of[:, None] == key_request[None, :]) & (
        key_offset[None, :] >= relative[:, None]
    )
    allowed = jnp.concatenate([local_ok, prefix_ok], axis=1)
    query_heads = query_rows.reshape(tok_count, head_local, HEAD_SIZE)
    key_heads = key_all.reshape(-1, head_local, HEAD_SIZE)
    value_heads = value_all.reshape(-1, head_local, HEAD_SIZE)
    scores = jnp.einsum(
        "thd,shd->hts", query_heads, key_heads, preferred_element_type=jnp.float32
    ) * (1.0 / math.sqrt(HEAD_SIZE))
    masked = jnp.where(allowed[None], scores, -1e30)
    row_max = jnp.max(masked, axis=-1, keepdims=True)
    exp_scores = jnp.exp(masked - row_max)
    weights = (exp_scores / jnp.sum(exp_scores, axis=-1, keepdims=True)).astype(jnp.bfloat16)
    mixed = (
        jnp.einsum("hts,shd->thd", weights, value_heads, preferred_element_type=jnp.float32)
        .astype(jnp.bfloat16)
        .reshape(tok_count, head_column_set)
    )
    attn_part = (
        jnp.dot(mixed, head_output_weight, preferred_element_type=jnp.float32)
        .astype(jnp.bfloat16)
        .astype(jnp.float32)
    )
    gain_wide = feedforward_norm_gain.astype(jnp.float32)[None, :]
    attn_full = lax.psum(attn_part.astype(jnp.bfloat16), "mdl").astype(jnp.float32)
    resid_full = (stream.astype(jnp.float32) + attn_full).astype(jnp.bfloat16)
    resid_wide = resid_full.astype(jnp.float32)
    mean_sq = jnp.mean(resid_wide * resid_wide, axis=1, keepdims=True)
    normed = (resid_wide * lax.rsqrt(mean_sq + 1e-06) * gain_wide).astype(jnp.bfloat16)
    resid_mine = lax.dynamic_slice_in_dim(resid_full, mdl_index * row_share, row_share, 0)
    full_mlp = lax.all_gather(feedforward_weight, "req", axis=1, tiled=True)
    gate_part = jnp.dot(normed, full_mlp[0], preferred_element_type=jnp.float32)
    up_part = jnp.dot(normed, full_mlp[1], preferred_element_type=jnp.float32)
    hidden = (jax.nn.silu(gate_part) * up_part).astype(jnp.bfloat16)
    mlp_part = (
        jnp.einsum("tf,df->td", hidden, full_mlp[2], preferred_element_type=jnp.float32)
        .astype(jnp.bfloat16)
        .astype(jnp.float32)
    )
    mlp_mine = scatter_sum(mlp_part.astype(jnp.bfloat16), lax.axis_size("mdl"), 1)
    return (resid_mine.astype(jnp.float32) + mlp_mine).astype(jnp.bfloat16)


def solution(mesh):
    return jax.shard_map(
        per_device,
        mesh=mesh,
        in_specs=(
            P("req", None),
            P(None, "mdl", None),
            P("mdl", None),
            P("mdl", None, None),
            P(None, "mdl", None),
            P(),
            P(),
            P(None, "req", "mdl"),
            P("req", None, "mdl", None),
            P("req"),
            P("req", None),
            P("req"),
            P(),
            P(),
            P(),
        ),
        out_specs=P(("req", "mdl"), None),
        check_vma=False,
    )
```

```python
import math

import jax
import jax.numpy as jnp
from jax import lax
from jax.experimental import pallas as pl
from jax.experimental.pallas import tpu as pltpu
from jax.sharding import PartitionSpec as P

HEAD_SIZE = 112
WINDOW = 64


def window_kernel(slot_ref, fill_ref, store_ref, out_ref, held, sems):
    count = out_ref.shape[0]

    def fetch(i):
        return pltpu.make_async_copy(store_ref.at[slot_ref[i]], held.at[i], sems.at[i])

    def start(i, carry):
        fetch(i).start()
        return carry

    lax.fori_loop(0, count, start, 0)
    page_rows = held.shape[-1]
    row_ids = lax.broadcasted_iota(jnp.int32, (WINDOW, page_rows), 1)
    out_ids = lax.broadcasted_iota(jnp.int32, (WINDOW, page_rows), 0)

    def pick_rows(i, carry):
        fetch(i).wait()
        pick = (row_ids == out_ids + (fill_ref[i] - WINDOW)).astype(held.dtype)
        for part in range(held.shape[1]):
            out_ref[i, part] = lax.dot_general(
                pick, held[i, part], (((1,), (1,)), ((), ())), preferred_element_type=jnp.float32
            ).astype(out_ref.dtype)
        return carry

    lax.fori_loop(0, count, pick_rows, 0)


def cut_windows(store, slots, fills):
    count = slots.shape[0]
    parts, width, page_rows = store.shape[1:]
    return pl.pallas_call(
        window_kernel,
        grid_spec=pltpu.PrefetchScalarGridSpec(
            num_scalar_prefetch=2,
            grid=(1,),
            in_specs=[pl.BlockSpec(memory_space=pl.ANY)],
            out_specs=pl.BlockSpec(memory_space=pltpu.VMEM),
            scratch_shapes=[
                pltpu.VMEM((count, parts, width, page_rows), store.dtype),
                pltpu.SemaphoreType.DMA((count,)),
            ],
        ),
        out_shape=jax.ShapeDtypeStruct((count, parts, WINDOW, width), store.dtype),
    )(slots, fills, store)


def per_device(
    stream,
    attention_projection_weight,
    head_output_weight,
    adapter_down_maps,
    adapter_up_maps,
    tenant_adapter_scale,
    feedforward_norm_gain,
    feedforward_weight,
    prefix_cache_store,
    token_adapter_index,
    request_token_lengths,
    request_tenant_index,
    last_page_holder,
    holder_page_slot,
    page_filled_rows,
):
    tok_count, model_width = stream.shape
    head_column_set = attention_projection_weight.shape[1]
    head_local = head_column_set // HEAD_SIZE
    req_per_dev = request_token_lengths.shape[1]
    rank_total_width = adapter_down_maps.shape[2]
    adapter_number = adapter_up_maps.shape[2] // rank_total_width
    req_devices = lax.axis_size("req")
    req_index = lax.axis_index("req")
    mdl_index = lax.axis_index("mdl")
    row_share = tok_count // lax.axis_size("mdl")
    cap_slots = max(2, (req_per_dev + req_devices - 1) // req_devices + 1)
    projected_rows = jnp.einsum(
        "td,kcd->ktc", stream, attention_projection_weight, preferred_element_type=jnp.float32
    )
    all_onehot = (
        token_adapter_index[:, None] == jnp.arange(adapter_number, dtype=jnp.int32)[None, :]
    )
    holder_count = adapter_down_maps.shape[0]
    holder_rank_rows = jnp.einsum(
        "qf,kfn->qkn", stream, adapter_down_maps, preferred_element_type=jnp.float32
    )
    held_onehot = (
        token_adapter_index[:, None]
        == (mdl_index * holder_count + jnp.arange(holder_count, dtype=jnp.int32))[None, :]
    )
    rank_part = jnp.sum(holder_rank_rows * held_onehot.astype(jnp.float32)[:, :, None], axis=1)
    rank_feat = lax.psum(rank_part.astype(jnp.bfloat16), "mdl")
    broadcast_result = (
        all_onehot.astype(jnp.bfloat16)[:, :, None] * rank_feat[:, None, :]
    ).reshape(tok_count, adapter_number * rank_total_width)
    adapter_column_set = jnp.einsum(
        "iu,pdu->ipd", broadcast_result, adapter_up_maps, preferred_element_type=jnp.float32
    )
    positions = jnp.arange(tok_count, dtype=jnp.int32)
    lengths_row = request_token_lengths[0]
    starts = jnp.cumsum(lengths_row) - lengths_row
    member = (positions[:, None] >= starts[None, :]) & (
        positions[:, None] < (starts + lengths_row)[None, :]
    )
    member_int = member.astype(jnp.int32)
    request_of = jnp.sum(member_int * jnp.arange(req_per_dev, dtype=jnp.int32)[None, :], axis=1)
    relative = positions - jnp.sum(member_int * starts[None, :], axis=1)
    tenant_hot = (
        request_tenant_index[:, None]
        == jnp.arange(tenant_adapter_scale.shape[0], dtype=jnp.int32)[None, :]
    ).astype(jnp.float32)
    request_scale = jnp.sum(tenant_hot * tenant_adapter_scale[None, :], axis=1)
    per_token_scale = jnp.sum(member.astype(jnp.float32) * request_scale[None, :], axis=1)[:, None]
    query_rows = (projected_rows[0] + per_token_scale * adapter_column_set[:, 0]).astype(
        jnp.bfloat16
    )
    key_rows = projected_rows[1].astype(jnp.bfloat16)
    value_row_block = (projected_rows[2] + per_token_scale * adapter_column_set[:, 1]).astype(
        jnp.bfloat16
    )
    owner_column = last_page_holder[:, 0]
    owner_table = owner_column.reshape(req_devices, req_per_dev)
    slot_table = holder_page_slot.reshape(req_devices, req_per_dev)
    owned = (owner_table == req_index).astype(jnp.int32)
    owned_rank = jnp.cumsum(owned, axis=1) - 1
    picked = owned[:, None, :] * (
        owned_rank[:, None, :] == jnp.arange(cap_slots, dtype=jnp.int32)[None, :, None]
    ).astype(jnp.int32)
    send_slot = jnp.sum(picked * slot_table[:, None, :], axis=2)
    fill_table = page_filled_rows.reshape(req_devices, req_per_dev)
    send_fill = jnp.sum(picked * fill_table[:, None, :], axis=2)
    my_owner = lax.dynamic_slice_in_dim(owner_column, req_index * req_per_dev, req_per_dev, 0)
    order_ids = jnp.arange(req_per_dev, dtype=jnp.int32)
    earlier = (my_owner[:, None] == my_owner[None, :]) & (order_ids[:, None] > order_ids[None, :])
    flat_pick = my_owner * cap_slots + jnp.sum(earlier.astype(jnp.int32), axis=1)
    page_inner = prefix_cache_store.shape[1:3]
    page_rows = prefix_cache_store.shape[3]
    source_pages = cut_windows(
        prefix_cache_store,
        jnp.clip(send_slot.reshape(-1), 0, prefix_cache_store.shape[0] - 1),
        send_fill.reshape(-1),
    )
    source_pages = source_pages.reshape((req_devices, cap_slots, 2, WINDOW, head_column_set))
    arrived = lax.all_to_all(source_pages, "req", split_axis=0, concat_axis=0, tiled=True)
    prefix = jnp.take(
        arrived.reshape((req_devices * cap_slots, 2, WINDOW, head_column_set)),
        flat_pick,
        axis=0,
        mode="clip",
    )
    ext_len = tok_count + req_per_dev * WINDOW
    block_count = ext_len // WINDOW
    ext_pos = jnp.arange(ext_len, dtype=jnp.int32)
    ext_start = starts + WINDOW * jnp.arange(req_per_dev, dtype=jnp.int32)
    in_req = (
        (ext_pos[:, None] >= ext_start[None, :])
        & (ext_pos[:, None] < (ext_start + WINDOW + lengths_row)[None, :])
    ).astype(jnp.int32)
    ext_req = jnp.sum(in_req * jnp.arange(req_per_dev, dtype=jnp.int32)[None, :], axis=1)
    ext_off = ext_pos - jnp.sum(in_req * ext_start[None, :], axis=1)
    token_src = jnp.sum(in_req * starts[None, :], axis=1) + ext_off - WINDOW
    prefix_src = tok_count + ext_req * WINDOW + ext_off
    src = jnp.where(ext_off < WINDOW, prefix_src, token_src)
    key_all = jnp.concatenate(
        [key_rows, prefix[:, 0].reshape(req_per_dev * WINDOW, head_column_set)], axis=0
    )
    value_all = jnp.concatenate(
        [value_row_block, prefix[:, 1].reshape(req_per_dev * WINDOW, head_column_set)], axis=0
    )
    key_ext = jnp.take(key_all, src, axis=0, mode="clip")
    value_ext = jnp.take(value_all, src, axis=0, mode="clip")
    query_ext = jnp.take(query_rows, jnp.clip(src, 0, tok_count - 1), axis=0, mode="clip")

    def pair_blocks(rows, fill):
        padded = jnp.concatenate(
            [jnp.full((WINDOW,) + rows.shape[1:], fill, rows.dtype), rows], axis=0
        ).reshape((block_count + 1, WINDOW) + rows.shape[1:])
        return jnp.concatenate([padded[:-1], padded[1:]], axis=1)

    query_heads = query_ext.reshape(block_count, WINDOW, head_local, HEAD_SIZE)
    key_heads = pair_blocks(key_ext, 0).reshape(block_count, 2 * WINDOW, head_local, HEAD_SIZE)
    value_heads = pair_blocks(value_ext, 0).reshape(block_count, 2 * WINDOW, head_local, HEAD_SIZE)
    key_req = pair_blocks(ext_req, -1)
    query_req = ext_req.reshape(block_count, WINDOW)
    gap = WINDOW + jnp.arange(WINDOW, dtype=jnp.int32)[:, None] - jnp.arange(2 * WINDOW, dtype=jnp.int32)[None, :]
    allowed = (query_req[:, :, None] == key_req[:, None, :]) & (gap >= 0)[None] & (gap <= WINDOW)[None]
    scores = jnp.einsum(
        "bqhd,bkhd->hbqk", query_heads, key_heads, preferred_element_type=jnp.float32
    ) * (1.0 / math.sqrt(HEAD_SIZE))
    masked = jnp.where(allowed[None], scores, -1e30)
    row_max = jnp.max(masked, axis=-1, keepdims=True)
    exp_scores = jnp.exp(masked - row_max)
    weights = (exp_scores / jnp.sum(exp_scores, axis=-1, keepdims=True)).astype(jnp.bfloat16)
    mixed_ext = (
        jnp.einsum("hbqk,bkhd->bqhd", weights, value_heads, preferred_element_type=jnp.float32)
        .astype(jnp.bfloat16)
        .reshape(ext_len, head_column_set)
    )
    token_ext = positions + WINDOW * (request_of + 1)
    mixed = jnp.take(mixed_ext, token_ext, axis=0, mode="clip")
    attn_part = (
        jnp.dot(mixed, head_output_weight, preferred_element_type=jnp.float32)
        .astype(jnp.bfloat16)
        .astype(jnp.float32)
    )
    gain_wide = feedforward_norm_gain.astype(jnp.float32)[None, :]
    attn_full = lax.psum(attn_part.astype(jnp.bfloat16), "mdl").astype(jnp.float32)
    resid_full = (stream.astype(jnp.float32) + attn_full).astype(jnp.bfloat16)
    resid_wide = resid_full.astype(jnp.float32)
    mean_sq = jnp.mean(resid_wide * resid_wide, axis=1, keepdims=True)
    normed = (resid_wide * lax.rsqrt(mean_sq + 1e-06) * gain_wide).astype(jnp.bfloat16)
    resid_mine = lax.dynamic_slice_in_dim(resid_full, mdl_index * row_share, row_share, 0)
    full_mlp = lax.all_gather(feedforward_weight, "req", axis=1, tiled=True)
    gate_part = jnp.dot(normed, full_mlp[0], preferred_element_type=jnp.float32)
    up_part = jnp.dot(normed, full_mlp[1], preferred_element_type=jnp.float32)
    hidden = (jax.nn.silu(gate_part) * up_part).astype(jnp.bfloat16)
    mlp_part = (
        jnp.einsum("tf,df->td", hidden, full_mlp[2], preferred_element_type=jnp.float32)
        .astype(jnp.bfloat16)
        .astype(jnp.float32)
    )
    mlp_mine = lax.psum_scatter(
        mlp_part.astype(jnp.bfloat16), "mdl", scatter_dimension=0, tiled=True
    ).astype(jnp.float32)
    return (resid_mine.astype(jnp.float32) + mlp_mine).astype(jnp.bfloat16)


def solution(mesh):
    return jax.shard_map(
        per_device,
        mesh=mesh,
        in_specs=(
            P("req", None),
            P(None, "mdl", None),
            P("mdl", None),
            P("mdl", None, None),
            P(None, "mdl", None),
            P(),
            P(),
            P(None, "req", "mdl"),
            P("req", None, "mdl", None),
            P("req"),
            P("req", None),
            P("req"),
            P(),
            P(),
            P(),
        ),
        out_specs=P(("req", "mdl"), None),
        check_vma=False,
    )
```

```python
import math

import jax
import jax.numpy as jnp
from jax import lax
from jax.experimental import pallas as pl
from jax.experimental.pallas import tpu as pltpu
from jax.sharding import PartitionSpec as P

HEAD_SIZE = 112
WINDOW = 64


def window_kernel(slot_ref, fill_ref, store_ref, out_ref, held, sems):
    count = out_ref.shape[0]

    def fetch(i):
        return pltpu.make_async_copy(store_ref.at[slot_ref[i]], held.at[i], sems.at[i])

    def start(i, carry):
        fetch(i).start()
        return carry

    lax.fori_loop(0, count, start, 0, unroll=8)
    page_rows = held.shape[-1]
    row_ids = lax.broadcasted_iota(jnp.int32, (WINDOW, page_rows), 1)
    out_ids = lax.broadcasted_iota(jnp.int32, (WINDOW, page_rows), 0)

    def pick_rows(i, carry):
        fetch(i).wait()
        pick = (row_ids == out_ids + (fill_ref[i] - WINDOW)).astype(held.dtype)
        for part in range(held.shape[1]):
            out_ref[i, part] = lax.dot_general(
                pick, held[i, part], (((1,), (1,)), ((), ())), preferred_element_type=jnp.float32
            ).astype(out_ref.dtype)
        return carry

    lax.fori_loop(0, count, pick_rows, 0, unroll=8)


def cut_windows(store, slots, fills):
    count = slots.shape[0]
    parts, width, page_rows = store.shape[1:]
    return pl.pallas_call(
        window_kernel,
        grid_spec=pltpu.PrefetchScalarGridSpec(
            num_scalar_prefetch=2,
            grid=(1,),
            in_specs=[pl.BlockSpec(memory_space=pl.ANY)],
            out_specs=pl.BlockSpec(memory_space=pltpu.VMEM),
            scratch_shapes=[
                pltpu.VMEM((count, parts, width, page_rows), store.dtype),
                pltpu.SemaphoreType.DMA((count,)),
            ],
        ),
        out_shape=jax.ShapeDtypeStruct((count, parts, WINDOW, width), store.dtype),
    )(slots, fills, store)


def per_device(
    stream,
    attention_projection_weight,
    head_output_weight,
    adapter_down_maps,
    adapter_up_maps,
    tenant_adapter_scale,
    feedforward_norm_gain,
    feedforward_weight,
    prefix_cache_store,
    token_adapter_index,
    request_token_lengths,
    request_tenant_index,
    last_page_holder,
    holder_page_slot,
    page_filled_rows,
):
    tok_count, model_width = stream.shape
    head_column_set = attention_projection_weight.shape[1]
    head_local = head_column_set // HEAD_SIZE
    req_per_dev = request_token_lengths.shape[1]
    rank_total_width = adapter_down_maps.shape[2]
    adapter_number = adapter_up_maps.shape[2] // rank_total_width
    req_devices = lax.axis_size("req")
    req_index = lax.axis_index("req")
    mdl_index = lax.axis_index("mdl")
    row_share = tok_count // lax.axis_size("mdl")
    cap_slots = max(2, (req_per_dev + req_devices - 1) // req_devices + 1)
    projected_rows = jnp.einsum(
        "td,kcd->ktc", stream, attention_projection_weight, preferred_element_type=jnp.float32
    )
    all_onehot = (
        token_adapter_index[:, None] == jnp.arange(adapter_number, dtype=jnp.int32)[None, :]
    )
    holder_count = adapter_down_maps.shape[0]
    holder_rank_rows = jnp.einsum(
        "qf,kfn->qkn", stream, adapter_down_maps, preferred_element_type=jnp.float32
    )
    held_onehot = (
        token_adapter_index[:, None]
        == (mdl_index * holder_count + jnp.arange(holder_count, dtype=jnp.int32))[None, :]
    )
    rank_part = jnp.sum(holder_rank_rows * held_onehot.astype(jnp.float32)[:, :, None], axis=1)
    rank_feat = lax.psum(rank_part.astype(jnp.bfloat16), "mdl")
    broadcast_result = (
        all_onehot.astype(jnp.bfloat16)[:, :, None] * rank_feat[:, None, :]
    ).reshape(tok_count, adapter_number * rank_total_width)
    adapter_column_set = jnp.einsum(
        "iu,pdu->ipd", broadcast_result, adapter_up_maps, preferred_element_type=jnp.float32
    )
    positions = jnp.arange(tok_count, dtype=jnp.int32)
    lengths_row = request_token_lengths[0]
    starts = jnp.cumsum(lengths_row) - lengths_row
    member = (positions[:, None] >= starts[None, :]) & (
        positions[:, None] < (starts + lengths_row)[None, :]
    )
    member_int = member.astype(jnp.int32)
    request_of = jnp.sum(member_int * jnp.arange(req_per_dev, dtype=jnp.int32)[None, :], axis=1)
    relative = positions - jnp.sum(member_int * starts[None, :], axis=1)
    tenant_hot = (
        request_tenant_index[:, None]
        == jnp.arange(tenant_adapter_scale.shape[0], dtype=jnp.int32)[None, :]
    ).astype(jnp.float32)
    request_scale = jnp.sum(tenant_hot * tenant_adapter_scale[None, :], axis=1)
    per_token_scale = jnp.sum(member.astype(jnp.float32) * request_scale[None, :], axis=1)[:, None]
    query_rows = (projected_rows[0] + per_token_scale * adapter_column_set[:, 0]).astype(
        jnp.bfloat16
    )
    key_rows = projected_rows[1].astype(jnp.bfloat16)
    value_row_block = (projected_rows[2] + per_token_scale * adapter_column_set[:, 1]).astype(
        jnp.bfloat16
    )
    owner_column = last_page_holder[:, 0]
    owner_table = owner_column.reshape(req_devices, req_per_dev)
    slot_table = holder_page_slot.reshape(req_devices, req_per_dev)
    owned = (owner_table == req_index).astype(jnp.int32)
    owned_rank = jnp.cumsum(owned, axis=1) - 1
    picked = owned[:, None, :] * (
        owned_rank[:, None, :] == jnp.arange(cap_slots, dtype=jnp.int32)[None, :, None]
    ).astype(jnp.int32)
    send_slot = jnp.sum(picked * slot_table[:, None, :], axis=2)
    fill_table = page_filled_rows.reshape(req_devices, req_per_dev)
    send_fill = jnp.sum(picked * fill_table[:, None, :], axis=2)
    my_owner = lax.dynamic_slice_in_dim(owner_column, req_index * req_per_dev, req_per_dev, 0)
    order_ids = jnp.arange(req_per_dev, dtype=jnp.int32)
    earlier = (my_owner[:, None] == my_owner[None, :]) & (order_ids[:, None] > order_ids[None, :])
    flat_pick = my_owner * cap_slots + jnp.sum(earlier.astype(jnp.int32), axis=1)
    page_inner = prefix_cache_store.shape[1:3]
    page_rows = prefix_cache_store.shape[3]
    source_pages = cut_windows(
        prefix_cache_store,
        jnp.clip(send_slot.reshape(-1), 0, prefix_cache_store.shape[0] - 1),
        send_fill.reshape(-1),
    )
    source_pages = source_pages.reshape((req_devices, cap_slots, 2, WINDOW, head_column_set))
    arrived = lax.all_to_all(source_pages, "req", split_axis=0, concat_axis=0, tiled=True)
    prefix = jnp.take(
        arrived.reshape((req_devices * cap_slots, 2, WINDOW, head_column_set)),
        flat_pick,
        axis=0,
        mode="clip",
    )
    key_all = jnp.concatenate(
        [key_rows, prefix[:, 0].reshape(req_per_dev * WINDOW, head_column_set)], axis=0
    )
    value_all = jnp.concatenate(
        [value_row_block, prefix[:, 1].reshape(req_per_dev * WINDOW, head_column_set)], axis=0
    )
    distance = positions[:, None] - positions[None, :]
    local_ok = (request_of[:, None] == request_of[None, :]) & (distance >= 0) & (distance <= WINDOW)
    key_request = jnp.repeat(jnp.arange(req_per_dev, dtype=jnp.int32), WINDOW)
    key_offset = jnp.tile(jnp.arange(WINDOW, dtype=jnp.int32), req_per_dev)
    prefix_ok = (request_of[:, None] == key_request[None, :]) & (
        key_offset[None, :] >= relative[:, None]
    )
    allowed = jnp.concatenate([local_ok, prefix_ok], axis=1)
    query_heads = query_rows.reshape(tok_count, head_local, HEAD_SIZE)
    key_heads = key_all.reshape(-1, head_local, HEAD_SIZE)
    value_heads = value_all.reshape(-1, head_local, HEAD_SIZE)
    scores = jnp.einsum(
        "thd,shd->hts", query_heads, key_heads, preferred_element_type=jnp.float32
    ) * (1.0 / math.sqrt(HEAD_SIZE))
    masked = jnp.where(allowed[None], scores, -1e30)
    row_max = jnp.max(masked, axis=-1, keepdims=True)
    exp_scores = jnp.exp(masked - row_max)
    weights = (exp_scores / jnp.sum(exp_scores, axis=-1, keepdims=True)).astype(jnp.bfloat16)
    mixed = (
        jnp.einsum("hts,shd->thd", weights, value_heads, preferred_element_type=jnp.float32)
        .astype(jnp.bfloat16)
        .reshape(tok_count, head_column_set)
    )
    attn_part = (
        jnp.dot(mixed, head_output_weight, preferred_element_type=jnp.float32)
        .astype(jnp.bfloat16)
        .astype(jnp.float32)
    )
    gain_wide = feedforward_norm_gain.astype(jnp.float32)[None, :]
    attn_full = lax.psum(attn_part.astype(jnp.bfloat16), "mdl").astype(jnp.float32)
    resid_full = (stream.astype(jnp.float32) + attn_full).astype(jnp.bfloat16)
    resid_wide = resid_full.astype(jnp.float32)
    mean_sq = jnp.mean(resid_wide * resid_wide, axis=1, keepdims=True)
    normed = (resid_wide * lax.rsqrt(mean_sq + 1e-06) * gain_wide).astype(jnp.bfloat16)
    resid_mine = lax.dynamic_slice_in_dim(resid_full, mdl_index * row_share, row_share, 0)
    full_mlp = lax.all_gather(feedforward_weight, "req", axis=1, tiled=True)
    gate_part = jnp.dot(normed, full_mlp[0], preferred_element_type=jnp.float32)
    up_part = jnp.dot(normed, full_mlp[1], preferred_element_type=jnp.float32)
    hidden = (jax.nn.silu(gate_part) * up_part).astype(jnp.bfloat16)
    mlp_part = (
        jnp.einsum("tf,df->td", hidden, full_mlp[2], preferred_element_type=jnp.float32)
        .astype(jnp.bfloat16)
        .astype(jnp.float32)
    )
    mlp_mine = lax.psum_scatter(
        mlp_part.astype(jnp.bfloat16), "mdl", scatter_dimension=0, tiled=True
    ).astype(jnp.float32)
    return (resid_mine.astype(jnp.float32) + mlp_mine).astype(jnp.bfloat16)


def solution(mesh):
    return jax.shard_map(
        per_device,
        mesh=mesh,
        in_specs=(
            P("req", None),
            P(None, "mdl", None),
            P("mdl", None),
            P("mdl", None, None),
            P(None, "mdl", None),
            P(),
            P(),
            P(None, "req", "mdl"),
            P("req", None, "mdl", None),
            P("req"),
            P("req", None),
            P("req"),
            P(),
            P(),
            P(),
        ),
        out_specs=P(("req", "mdl"), None),
        check_vma=False,
    )
```

```python
import math

import jax
import jax.numpy as jnp
from jax import lax
from jax.experimental import pallas as pl
from jax.experimental.pallas import tpu as pltpu
from jax.sharding import PartitionSpec as P

HEAD_SIZE = 112
WINDOW = 64


def window_kernel(slot_ref, fill_ref, store_ref, out_ref, held, sems):
    count = out_ref.shape[0]

    def fetch(i):
        return pltpu.make_async_copy(store_ref.at[slot_ref[i]], held.at[i], sems.at[i])

    def start(i, carry):
        fetch(i).start()
        return carry

    lax.fori_loop(0, count, start, 0, unroll=8)
    page_rows = held.shape[-1]
    row_ids = lax.broadcasted_iota(jnp.int32, (WINDOW, page_rows), 1)
    out_ids = lax.broadcasted_iota(jnp.int32, (WINDOW, page_rows), 0)

    def pick_rows(i, carry):
        fetch(i).wait()
        pick = (row_ids == out_ids + (fill_ref[i] - WINDOW)).astype(held.dtype)
        for part in range(held.shape[1]):
            out_ref[i, part] = lax.dot_general(
                pick, held[i, part], (((1,), (1,)), ((), ())), preferred_element_type=jnp.float32
            ).astype(out_ref.dtype)
        return carry

    lax.fori_loop(0, count, pick_rows, 0, unroll=8)


def cut_windows(store, slots, fills):
    count = slots.shape[0]
    parts, width, page_rows = store.shape[1:]
    return pl.pallas_call(
        window_kernel,
        grid_spec=pltpu.PrefetchScalarGridSpec(
            num_scalar_prefetch=2,
            grid=(1,),
            in_specs=[pl.BlockSpec(memory_space=pl.ANY)],
            out_specs=pl.BlockSpec(memory_space=pltpu.VMEM),
            scratch_shapes=[
                pltpu.VMEM((count, parts, width, page_rows), store.dtype),
                pltpu.SemaphoreType.DMA((count,)),
            ],
        ),
        out_shape=jax.ShapeDtypeStruct((count, parts, WINDOW, width), store.dtype),
    )(slots, fills, store)


def per_device(
    stream,
    attention_projection_weight,
    head_output_weight,
    adapter_down_maps,
    adapter_up_maps,
    tenant_adapter_scale,
    feedforward_norm_gain,
    feedforward_weight,
    prefix_cache_store,
    token_adapter_index,
    request_token_lengths,
    request_tenant_index,
    last_page_holder,
    holder_page_slot,
    page_filled_rows,
):
    tok_count, model_width = stream.shape
    head_column_set = attention_projection_weight.shape[1]
    head_local = head_column_set // HEAD_SIZE
    req_per_dev = request_token_lengths.shape[1]
    rank_total_width = adapter_down_maps.shape[2]
    adapter_number = adapter_up_maps.shape[2] // rank_total_width
    req_devices = lax.axis_size("req")
    req_index = lax.axis_index("req")
    mdl_index = lax.axis_index("mdl")
    row_share = tok_count // lax.axis_size("mdl")
    cap_slots = max(2, (req_per_dev + req_devices - 1) // req_devices + 1)
    projected_rows = jnp.einsum(
        "td,kcd->ktc", stream, attention_projection_weight, preferred_element_type=jnp.float32
    )
    all_onehot = (
        token_adapter_index[:, None] == jnp.arange(adapter_number, dtype=jnp.int32)[None, :]
    )
    holder_count = adapter_down_maps.shape[0]
    holder_rank_rows = jnp.einsum(
        "qf,kfn->qkn", stream, adapter_down_maps, preferred_element_type=jnp.float32
    )
    held_onehot = (
        token_adapter_index[:, None]
        == (mdl_index * holder_count + jnp.arange(holder_count, dtype=jnp.int32))[None, :]
    )
    rank_part = jnp.sum(holder_rank_rows * held_onehot.astype(jnp.float32)[:, :, None], axis=1)
    rank_feat = lax.psum(rank_part.astype(jnp.bfloat16), "mdl")
    broadcast_result = (
        all_onehot.astype(jnp.bfloat16)[:, :, None] * rank_feat[:, None, :]
    ).reshape(tok_count, adapter_number * rank_total_width)
    adapter_column_set = jnp.einsum(
        "iu,pdu->ipd", broadcast_result, adapter_up_maps, preferred_element_type=jnp.float32
    )
    positions = jnp.arange(tok_count, dtype=jnp.int32)
    lengths_row = request_token_lengths[0]
    starts = jnp.cumsum(lengths_row) - lengths_row
    member = (positions[:, None] >= starts[None, :]) & (
        positions[:, None] < (starts + lengths_row)[None, :]
    )
    member_int = member.astype(jnp.int32)
    request_of = jnp.sum(member_int * jnp.arange(req_per_dev, dtype=jnp.int32)[None, :], axis=1)
    relative = positions - jnp.sum(member_int * starts[None, :], axis=1)
    tenant_hot = (
        request_tenant_index[:, None]
        == jnp.arange(tenant_adapter_scale.shape[0], dtype=jnp.int32)[None, :]
    ).astype(jnp.float32)
    request_scale = jnp.sum(tenant_hot * tenant_adapter_scale[None, :], axis=1)
    per_token_scale = jnp.sum(member.astype(jnp.float32) * request_scale[None, :], axis=1)[:, None]
    query_rows = (projected_rows[0] + per_token_scale * adapter_column_set[:, 0]).astype(
        jnp.bfloat16
    )
    key_rows = projected_rows[1].astype(jnp.bfloat16)
    value_row_block = (projected_rows[2] + per_token_scale * adapter_column_set[:, 1]).astype(
        jnp.bfloat16
    )
    owner_column = last_page_holder[:, 0]
    owner_table = owner_column.reshape(req_devices, req_per_dev)
    slot_table = holder_page_slot.reshape(req_devices, req_per_dev)
    owned = (owner_table == req_index).astype(jnp.int32)
    owned_rank = jnp.cumsum(owned, axis=1) - 1
    picked = owned[:, None, :] * (
        owned_rank[:, None, :] == jnp.arange(cap_slots, dtype=jnp.int32)[None, :, None]
    ).astype(jnp.int32)
    send_slot = jnp.sum(picked * slot_table[:, None, :], axis=2)
    fill_table = page_filled_rows.reshape(req_devices, req_per_dev)
    send_fill = jnp.sum(picked * fill_table[:, None, :], axis=2)
    my_owner = lax.dynamic_slice_in_dim(owner_column, req_index * req_per_dev, req_per_dev, 0)
    order_ids = jnp.arange(req_per_dev, dtype=jnp.int32)
    earlier = (my_owner[:, None] == my_owner[None, :]) & (order_ids[:, None] > order_ids[None, :])
    flat_pick = my_owner * cap_slots + jnp.sum(earlier.astype(jnp.int32), axis=1)
    page_inner = prefix_cache_store.shape[1:3]
    page_rows = prefix_cache_store.shape[3]
    source_pages = cut_windows(
        prefix_cache_store,
        jnp.clip(send_slot.reshape(-1), 0, prefix_cache_store.shape[0] - 1),
        send_fill.reshape(-1),
    )
    source_pages = source_pages.reshape((req_devices, cap_slots, 2, WINDOW, head_column_set))
    arrived = lax.all_to_all(source_pages, "req", split_axis=0, concat_axis=0, tiled=True)
    prefix = jnp.take(
        arrived.reshape((req_devices * cap_slots, 2, WINDOW, head_column_set)),
        flat_pick,
        axis=0,
        mode="clip",
    )
    key_all = jnp.concatenate(
        [key_rows, prefix[:, 0].reshape(req_per_dev * WINDOW, head_column_set)], axis=0
    )
    value_all = jnp.concatenate(
        [value_row_block, prefix[:, 1].reshape(req_per_dev * WINDOW, head_column_set)], axis=0
    )
    distance = positions[:, None] - positions[None, :]
    local_ok = (request_of[:, None] == request_of[None, :]) & (distance >= 0) & (distance <= WINDOW)
    key_request = jnp.repeat(jnp.arange(req_per_dev, dtype=jnp.int32), WINDOW)
    key_offset = jnp.tile(jnp.arange(WINDOW, dtype=jnp.int32), req_per_dev)
    prefix_ok = (request_of[:, None] == key_request[None, :]) & (
        key_offset[None, :] >= relative[:, None]
    )
    allowed = jnp.concatenate([local_ok, prefix_ok], axis=1)
    query_heads = query_rows.reshape(tok_count, head_local, HEAD_SIZE)
    key_heads = key_all.reshape(-1, head_local, HEAD_SIZE)
    value_heads = value_all.reshape(-1, head_local, HEAD_SIZE)
    scores = jnp.einsum(
        "thd,shd->hts", query_heads, key_heads, preferred_element_type=jnp.float32
    ) * (1.0 / math.sqrt(HEAD_SIZE))
    masked = jnp.where(allowed[None], scores, -1e30)
    row_max = jnp.max(masked, axis=-1, keepdims=True)
    exp_scores = jnp.exp(masked - row_max)
    weights = (exp_scores / jnp.sum(exp_scores, axis=-1, keepdims=True)).astype(jnp.bfloat16)
    mixed = (
        jnp.einsum("hts,shd->thd", weights, value_heads, preferred_element_type=jnp.float32)
        .astype(jnp.bfloat16)
        .reshape(tok_count, head_column_set)
    )
    attn_part = (
        jnp.dot(mixed, head_output_weight, preferred_element_type=jnp.float32)
        .astype(jnp.bfloat16)
        .astype(jnp.float32)
    )
    gain_wide = feedforward_norm_gain.astype(jnp.float32)[None, :]
    attn_full = lax.psum(attn_part.astype(jnp.bfloat16), "mdl").astype(jnp.float32)
    resid_full = (stream.astype(jnp.float32) + attn_full).astype(jnp.bfloat16)
    resid_wide = resid_full.astype(jnp.float32)
    mean_sq = jnp.mean(resid_wide * resid_wide, axis=1, keepdims=True)
    normed = (resid_wide * lax.rsqrt(mean_sq + 1e-06) * gain_wide).astype(jnp.bfloat16)
    resid_mine = lax.dynamic_slice_in_dim(resid_full, mdl_index * row_share, row_share, 0)
    full_mlp = lax.all_gather(feedforward_weight[:2], "req", axis=1, tiled=True)
    down_rows = lax.all_gather(feedforward_weight[2].T, "req", axis=1, tiled=True)
    gate_part = jnp.dot(normed, full_mlp[0], preferred_element_type=jnp.float32)
    up_part = jnp.dot(normed, full_mlp[1], preferred_element_type=jnp.float32)
    hidden = (jax.nn.silu(gate_part) * up_part).astype(jnp.bfloat16)
    mlp_part = (
        jnp.dot(hidden, down_rows, preferred_element_type=jnp.float32)
        .astype(jnp.bfloat16)
        .astype(jnp.float32)
    )
    mlp_mine = lax.psum_scatter(
        mlp_part.astype(jnp.bfloat16), "mdl", scatter_dimension=0, tiled=True
    ).astype(jnp.float32)
    return (resid_mine.astype(jnp.float32) + mlp_mine).astype(jnp.bfloat16)


def solution(mesh):
    return jax.shard_map(
        per_device,
        mesh=mesh,
        in_specs=(
            P("req", None),
            P(None, "mdl", None),
            P("mdl", None),
            P("mdl", None, None),
            P(None, "mdl", None),
            P(),
            P(),
            P(None, "req", "mdl"),
            P("req", None, "mdl", None),
            P("req"),
            P("req", None),
            P("req"),
            P(),
            P(),
            P(),
        ),
        out_specs=P(("req", "mdl"), None),
        check_vma=False,
    )
```

```python
import math

import jax
import jax.numpy as jnp
from jax import lax
from jax.experimental import pallas as pl
from jax.experimental.pallas import tpu as pltpu
from jax.sharding import PartitionSpec as P

HEAD_SIZE = 112
WINDOW = 64


def window_kernel(slot_ref, fill_ref, store_ref, out_ref):
    count = out_ref.shape[0]
    page_rows = store_ref.shape[-1]
    row_ids = lax.broadcasted_iota(jnp.int32, (WINDOW, page_rows), 1)
    out_ids = lax.broadcasted_iota(jnp.int32, (WINDOW, page_rows), 0)

    def pick_rows(i, carry):
        pick = (row_ids == out_ids + (fill_ref[i] - WINDOW)).astype(store_ref.dtype)
        for part in range(store_ref.shape[1]):
            out_ref[i, part] = lax.dot_general(
                pick,
                store_ref[slot_ref[i], part],
                (((1,), (1,)), ((), ())),
                preferred_element_type=jnp.float32,
            ).astype(out_ref.dtype)
        return carry

    lax.fori_loop(0, count, pick_rows, 0, unroll=8)


def cut_windows(store, slots, fills):
    count = slots.shape[0]
    parts, width, page_rows = store.shape[1:]
    return pl.pallas_call(
        window_kernel,
        grid_spec=pltpu.PrefetchScalarGridSpec(
            num_scalar_prefetch=2,
            grid=(1,),
            in_specs=[pl.BlockSpec(memory_space=pltpu.VMEM)],
            out_specs=pl.BlockSpec(memory_space=pltpu.VMEM),
        ),
        out_shape=jax.ShapeDtypeStruct((count, parts, WINDOW, width), store.dtype),
    )(slots, fills, store)


def per_device(
    stream,
    attention_projection_weight,
    head_output_weight,
    adapter_down_maps,
    adapter_up_maps,
    tenant_adapter_scale,
    feedforward_norm_gain,
    feedforward_weight,
    prefix_cache_store,
    token_adapter_index,
    request_token_lengths,
    request_tenant_index,
    last_page_holder,
    holder_page_slot,
    page_filled_rows,
):
    tok_count, model_width = stream.shape
    head_column_set = attention_projection_weight.shape[1]
    head_local = head_column_set // HEAD_SIZE
    req_per_dev = request_token_lengths.shape[1]
    rank_total_width = adapter_down_maps.shape[2]
    adapter_number = adapter_up_maps.shape[2] // rank_total_width
    req_devices = lax.axis_size("req")
    req_index = lax.axis_index("req")
    mdl_index = lax.axis_index("mdl")
    row_share = tok_count // lax.axis_size("mdl")
    cap_slots = max(2, (req_per_dev + req_devices - 1) // req_devices + 1)
    projected_rows = jnp.einsum(
        "td,kcd->ktc", stream, attention_projection_weight, preferred_element_type=jnp.float32
    )
    all_onehot = (
        token_adapter_index[:, None] == jnp.arange(adapter_number, dtype=jnp.int32)[None, :]
    )
    holder_count = adapter_down_maps.shape[0]
    holder_rank_rows = jnp.einsum(
        "qf,kfn->qkn", stream, adapter_down_maps, preferred_element_type=jnp.float32
    )
    held_onehot = (
        token_adapter_index[:, None]
        == (mdl_index * holder_count + jnp.arange(holder_count, dtype=jnp.int32))[None, :]
    )
    rank_part = jnp.sum(holder_rank_rows * held_onehot.astype(jnp.float32)[:, :, None], axis=1)
    rank_feat = lax.psum(rank_part.astype(jnp.bfloat16), "mdl")
    broadcast_result = (
        all_onehot.astype(jnp.bfloat16)[:, :, None] * rank_feat[:, None, :]
    ).reshape(tok_count, adapter_number * rank_total_width)
    adapter_column_set = jnp.einsum(
        "iu,pdu->ipd", broadcast_result, adapter_up_maps, preferred_element_type=jnp.float32
    )
    positions = jnp.arange(tok_count, dtype=jnp.int32)
    lengths_row = request_token_lengths[0]
    starts = jnp.cumsum(lengths_row) - lengths_row
    member = (positions[:, None] >= starts[None, :]) & (
        positions[:, None] < (starts + lengths_row)[None, :]
    )
    member_int = member.astype(jnp.int32)
    request_of = jnp.sum(member_int * jnp.arange(req_per_dev, dtype=jnp.int32)[None, :], axis=1)
    relative = positions - jnp.sum(member_int * starts[None, :], axis=1)
    tenant_hot = (
        request_tenant_index[:, None]
        == jnp.arange(tenant_adapter_scale.shape[0], dtype=jnp.int32)[None, :]
    ).astype(jnp.float32)
    request_scale = jnp.sum(tenant_hot * tenant_adapter_scale[None, :], axis=1)
    per_token_scale = jnp.sum(member.astype(jnp.float32) * request_scale[None, :], axis=1)[:, None]
    query_rows = (projected_rows[0] + per_token_scale * adapter_column_set[:, 0]).astype(
        jnp.bfloat16
    )
    key_rows = projected_rows[1].astype(jnp.bfloat16)
    value_row_block = (projected_rows[2] + per_token_scale * adapter_column_set[:, 1]).astype(
        jnp.bfloat16
    )
    owner_column = last_page_holder[:, 0]
    owner_table = owner_column.reshape(req_devices, req_per_dev)
    slot_table = holder_page_slot.reshape(req_devices, req_per_dev)
    owned = (owner_table == req_index).astype(jnp.int32)
    owned_rank = jnp.cumsum(owned, axis=1) - 1
    picked = owned[:, None, :] * (
        owned_rank[:, None, :] == jnp.arange(cap_slots, dtype=jnp.int32)[None, :, None]
    ).astype(jnp.int32)
    send_slot = jnp.sum(picked * slot_table[:, None, :], axis=2)
    fill_table = page_filled_rows.reshape(req_devices, req_per_dev)
    send_fill = jnp.sum(picked * fill_table[:, None, :], axis=2)
    my_owner = lax.dynamic_slice_in_dim(owner_column, req_index * req_per_dev, req_per_dev, 0)
    order_ids = jnp.arange(req_per_dev, dtype=jnp.int32)
    earlier = (my_owner[:, None] == my_owner[None, :]) & (order_ids[:, None] > order_ids[None, :])
    flat_pick = my_owner * cap_slots + jnp.sum(earlier.astype(jnp.int32), axis=1)
    page_inner = prefix_cache_store.shape[1:3]
    page_rows = prefix_cache_store.shape[3]
    source_pages = cut_windows(
        prefix_cache_store,
        jnp.clip(send_slot.reshape(-1), 0, prefix_cache_store.shape[0] - 1),
        send_fill.reshape(-1),
    )
    source_pages = source_pages.reshape((req_devices, cap_slots, 2, WINDOW, head_column_set))
    arrived = lax.all_to_all(source_pages, "req", split_axis=0, concat_axis=0, tiled=True)
    prefix = jnp.take(
        arrived.reshape((req_devices * cap_slots, 2, WINDOW, head_column_set)),
        flat_pick,
        axis=0,
        mode="clip",
    )
    key_all = jnp.concatenate(
        [key_rows, prefix[:, 0].reshape(req_per_dev * WINDOW, head_column_set)], axis=0
    )
    value_all = jnp.concatenate(
        [value_row_block, prefix[:, 1].reshape(req_per_dev * WINDOW, head_column_set)], axis=0
    )
    distance = positions[:, None] - positions[None, :]
    local_ok = (request_of[:, None] == request_of[None, :]) & (distance >= 0) & (distance <= WINDOW)
    key_request = jnp.repeat(jnp.arange(req_per_dev, dtype=jnp.int32), WINDOW)
    key_offset = jnp.tile(jnp.arange(WINDOW, dtype=jnp.int32), req_per_dev)
    prefix_ok = (request_of[:, None] == key_request[None, :]) & (
        key_offset[None, :] >= relative[:, None]
    )
    allowed = jnp.concatenate([local_ok, prefix_ok], axis=1)
    query_heads = query_rows.reshape(tok_count, head_local, HEAD_SIZE)
    key_heads = key_all.reshape(-1, head_local, HEAD_SIZE)
    value_heads = value_all.reshape(-1, head_local, HEAD_SIZE)
    scores = jnp.einsum(
        "thd,shd->hts", query_heads, key_heads, preferred_element_type=jnp.float32
    ) * (1.0 / math.sqrt(HEAD_SIZE))
    masked = jnp.where(allowed[None], scores, -1e30)
    row_max = jnp.max(masked, axis=-1, keepdims=True)
    exp_scores = jnp.exp(masked - row_max)
    weights = (exp_scores / jnp.sum(exp_scores, axis=-1, keepdims=True)).astype(jnp.bfloat16)
    mixed = (
        jnp.einsum("hts,shd->thd", weights, value_heads, preferred_element_type=jnp.float32)
        .astype(jnp.bfloat16)
        .reshape(tok_count, head_column_set)
    )
    attn_part = (
        jnp.dot(mixed, head_output_weight, preferred_element_type=jnp.float32)
        .astype(jnp.bfloat16)
        .astype(jnp.float32)
    )
    gain_wide = feedforward_norm_gain.astype(jnp.float32)[None, :]
    attn_full = lax.psum(attn_part.astype(jnp.bfloat16), "mdl").astype(jnp.float32)
    resid_full = (stream.astype(jnp.float32) + attn_full).astype(jnp.bfloat16)
    resid_wide = resid_full.astype(jnp.float32)
    mean_sq = jnp.mean(resid_wide * resid_wide, axis=1, keepdims=True)
    normed = (resid_wide * lax.rsqrt(mean_sq + 1e-06) * gain_wide).astype(jnp.bfloat16)
    resid_mine = lax.dynamic_slice_in_dim(resid_full, mdl_index * row_share, row_share, 0)
    full_mlp = lax.all_gather(feedforward_weight, "req", axis=1, tiled=True)
    gate_part = jnp.dot(normed, full_mlp[0], preferred_element_type=jnp.float32)
    up_part = jnp.dot(normed, full_mlp[1], preferred_element_type=jnp.float32)
    hidden = (jax.nn.silu(gate_part) * up_part).astype(jnp.bfloat16)
    mlp_part = (
        jnp.einsum("tf,df->td", hidden, full_mlp[2], preferred_element_type=jnp.float32)
        .astype(jnp.bfloat16)
        .astype(jnp.float32)
    )
    mlp_mine = lax.psum_scatter(
        mlp_part.astype(jnp.bfloat16), "mdl", scatter_dimension=0, tiled=True
    ).astype(jnp.float32)
    return (resid_mine.astype(jnp.float32) + mlp_mine).astype(jnp.bfloat16)


def solution(mesh):
    return jax.shard_map(
        per_device,
        mesh=mesh,
        in_specs=(
            P("req", None),
            P(None, "mdl", None),
            P("mdl", None),
            P("mdl", None, None),
            P(None, "mdl", None),
            P(),
            P(),
            P(None, "req", "mdl"),
            P("req", None, "mdl", None),
            P("req"),
            P("req", None),
            P("req"),
            P(),
            P(),
            P(),
        ),
        out_specs=P(("req", "mdl"), None),
        check_vma=False,
    )
```

```python
import math

import jax
import jax.numpy as jnp
from jax import lax
from jax.experimental import pallas as pl
from jax.experimental.pallas import tpu as pltpu
from jax.sharding import PartitionSpec as P

HEAD_SIZE = 112
WINDOW = 64


def window_kernel(slot_ref, fill_ref, store_ref, out_ref):
    count = out_ref.shape[0]
    page_rows = store_ref.shape[-1]
    row_ids = lax.broadcasted_iota(jnp.int32, (WINDOW, page_rows), 1)
    out_ids = lax.broadcasted_iota(jnp.int32, (WINDOW, page_rows), 0)

    def pick_rows(i, carry):
        pick = (row_ids == out_ids + (fill_ref[i] - WINDOW)).astype(store_ref.dtype)
        page = store_ref[slot_ref[i]].reshape(-1, page_rows)
        out_ref[i] = lax.dot_general(
            pick, page, (((1,), (1,)), ((), ())), preferred_element_type=jnp.float32
        ).astype(out_ref.dtype)
        return carry

    lax.fori_loop(0, count, pick_rows, 0, unroll=8)


def cut_windows(store, slots, fills):
    count = slots.shape[0]
    parts, width, page_rows = store.shape[1:]
    return pl.pallas_call(
        window_kernel,
        grid_spec=pltpu.PrefetchScalarGridSpec(
            num_scalar_prefetch=2,
            grid=(1,),
            in_specs=[pl.BlockSpec(memory_space=pltpu.VMEM)],
            out_specs=pl.BlockSpec(memory_space=pltpu.VMEM),
        ),
        out_shape=jax.ShapeDtypeStruct((count, WINDOW, parts * width), store.dtype),
    )(slots, fills, store)


def per_device(
    stream,
    attention_projection_weight,
    head_output_weight,
    adapter_down_maps,
    adapter_up_maps,
    tenant_adapter_scale,
    feedforward_norm_gain,
    feedforward_weight,
    prefix_cache_store,
    token_adapter_index,
    request_token_lengths,
    request_tenant_index,
    last_page_holder,
    holder_page_slot,
    page_filled_rows,
):
    tok_count, model_width = stream.shape
    head_column_set = attention_projection_weight.shape[1]
    head_local = head_column_set // HEAD_SIZE
    req_per_dev = request_token_lengths.shape[1]
    rank_total_width = adapter_down_maps.shape[2]
    adapter_number = adapter_up_maps.shape[2] // rank_total_width
    req_devices = lax.axis_size("req")
    req_index = lax.axis_index("req")
    mdl_index = lax.axis_index("mdl")
    row_share = tok_count // lax.axis_size("mdl")
    cap_slots = max(2, (req_per_dev + req_devices - 1) // req_devices + 1)
    projected_rows = jnp.einsum(
        "td,kcd->ktc", stream, attention_projection_weight, preferred_element_type=jnp.float32
    )
    all_onehot = (
        token_adapter_index[:, None] == jnp.arange(adapter_number, dtype=jnp.int32)[None, :]
    )
    holder_count = adapter_down_maps.shape[0]
    holder_rank_rows = jnp.einsum(
        "qf,kfn->qkn", stream, adapter_down_maps, preferred_element_type=jnp.float32
    )
    held_onehot = (
        token_adapter_index[:, None]
        == (mdl_index * holder_count + jnp.arange(holder_count, dtype=jnp.int32))[None, :]
    )
    rank_part = jnp.sum(holder_rank_rows * held_onehot.astype(jnp.float32)[:, :, None], axis=1)
    rank_feat = lax.psum(rank_part.astype(jnp.bfloat16), "mdl")
    broadcast_result = (
        all_onehot.astype(jnp.bfloat16)[:, :, None] * rank_feat[:, None, :]
    ).reshape(tok_count, adapter_number * rank_total_width)
    adapter_column_set = jnp.einsum(
        "iu,pdu->ipd", broadcast_result, adapter_up_maps, preferred_element_type=jnp.float32
    )
    positions = jnp.arange(tok_count, dtype=jnp.int32)
    lengths_row = request_token_lengths[0]
    starts = jnp.cumsum(lengths_row) - lengths_row
    member = (positions[:, None] >= starts[None, :]) & (
        positions[:, None] < (starts + lengths_row)[None, :]
    )
    member_int = member.astype(jnp.int32)
    request_of = jnp.sum(member_int * jnp.arange(req_per_dev, dtype=jnp.int32)[None, :], axis=1)
    relative = positions - jnp.sum(member_int * starts[None, :], axis=1)
    tenant_hot = (
        request_tenant_index[:, None]
        == jnp.arange(tenant_adapter_scale.shape[0], dtype=jnp.int32)[None, :]
    ).astype(jnp.float32)
    request_scale = jnp.sum(tenant_hot * tenant_adapter_scale[None, :], axis=1)
    per_token_scale = jnp.sum(member.astype(jnp.float32) * request_scale[None, :], axis=1)[:, None]
    query_rows = (projected_rows[0] + per_token_scale * adapter_column_set[:, 0]).astype(
        jnp.bfloat16
    )
    key_rows = projected_rows[1].astype(jnp.bfloat16)
    value_row_block = (projected_rows[2] + per_token_scale * adapter_column_set[:, 1]).astype(
        jnp.bfloat16
    )
    owner_column = last_page_holder[:, 0]
    owner_table = owner_column.reshape(req_devices, req_per_dev)
    slot_table = holder_page_slot.reshape(req_devices, req_per_dev)
    owned = (owner_table == req_index).astype(jnp.int32)
    owned_rank = jnp.cumsum(owned, axis=1) - 1
    picked = owned[:, None, :] * (
        owned_rank[:, None, :] == jnp.arange(cap_slots, dtype=jnp.int32)[None, :, None]
    ).astype(jnp.int32)
    send_slot = jnp.sum(picked * slot_table[:, None, :], axis=2)
    fill_table = page_filled_rows.reshape(req_devices, req_per_dev)
    send_fill = jnp.sum(picked * fill_table[:, None, :], axis=2)
    my_owner = lax.dynamic_slice_in_dim(owner_column, req_index * req_per_dev, req_per_dev, 0)
    order_ids = jnp.arange(req_per_dev, dtype=jnp.int32)
    earlier = (my_owner[:, None] == my_owner[None, :]) & (order_ids[:, None] > order_ids[None, :])
    flat_pick = my_owner * cap_slots + jnp.sum(earlier.astype(jnp.int32), axis=1)
    page_inner = prefix_cache_store.shape[1:3]
    page_rows = prefix_cache_store.shape[3]
    source_pages = cut_windows(
        prefix_cache_store,
        jnp.clip(send_slot.reshape(-1), 0, prefix_cache_store.shape[0] - 1),
        send_fill.reshape(-1),
    )
    source_pages = source_pages.reshape((req_devices, cap_slots, WINDOW, 2 * head_column_set))
    arrived = lax.all_to_all(source_pages, "req", split_axis=0, concat_axis=0, tiled=True)
    prefix = jnp.take(
        arrived.reshape((req_devices * cap_slots, WINDOW, 2 * head_column_set)),
        flat_pick,
        axis=0,
        mode="clip",
    )
    key_all = jnp.concatenate(
        [key_rows, prefix[:, :, :head_column_set].reshape(req_per_dev * WINDOW, head_column_set)], axis=0
    )
    value_all = jnp.concatenate(
        [value_row_block, prefix[:, :, head_column_set:].reshape(req_per_dev * WINDOW, head_column_set)], axis=0
    )
    distance = positions[:, None] - positions[None, :]
    local_ok = (request_of[:, None] == request_of[None, :]) & (distance >= 0) & (distance <= WINDOW)
    key_request = jnp.repeat(jnp.arange(req_per_dev, dtype=jnp.int32), WINDOW)
    key_offset = jnp.tile(jnp.arange(WINDOW, dtype=jnp.int32), req_per_dev)
    prefix_ok = (request_of[:, None] == key_request[None, :]) & (
        key_offset[None, :] >= relative[:, None]
    )
    allowed = jnp.concatenate([local_ok, prefix_ok], axis=1)
    query_heads = query_rows.reshape(tok_count, head_local, HEAD_SIZE)
    key_heads = key_all.reshape(-1, head_local, HEAD_SIZE)
    value_heads = value_all.reshape(-1, head_local, HEAD_SIZE)
    scores = jnp.einsum(
        "thd,shd->hts", query_heads, key_heads, preferred_element_type=jnp.float32
    ) * (1.0 / math.sqrt(HEAD_SIZE))
    masked = jnp.where(allowed[None], scores, -1e30)
    row_max = jnp.max(masked, axis=-1, keepdims=True)
    exp_scores = jnp.exp(masked - row_max)
    weights = (exp_scores / jnp.sum(exp_scores, axis=-1, keepdims=True)).astype(jnp.bfloat16)
    mixed = (
        jnp.einsum("hts,shd->thd", weights, value_heads, preferred_element_type=jnp.float32)
        .astype(jnp.bfloat16)
        .reshape(tok_count, head_column_set)
    )
    attn_part = (
        jnp.dot(mixed, head_output_weight, preferred_element_type=jnp.float32)
        .astype(jnp.bfloat16)
        .astype(jnp.float32)
    )
    gain_wide = feedforward_norm_gain.astype(jnp.float32)[None, :]
    attn_full = lax.psum(attn_part.astype(jnp.bfloat16), "mdl").astype(jnp.float32)
    resid_full = (stream.astype(jnp.float32) + attn_full).astype(jnp.bfloat16)
    resid_wide = resid_full.astype(jnp.float32)
    mean_sq = jnp.mean(resid_wide * resid_wide, axis=1, keepdims=True)
    normed = (resid_wide * lax.rsqrt(mean_sq + 1e-06) * gain_wide).astype(jnp.bfloat16)
    resid_mine = lax.dynamic_slice_in_dim(resid_full, mdl_index * row_share, row_share, 0)
    full_mlp = lax.all_gather(feedforward_weight, "req", axis=1, tiled=True)
    gate_part = jnp.dot(normed, full_mlp[0], preferred_element_type=jnp.float32)
    up_part = jnp.dot(normed, full_mlp[1], preferred_element_type=jnp.float32)
    hidden = (jax.nn.silu(gate_part) * up_part).astype(jnp.bfloat16)
    mlp_part = (
        jnp.einsum("tf,df->td", hidden, full_mlp[2], preferred_element_type=jnp.float32)
        .astype(jnp.bfloat16)
        .astype(jnp.float32)
    )
    mlp_mine = lax.psum_scatter(
        mlp_part.astype(jnp.bfloat16), "mdl", scatter_dimension=0, tiled=True
    ).astype(jnp.float32)
    return (resid_mine.astype(jnp.float32) + mlp_mine).astype(jnp.bfloat16)


def solution(mesh):
    return jax.shard_map(
        per_device,
        mesh=mesh,
        in_specs=(
            P("req", None),
            P(None, "mdl", None),
            P("mdl", None),
            P("mdl", None, None),
            P(None, "mdl", None),
            P(),
            P(),
            P(None, "req", "mdl"),
            P("req", None, "mdl", None),
            P("req"),
            P("req", None),
            P("req"),
            P(),
            P(),
            P(),
        ),
        out_specs=P(("req", "mdl"), None),
        check_vma=False,
    )
```

```python
import math

import jax
import jax.numpy as jnp
from jax import lax
from jax.experimental import pallas as pl
from jax.experimental.pallas import tpu as pltpu
from jax.sharding import PartitionSpec as P

HEAD_SIZE = 112
WINDOW = 64


def window_kernel(slot_ref, fill_ref, store_ref, out_ref):
    count = out_ref.shape[0]
    page_rows = store_ref.shape[-1]
    row_ids = lax.broadcasted_iota(jnp.int32, (WINDOW, page_rows), 1)
    out_ids = lax.broadcasted_iota(jnp.int32, (WINDOW, page_rows), 0)

    def pick_rows(i, carry):
        pick = (row_ids == out_ids + (fill_ref[i] - WINDOW)).astype(store_ref.dtype)
        page = store_ref[slot_ref[i]].reshape(-1, page_rows)
        out_ref[i] = lax.dot_general(
            pick, page, (((1,), (1,)), ((), ())), preferred_element_type=jnp.float32
        ).astype(out_ref.dtype)
        return carry

    lax.fori_loop(0, count, pick_rows, 0, unroll=8)


def cut_windows(store, slots, fills):
    count = slots.shape[0]
    parts, width, page_rows = store.shape[1:]
    return pl.pallas_call(
        window_kernel,
        grid_spec=pltpu.PrefetchScalarGridSpec(
            num_scalar_prefetch=2,
            grid=(1,),
            in_specs=[pl.BlockSpec(memory_space=pltpu.VMEM)],
            out_specs=pl.BlockSpec(memory_space=pltpu.VMEM),
        ),
        out_shape=jax.ShapeDtypeStruct((count, WINDOW, parts * width), store.dtype),
    )(slots, fills, store)


def per_device(
    stream,
    attention_projection_weight,
    head_output_weight,
    adapter_down_maps,
    adapter_up_maps,
    tenant_adapter_scale,
    feedforward_norm_gain,
    feedforward_weight,
    prefix_cache_store,
    token_adapter_index,
    request_token_lengths,
    request_tenant_index,
    last_page_holder,
    holder_page_slot,
    page_filled_rows,
):
    tok_count, model_width = stream.shape
    head_column_set = attention_projection_weight.shape[1]
    head_local = head_column_set // HEAD_SIZE
    req_per_dev = request_token_lengths.shape[1]
    rank_total_width = adapter_down_maps.shape[2]
    adapter_number = adapter_up_maps.shape[2] // rank_total_width
    req_devices = lax.axis_size("req")
    req_index = lax.axis_index("req")
    mdl_index = lax.axis_index("mdl")
    row_share = tok_count // lax.axis_size("mdl")
    cap_slots = max(2, (req_per_dev + req_devices - 1) // req_devices + 1)
    projected_rows = jnp.einsum(
        "td,kcd->ktc", stream, attention_projection_weight, preferred_element_type=jnp.float32
    )
    all_onehot = (
        token_adapter_index[:, None] == jnp.arange(adapter_number, dtype=jnp.int32)[None, :]
    )
    holder_count = adapter_down_maps.shape[0]
    holder_rank_rows = jnp.einsum(
        "qf,kfn->qkn", stream, adapter_down_maps, preferred_element_type=jnp.float32
    )
    held_onehot = (
        token_adapter_index[:, None]
        == (mdl_index * holder_count + jnp.arange(holder_count, dtype=jnp.int32))[None, :]
    )
    rank_part = jnp.sum(holder_rank_rows * held_onehot.astype(jnp.float32)[:, :, None], axis=1)
    rank_feat = lax.psum(rank_part.astype(jnp.bfloat16), "mdl")
    broadcast_result = (
        all_onehot.astype(jnp.bfloat16)[:, :, None] * rank_feat[:, None, :]
    ).reshape(tok_count, adapter_number * rank_total_width)
    adapter_column_set = jnp.einsum(
        "iu,pdu->ipd", broadcast_result, adapter_up_maps, preferred_element_type=jnp.float32
    )
    positions = jnp.arange(tok_count, dtype=jnp.int32)
    lengths_row = request_token_lengths[0]
    starts = jnp.cumsum(lengths_row) - lengths_row
    member = (positions[:, None] >= starts[None, :]) & (
        positions[:, None] < (starts + lengths_row)[None, :]
    )
    member_int = member.astype(jnp.int32)
    request_of = jnp.sum(member_int * jnp.arange(req_per_dev, dtype=jnp.int32)[None, :], axis=1)
    relative = positions - jnp.sum(member_int * starts[None, :], axis=1)
    tenant_hot = (
        request_tenant_index[:, None]
        == jnp.arange(tenant_adapter_scale.shape[0], dtype=jnp.int32)[None, :]
    ).astype(jnp.float32)
    request_scale = jnp.sum(tenant_hot * tenant_adapter_scale[None, :], axis=1)
    per_token_scale = jnp.sum(member.astype(jnp.float32) * request_scale[None, :], axis=1)[:, None]
    query_rows = (projected_rows[0] + per_token_scale * adapter_column_set[:, 0]).astype(
        jnp.bfloat16
    )
    key_rows = projected_rows[1].astype(jnp.bfloat16)
    value_row_block = (projected_rows[2] + per_token_scale * adapter_column_set[:, 1]).astype(
        jnp.bfloat16
    )
    owner_column = last_page_holder[:, 0]
    owner_table = owner_column.reshape(req_devices, req_per_dev)
    slot_table = holder_page_slot.reshape(req_devices, req_per_dev)
    owned = (owner_table == req_index).astype(jnp.int32)
    owned_rank = jnp.cumsum(owned, axis=1) - 1
    picked = owned[:, None, :] * (
        owned_rank[:, None, :] == jnp.arange(cap_slots, dtype=jnp.int32)[None, :, None]
    ).astype(jnp.int32)
    fill_table = page_filled_rows.reshape(req_devices, req_per_dev)
    send_both = jnp.sum(
        picked[None] * jnp.stack([slot_table, fill_table])[:, :, None, :], axis=3
    ).reshape(2, -1)
    my_owner = lax.dynamic_slice_in_dim(owner_column, req_index * req_per_dev, req_per_dev, 0)
    order_ids = jnp.arange(req_per_dev, dtype=jnp.int32)
    earlier = (my_owner[:, None] == my_owner[None, :]) & (order_ids[:, None] > order_ids[None, :])
    flat_pick = my_owner * cap_slots + jnp.sum(earlier.astype(jnp.int32), axis=1)
    page_inner = prefix_cache_store.shape[1:3]
    page_rows = prefix_cache_store.shape[3]
    source_pages = cut_windows(
        prefix_cache_store,
        send_both[0],
        send_both[1],
    )
    source_pages = source_pages.reshape((req_devices, cap_slots, WINDOW, 2 * head_column_set))
    arrived = lax.all_to_all(source_pages, "req", split_axis=0, concat_axis=0, tiled=True)
    prefix = jnp.take(
        arrived.reshape((req_devices * cap_slots, WINDOW, 2 * head_column_set)),
        flat_pick,
        axis=0,
        mode="clip",
    )
    key_all = jnp.concatenate(
        [key_rows, prefix[:, :, :head_column_set].reshape(req_per_dev * WINDOW, head_column_set)], axis=0
    )
    value_all = jnp.concatenate(
        [value_row_block, prefix[:, :, head_column_set:].reshape(req_per_dev * WINDOW, head_column_set)], axis=0
    )
    distance = positions[:, None] - positions[None, :]
    local_ok = (request_of[:, None] == request_of[None, :]) & (distance >= 0) & (distance <= WINDOW)
    key_request = jnp.repeat(jnp.arange(req_per_dev, dtype=jnp.int32), WINDOW)
    key_offset = jnp.tile(jnp.arange(WINDOW, dtype=jnp.int32), req_per_dev)
    prefix_ok = (request_of[:, None] == key_request[None, :]) & (
        key_offset[None, :] >= relative[:, None]
    )
    allowed = jnp.concatenate([local_ok, prefix_ok], axis=1)
    query_heads = query_rows.reshape(tok_count, head_local, HEAD_SIZE)
    key_heads = key_all.reshape(-1, head_local, HEAD_SIZE)
    value_heads = value_all.reshape(-1, head_local, HEAD_SIZE)
    scores = jnp.einsum(
        "thd,shd->hts", query_heads, key_heads, preferred_element_type=jnp.float32
    ) * (1.0 / math.sqrt(HEAD_SIZE))
    masked = jnp.where(allowed[None], scores, -1e30)
    row_max = jnp.max(masked, axis=-1, keepdims=True)
    exp_scores = jnp.exp(masked - row_max)
    weights = (exp_scores / jnp.sum(exp_scores, axis=-1, keepdims=True)).astype(jnp.bfloat16)
    mixed = (
        jnp.einsum("hts,shd->thd", weights, value_heads, preferred_element_type=jnp.float32)
        .astype(jnp.bfloat16)
        .reshape(tok_count, head_column_set)
    )
    attn_part = (
        jnp.dot(mixed, head_output_weight, preferred_element_type=jnp.float32)
        .astype(jnp.bfloat16)
        .astype(jnp.float32)
    )
    gain_wide = feedforward_norm_gain.astype(jnp.float32)[None, :]
    attn_full = lax.psum(attn_part.astype(jnp.bfloat16), "mdl").astype(jnp.float32)
    resid_full = (stream.astype(jnp.float32) + attn_full).astype(jnp.bfloat16)
    resid_wide = resid_full.astype(jnp.float32)
    mean_sq = jnp.mean(resid_wide * resid_wide, axis=1, keepdims=True)
    normed = (resid_wide * lax.rsqrt(mean_sq + 1e-06) * gain_wide).astype(jnp.bfloat16)
    resid_mine = lax.dynamic_slice_in_dim(resid_full, mdl_index * row_share, row_share, 0)
    full_mlp = lax.all_gather(feedforward_weight, "req", axis=1, tiled=True)
    gate_part = jnp.dot(normed, full_mlp[0], preferred_element_type=jnp.float32)
    up_part = jnp.dot(normed, full_mlp[1], preferred_element_type=jnp.float32)
    hidden = (jax.nn.silu(gate_part) * up_part).astype(jnp.bfloat16)
    mlp_part = (
        jnp.einsum("tf,df->td", hidden, full_mlp[2], preferred_element_type=jnp.float32)
        .astype(jnp.bfloat16)
        .astype(jnp.float32)
    )
    mlp_mine = lax.psum_scatter(
        mlp_part.astype(jnp.bfloat16), "mdl", scatter_dimension=0, tiled=True
    ).astype(jnp.float32)
    return (resid_mine.astype(jnp.float32) + mlp_mine).astype(jnp.bfloat16)


def solution(mesh):
    return jax.shard_map(
        per_device,
        mesh=mesh,
        in_specs=(
            P("req", None),
            P(None, "mdl", None),
            P("mdl", None),
            P("mdl", None, None),
            P(None, "mdl", None),
            P(),
            P(),
            P(None, "req", "mdl"),
            P("req", None, "mdl", None),
            P("req"),
            P("req", None),
            P("req"),
            P(),
            P(),
            P(),
        ),
        out_specs=P(("req", "mdl"), None),
        check_vma=False,
    )
```

```python
import math

import jax
import jax.numpy as jnp
from jax import lax
from jax.experimental import pallas as pl
from jax.experimental.pallas import tpu as pltpu
from jax.sharding import PartitionSpec as P

HEAD_SIZE = 112
WINDOW = 64


def window_kernel(slot_ref, fill_ref, store_ref, out_ref):
    count = out_ref.shape[0]
    page_rows = store_ref.shape[-1]
    row_ids = lax.broadcasted_iota(jnp.int32, (WINDOW, page_rows), 1)
    out_ids = lax.broadcasted_iota(jnp.int32, (WINDOW, page_rows), 0)

    def pick_rows(i, carry):
        pick = (row_ids == out_ids + (fill_ref[i] - WINDOW)).astype(store_ref.dtype)
        page = store_ref[slot_ref[i]].reshape(-1, page_rows)
        out_ref[i] = lax.dot_general(
            pick, page, (((1,), (1,)), ((), ())), preferred_element_type=jnp.float32
        ).astype(out_ref.dtype)
        return carry

    lax.fori_loop(0, count, pick_rows, 0, unroll=8)


def cut_windows(store, slots, fills):
    count = slots.shape[0]
    parts, width, page_rows = store.shape[1:]
    return pl.pallas_call(
        window_kernel,
        grid_spec=pltpu.PrefetchScalarGridSpec(
            num_scalar_prefetch=2,
            grid=(1,),
            in_specs=[pl.BlockSpec(memory_space=pltpu.VMEM)],
            out_specs=pl.BlockSpec(memory_space=pltpu.VMEM),
        ),
        out_shape=jax.ShapeDtypeStruct((count, WINDOW, parts * width), store.dtype),
    )(slots, fills, store)


def per_device(
    stream,
    attention_projection_weight,
    head_output_weight,
    adapter_down_maps,
    adapter_up_maps,
    tenant_adapter_scale,
    feedforward_norm_gain,
    feedforward_weight,
    prefix_cache_store,
    token_adapter_index,
    request_token_lengths,
    request_tenant_index,
    last_page_holder,
    holder_page_slot,
    page_filled_rows,
):
    tok_count, model_width = stream.shape
    head_column_set = attention_projection_weight.shape[1]
    head_local = head_column_set // HEAD_SIZE
    req_per_dev = request_token_lengths.shape[1]
    rank_total_width = adapter_down_maps.shape[2]
    adapter_number = adapter_up_maps.shape[2] // rank_total_width
    req_devices = lax.axis_size("req")
    req_index = lax.axis_index("req")
    mdl_index = lax.axis_index("mdl")
    row_share = tok_count // lax.axis_size("mdl")
    cap_slots = max(2, (req_per_dev + req_devices - 1) // req_devices + 1)
    projected_rows = jnp.einsum(
        "td,kcd->ktc", stream, attention_projection_weight, preferred_element_type=jnp.float32
    )
    all_onehot = (
        token_adapter_index[:, None] == jnp.arange(adapter_number, dtype=jnp.int32)[None, :]
    )
    holder_count = adapter_down_maps.shape[0]
    holder_rank_rows = jnp.einsum(
        "qf,kfn->qkn", stream, adapter_down_maps, preferred_element_type=jnp.float32
    )
    held_onehot = (
        token_adapter_index[:, None]
        == (mdl_index * holder_count + jnp.arange(holder_count, dtype=jnp.int32))[None, :]
    )
    rank_part = jnp.sum(holder_rank_rows * held_onehot.astype(jnp.float32)[:, :, None], axis=1)
    rank_feat = lax.psum(rank_part.astype(jnp.bfloat16), "mdl")
    broadcast_result = (
        all_onehot.astype(jnp.bfloat16)[:, :, None] * rank_feat[:, None, :]
    ).reshape(tok_count, adapter_number * rank_total_width)
    adapter_column_set = jnp.einsum(
        "iu,pdu->ipd", broadcast_result, adapter_up_maps, preferred_element_type=jnp.float32
    )
    positions = jnp.arange(tok_count, dtype=jnp.int32)
    lengths_row = request_token_lengths[0]
    starts = jnp.cumsum(lengths_row) - lengths_row
    member = (positions[:, None] >= starts[None, :]) & (
        positions[:, None] < (starts + lengths_row)[None, :]
    )
    member_int = member.astype(jnp.int32)
    request_of = jnp.sum(member_int * jnp.arange(req_per_dev, dtype=jnp.int32)[None, :], axis=1)
    relative = positions - jnp.sum(member_int * starts[None, :], axis=1)
    tenant_hot = (
        request_tenant_index[:, None]
        == jnp.arange(tenant_adapter_scale.shape[0], dtype=jnp.int32)[None, :]
    ).astype(jnp.float32)
    request_scale = jnp.sum(tenant_hot * tenant_adapter_scale[None, :], axis=1)
    per_token_scale = jnp.sum(member.astype(jnp.float32) * request_scale[None, :], axis=1)[:, None]
    query_rows = (projected_rows[0] + per_token_scale * adapter_column_set[:, 0]).astype(
        jnp.bfloat16
    )
    key_rows = projected_rows[1].astype(jnp.bfloat16)
    value_row_block = (projected_rows[2] + per_token_scale * adapter_column_set[:, 1]).astype(
        jnp.bfloat16
    )
    owner_column = last_page_holder[:, 0]
    owner_table = owner_column.reshape(req_devices, req_per_dev)
    slot_table = holder_page_slot.reshape(req_devices, req_per_dev)
    owned = (owner_table == req_index).astype(jnp.int32)
    owned_rank = jnp.cumsum(owned, axis=1) - 1
    picked = owned[:, None, :] * (
        owned_rank[:, None, :] == jnp.arange(cap_slots, dtype=jnp.int32)[None, :, None]
    ).astype(jnp.int32)
    send_slot = jnp.sum(picked * slot_table[:, None, :], axis=2)
    fill_table = page_filled_rows.reshape(req_devices, req_per_dev)
    send_fill = jnp.sum(picked * fill_table[:, None, :], axis=2)
    my_owner = lax.dynamic_slice_in_dim(owner_column, req_index * req_per_dev, req_per_dev, 0)
    order_ids = jnp.arange(req_per_dev, dtype=jnp.int32)
    earlier = (my_owner[:, None] == my_owner[None, :]) & (order_ids[:, None] > order_ids[None, :])
    flat_pick = my_owner * cap_slots + jnp.sum(earlier.astype(jnp.int32), axis=1)
    page_inner = prefix_cache_store.shape[1:3]
    page_rows = prefix_cache_store.shape[3]
    source_pages = cut_windows(
        prefix_cache_store,
        jnp.clip(send_slot.reshape(-1), 0, prefix_cache_store.shape[0] - 1),
        send_fill.reshape(-1),
    )
    source_pages = source_pages.reshape((req_devices, cap_slots, WINDOW, 2 * head_column_set))
    arrived = lax.all_to_all(source_pages, "req", split_axis=0, concat_axis=0, tiled=True)
    prefix = jnp.take(
        arrived.reshape((req_devices * cap_slots, WINDOW, 2 * head_column_set)),
        flat_pick,
        axis=0,
        mode="clip",
    )
    prefix_keys = prefix[:, :, :head_column_set].reshape(req_per_dev * WINDOW, head_local, HEAD_SIZE)
    prefix_values = prefix[:, :, head_column_set:].reshape(req_per_dev * WINDOW, head_local, HEAD_SIZE)
    distance = positions[:, None] - positions[None, :]
    local_ok = (request_of[:, None] == request_of[None, :]) & (distance >= 0) & (distance <= WINDOW)
    key_request = jnp.repeat(jnp.arange(req_per_dev, dtype=jnp.int32), WINDOW)
    key_offset = jnp.tile(jnp.arange(WINDOW, dtype=jnp.int32), req_per_dev)
    prefix_ok = (request_of[:, None] == key_request[None, :]) & (
        key_offset[None, :] >= relative[:, None]
    )
    query_heads = query_rows.reshape(tok_count, head_local, HEAD_SIZE)
    key_heads = key_rows.reshape(tok_count, head_local, HEAD_SIZE)
    value_heads = value_row_block.reshape(tok_count, head_local, HEAD_SIZE)
    scale = 1.0 / math.sqrt(HEAD_SIZE)
    local_scores = jnp.where(
        local_ok[None],
        jnp.einsum("thd,shd->hts", query_heads, key_heads, preferred_element_type=jnp.float32) * scale,
        -1e30,
    )
    prefix_scores = jnp.where(
        prefix_ok[None],
        jnp.einsum("thd,shd->hts", query_heads, prefix_keys, preferred_element_type=jnp.float32) * scale,
        -1e30,
    )
    row_max = jnp.maximum(
        jnp.max(local_scores, axis=-1, keepdims=True), jnp.max(prefix_scores, axis=-1, keepdims=True)
    )
    local_exp = jnp.exp(local_scores - row_max)
    prefix_exp = jnp.exp(prefix_scores - row_max)
    denom = jnp.sum(local_exp, axis=-1, keepdims=True) + jnp.sum(prefix_exp, axis=-1, keepdims=True)
    local_weights = (local_exp / denom).astype(jnp.bfloat16)
    prefix_weights = (prefix_exp / denom).astype(jnp.bfloat16)
    mixed = (
        (
            jnp.einsum("hts,shd->thd", local_weights, value_heads, preferred_element_type=jnp.float32)
            + jnp.einsum(
                "hts,shd->thd", prefix_weights, prefix_values, preferred_element_type=jnp.float32
            )
        )
        .astype(jnp.bfloat16)
        .reshape(tok_count, head_column_set)
    )
    attn_part = (
        jnp.dot(mixed, head_output_weight, preferred_element_type=jnp.float32)
        .astype(jnp.bfloat16)
        .astype(jnp.float32)
    )
    gain_wide = feedforward_norm_gain.astype(jnp.float32)[None, :]
    attn_full = lax.psum(attn_part.astype(jnp.bfloat16), "mdl").astype(jnp.float32)
    resid_full = (stream.astype(jnp.float32) + attn_full).astype(jnp.bfloat16)
    resid_wide = resid_full.astype(jnp.float32)
    mean_sq = jnp.mean(resid_wide * resid_wide, axis=1, keepdims=True)
    normed = (resid_wide * lax.rsqrt(mean_sq + 1e-06) * gain_wide).astype(jnp.bfloat16)
    resid_mine = lax.dynamic_slice_in_dim(resid_full, mdl_index * row_share, row_share, 0)
    full_mlp = lax.all_gather(feedforward_weight, "req", axis=1, tiled=True)
    gate_part = jnp.dot(normed, full_mlp[0], preferred_element_type=jnp.float32)
    up_part = jnp.dot(normed, full_mlp[1], preferred_element_type=jnp.float32)
    hidden = (jax.nn.silu(gate_part) * up_part).astype(jnp.bfloat16)
    mlp_part = (
        jnp.einsum("tf,df->td", hidden, full_mlp[2], preferred_element_type=jnp.float32)
        .astype(jnp.bfloat16)
        .astype(jnp.float32)
    )
    mlp_mine = lax.psum_scatter(
        mlp_part.astype(jnp.bfloat16), "mdl", scatter_dimension=0, tiled=True
    ).astype(jnp.float32)
    return (resid_mine.astype(jnp.float32) + mlp_mine).astype(jnp.bfloat16)


def solution(mesh):
    return jax.shard_map(
        per_device,
        mesh=mesh,
        in_specs=(
            P("req", None),
            P(None, "mdl", None),
            P("mdl", None),
            P("mdl", None, None),
            P(None, "mdl", None),
            P(),
            P(),
            P(None, "req", "mdl"),
            P("req", None, "mdl", None),
            P("req"),
            P("req", None),
            P("req"),
            P(),
            P(),
            P(),
        ),
        out_specs=P(("req", "mdl"), None),
        check_vma=False,
    )
```

```python
import math

import jax
import jax.numpy as jnp
from jax import lax
from jax.experimental import pallas as pl
from jax.experimental.pallas import tpu as pltpu
from jax.sharding import PartitionSpec as P

HEAD_SIZE = 112
WINDOW = 64


def window_kernel(slot_ref, fill_ref, store_ref, out_ref):
    count = out_ref.shape[0]
    page_rows = store_ref.shape[-1]
    row_ids = lax.broadcasted_iota(jnp.int32, (WINDOW, page_rows), 1)
    out_ids = lax.broadcasted_iota(jnp.int32, (WINDOW, page_rows), 0)

    def pick_rows(i, carry):
        pick = (row_ids == out_ids + (fill_ref[i] - WINDOW)).astype(store_ref.dtype)
        page = store_ref[slot_ref[i]].reshape(-1, page_rows)
        out_ref[i] = lax.dot_general(
            pick, page, (((1,), (1,)), ((), ())), preferred_element_type=jnp.float32
        ).astype(out_ref.dtype)
        return carry

    lax.fori_loop(0, count, pick_rows, 0, unroll=16)


def cut_windows(store, slots, fills):
    count = slots.shape[0]
    parts, width, page_rows = store.shape[1:]
    return pl.pallas_call(
        window_kernel,
        grid_spec=pltpu.PrefetchScalarGridSpec(
            num_scalar_prefetch=2,
            grid=(1,),
            in_specs=[pl.BlockSpec(memory_space=pltpu.VMEM)],
            out_specs=pl.BlockSpec(memory_space=pltpu.VMEM),
        ),
        out_shape=jax.ShapeDtypeStruct((count, WINDOW, parts * width), store.dtype),
    )(slots, fills, store)


def per_device(
    stream,
    attention_projection_weight,
    head_output_weight,
    adapter_down_maps,
    adapter_up_maps,
    tenant_adapter_scale,
    feedforward_norm_gain,
    feedforward_weight,
    prefix_cache_store,
    token_adapter_index,
    request_token_lengths,
    request_tenant_index,
    last_page_holder,
    holder_page_slot,
    page_filled_rows,
):
    tok_count, model_width = stream.shape
    head_column_set = attention_projection_weight.shape[1]
    head_local = head_column_set // HEAD_SIZE
    req_per_dev = request_token_lengths.shape[1]
    rank_total_width = adapter_down_maps.shape[2]
    adapter_number = adapter_up_maps.shape[2] // rank_total_width
    req_devices = lax.axis_size("req")
    req_index = lax.axis_index("req")
    mdl_index = lax.axis_index("mdl")
    row_share = tok_count // lax.axis_size("mdl")
    cap_slots = max(2, (req_per_dev + req_devices - 1) // req_devices + 1)
    projected_rows = jnp.einsum(
        "td,kcd->ktc", stream, attention_projection_weight, preferred_element_type=jnp.float32
    )
    all_onehot = (
        token_adapter_index[:, None] == jnp.arange(adapter_number, dtype=jnp.int32)[None, :]
    )
    holder_count = adapter_down_maps.shape[0]
    holder_rank_rows = jnp.einsum(
        "qf,kfn->qkn", stream, adapter_down_maps, preferred_element_type=jnp.float32
    )
    held_onehot = (
        token_adapter_index[:, None]
        == (mdl_index * holder_count + jnp.arange(holder_count, dtype=jnp.int32))[None, :]
    )
    rank_part = jnp.sum(holder_rank_rows * held_onehot.astype(jnp.float32)[:, :, None], axis=1)
    rank_feat = lax.psum(rank_part.astype(jnp.bfloat16), "mdl")
    broadcast_result = (
        all_onehot.astype(jnp.bfloat16)[:, :, None] * rank_feat[:, None, :]
    ).reshape(tok_count, adapter_number * rank_total_width)
    adapter_column_set = jnp.einsum(
        "iu,pdu->ipd", broadcast_result, adapter_up_maps, preferred_element_type=jnp.float32
    )
    positions = jnp.arange(tok_count, dtype=jnp.int32)
    lengths_row = request_token_lengths[0]
    starts = jnp.cumsum(lengths_row) - lengths_row
    member = (positions[:, None] >= starts[None, :]) & (
        positions[:, None] < (starts + lengths_row)[None, :]
    )
    member_int = member.astype(jnp.int32)
    request_of = jnp.sum(member_int * jnp.arange(req_per_dev, dtype=jnp.int32)[None, :], axis=1)
    relative = positions - jnp.sum(member_int * starts[None, :], axis=1)
    tenant_hot = (
        request_tenant_index[:, None]
        == jnp.arange(tenant_adapter_scale.shape[0], dtype=jnp.int32)[None, :]
    ).astype(jnp.float32)
    request_scale = jnp.sum(tenant_hot * tenant_adapter_scale[None, :], axis=1)
    per_token_scale = jnp.sum(member.astype(jnp.float32) * request_scale[None, :], axis=1)[:, None]
    query_rows = (projected_rows[0] + per_token_scale * adapter_column_set[:, 0]).astype(
        jnp.bfloat16
    )
    key_rows = projected_rows[1].astype(jnp.bfloat16)
    value_row_block = (projected_rows[2] + per_token_scale * adapter_column_set[:, 1]).astype(
        jnp.bfloat16
    )
    owner_column = last_page_holder[:, 0]
    owner_table = owner_column.reshape(req_devices, req_per_dev)
    slot_table = holder_page_slot.reshape(req_devices, req_per_dev)
    owned = (owner_table == req_index).astype(jnp.int32)
    owned_rank = jnp.cumsum(owned, axis=1) - 1
    picked = owned[:, None, :] * (
        owned_rank[:, None, :] == jnp.arange(cap_slots, dtype=jnp.int32)[None, :, None]
    ).astype(jnp.int32)
    send_slot = jnp.sum(picked * slot_table[:, None, :], axis=2)
    fill_table = page_filled_rows.reshape(req_devices, req_per_dev)
    send_fill = jnp.sum(picked * fill_table[:, None, :], axis=2)
    my_owner = lax.dynamic_slice_in_dim(owner_column, req_index * req_per_dev, req_per_dev, 0)
    order_ids = jnp.arange(req_per_dev, dtype=jnp.int32)
    earlier = (my_owner[:, None] == my_owner[None, :]) & (order_ids[:, None] > order_ids[None, :])
    flat_pick = my_owner * cap_slots + jnp.sum(earlier.astype(jnp.int32), axis=1)
    page_inner = prefix_cache_store.shape[1:3]
    page_rows = prefix_cache_store.shape[3]
    source_pages = cut_windows(
        prefix_cache_store,
        jnp.clip(send_slot.reshape(-1), 0, prefix_cache_store.shape[0] - 1),
        send_fill.reshape(-1),
    )
    source_pages = source_pages.reshape((req_devices, cap_slots, WINDOW, 2 * head_column_set))
    arrived = lax.all_to_all(source_pages, "req", split_axis=0, concat_axis=0, tiled=True)
    prefix = jnp.take(
        arrived.reshape((req_devices * cap_slots, WINDOW, 2 * head_column_set)),
        flat_pick,
        axis=0,
        mode="clip",
    )
    key_all = jnp.concatenate(
        [key_rows, prefix[:, :, :head_column_set].reshape(req_per_dev * WINDOW, head_column_set)], axis=0
    )
    value_all = jnp.concatenate(
        [value_row_block, prefix[:, :, head_column_set:].reshape(req_per_dev * WINDOW, head_column_set)], axis=0
    )
    distance = positions[:, None] - positions[None, :]
    local_ok = (request_of[:, None] == request_of[None, :]) & (distance >= 0) & (distance <= WINDOW)
    key_request = jnp.repeat(jnp.arange(req_per_dev, dtype=jnp.int32), WINDOW)
    key_offset = jnp.tile(jnp.arange(WINDOW, dtype=jnp.int32), req_per_dev)
    prefix_ok = (request_of[:, None] == key_request[None, :]) & (
        key_offset[None, :] >= relative[:, None]
    )
    allowed = jnp.concatenate([local_ok, prefix_ok], axis=1)
    query_heads = query_rows.reshape(tok_count, head_local, HEAD_SIZE)
    key_heads = key_all.reshape(-1, head_local, HEAD_SIZE)
    value_heads = value_all.reshape(-1, head_local, HEAD_SIZE)
    scores = jnp.einsum(
        "thd,shd->hts", query_heads, key_heads, preferred_element_type=jnp.float32
    ) * (1.0 / math.sqrt(HEAD_SIZE))
    masked = jnp.where(allowed[None], scores, -1e30)
    row_max = jnp.max(masked, axis=-1, keepdims=True)
    exp_scores = jnp.exp(masked - row_max)
    weights = (exp_scores / jnp.sum(exp_scores, axis=-1, keepdims=True)).astype(jnp.bfloat16)
    mixed = (
        jnp.einsum("hts,shd->thd", weights, value_heads, preferred_element_type=jnp.float32)
        .astype(jnp.bfloat16)
        .reshape(tok_count, head_column_set)
    )
    attn_part = (
        jnp.dot(mixed, head_output_weight, preferred_element_type=jnp.float32)
        .astype(jnp.bfloat16)
        .astype(jnp.float32)
    )
    gain_wide = feedforward_norm_gain.astype(jnp.float32)[None, :]
    attn_full = lax.psum(attn_part.astype(jnp.bfloat16), "mdl").astype(jnp.float32)
    resid_full = (stream.astype(jnp.float32) + attn_full).astype(jnp.bfloat16)
    resid_wide = resid_full.astype(jnp.float32)
    mean_sq = jnp.mean(resid_wide * resid_wide, axis=1, keepdims=True)
    normed = (resid_wide * lax.rsqrt(mean_sq + 1e-06) * gain_wide).astype(jnp.bfloat16)
    resid_mine = lax.dynamic_slice_in_dim(resid_full, mdl_index * row_share, row_share, 0)
    full_mlp = lax.all_gather(feedforward_weight, "req", axis=1, tiled=True)
    gate_part = jnp.dot(normed, full_mlp[0], preferred_element_type=jnp.float32)
    up_part = jnp.dot(normed, full_mlp[1], preferred_element_type=jnp.float32)
    hidden = (jax.nn.silu(gate_part) * up_part).astype(jnp.bfloat16)
    mlp_part = (
        jnp.einsum("tf,df->td", hidden, full_mlp[2], preferred_element_type=jnp.float32)
        .astype(jnp.bfloat16)
        .astype(jnp.float32)
    )
    mlp_mine = lax.psum_scatter(
        mlp_part.astype(jnp.bfloat16), "mdl", scatter_dimension=0, tiled=True
    ).astype(jnp.float32)
    return (resid_mine.astype(jnp.float32) + mlp_mine).astype(jnp.bfloat16)


def solution(mesh):
    return jax.shard_map(
        per_device,
        mesh=mesh,
        in_specs=(
            P("req", None),
            P(None, "mdl", None),
            P("mdl", None),
            P("mdl", None, None),
            P(None, "mdl", None),
            P(),
            P(),
            P(None, "req", "mdl"),
            P("req", None, "mdl", None),
            P("req"),
            P("req", None),
            P("req"),
            P(),
            P(),
            P(),
        ),
        out_specs=P(("req", "mdl"), None),
        check_vma=False,
    )
```

```python
import math

import jax
import jax.numpy as jnp
from jax import lax
from jax.experimental import pallas as pl
from jax.experimental.pallas import tpu as pltpu
from jax.sharding import PartitionSpec as P

HEAD_SIZE = 112
WINDOW = 64


def window_kernel(slot_ref, fill_ref, store_ref, out_ref):
    count = out_ref.shape[0]
    page_rows = store_ref.shape[-1]
    row_ids = lax.broadcasted_iota(jnp.int32, (WINDOW, page_rows), 1)
    out_ids = lax.broadcasted_iota(jnp.int32, (WINDOW, page_rows), 0)

    def pick_rows(i, carry):
        pick = (row_ids == out_ids + (fill_ref[i] - WINDOW)).astype(store_ref.dtype)
        page = store_ref[slot_ref[i]].reshape(-1, page_rows)
        out_ref[i] = lax.dot_general(
            pick, page, (((1,), (1,)), ((), ())), preferred_element_type=jnp.float32
        ).astype(out_ref.dtype)
        return carry

    lax.fori_loop(0, count, pick_rows, 0, unroll=32)


def cut_windows(store, slots, fills):
    count = slots.shape[0]
    parts, width, page_rows = store.shape[1:]
    return pl.pallas_call(
        window_kernel,
        grid_spec=pltpu.PrefetchScalarGridSpec(
            num_scalar_prefetch=2,
            grid=(1,),
            in_specs=[pl.BlockSpec(memory_space=pltpu.VMEM)],
            out_specs=pl.BlockSpec(memory_space=pltpu.VMEM),
        ),
        out_shape=jax.ShapeDtypeStruct((count, WINDOW, parts * width), store.dtype),
    )(slots, fills, store)


def per_device(
    stream,
    attention_projection_weight,
    head_output_weight,
    adapter_down_maps,
    adapter_up_maps,
    tenant_adapter_scale,
    feedforward_norm_gain,
    feedforward_weight,
    prefix_cache_store,
    token_adapter_index,
    request_token_lengths,
    request_tenant_index,
    last_page_holder,
    holder_page_slot,
    page_filled_rows,
):
    tok_count, model_width = stream.shape
    head_column_set = attention_projection_weight.shape[1]
    head_local = head_column_set // HEAD_SIZE
    req_per_dev = request_token_lengths.shape[1]
    rank_total_width = adapter_down_maps.shape[2]
    adapter_number = adapter_up_maps.shape[2] // rank_total_width
    req_devices = lax.axis_size("req")
    req_index = lax.axis_index("req")
    mdl_index = lax.axis_index("mdl")
    row_share = tok_count // lax.axis_size("mdl")
    cap_slots = max(2, (req_per_dev + req_devices - 1) // req_devices + 1)
    projected_rows = jnp.einsum(
        "td,kcd->ktc", stream, attention_projection_weight, preferred_element_type=jnp.float32
    )
    all_onehot = (
        token_adapter_index[:, None] == jnp.arange(adapter_number, dtype=jnp.int32)[None, :]
    )
    holder_count = adapter_down_maps.shape[0]
    holder_rank_rows = jnp.einsum(
        "qf,kfn->qkn", stream, adapter_down_maps, preferred_element_type=jnp.float32
    )
    held_onehot = (
        token_adapter_index[:, None]
        == (mdl_index * holder_count + jnp.arange(holder_count, dtype=jnp.int32))[None, :]
    )
    rank_part = jnp.sum(holder_rank_rows * held_onehot.astype(jnp.float32)[:, :, None], axis=1)
    rank_feat = lax.psum(rank_part.astype(jnp.bfloat16), "mdl")
    broadcast_result = (
        all_onehot.astype(jnp.bfloat16)[:, :, None] * rank_feat[:, None, :]
    ).reshape(tok_count, adapter_number * rank_total_width)
    adapter_column_set = jnp.einsum(
        "iu,pdu->ipd", broadcast_result, adapter_up_maps, preferred_element_type=jnp.float32
    )
    positions = jnp.arange(tok_count, dtype=jnp.int32)
    lengths_row = request_token_lengths[0]
    starts = jnp.cumsum(lengths_row) - lengths_row
    member = (positions[:, None] >= starts[None, :]) & (
        positions[:, None] < (starts + lengths_row)[None, :]
    )
    member_int = member.astype(jnp.int32)
    request_of = jnp.sum(member_int * jnp.arange(req_per_dev, dtype=jnp.int32)[None, :], axis=1)
    relative = positions - jnp.sum(member_int * starts[None, :], axis=1)
    tenant_hot = (
        request_tenant_index[:, None]
        == jnp.arange(tenant_adapter_scale.shape[0], dtype=jnp.int32)[None, :]
    ).astype(jnp.float32)
    request_scale = jnp.sum(tenant_hot * tenant_adapter_scale[None, :], axis=1)
    per_token_scale = jnp.sum(member.astype(jnp.float32) * request_scale[None, :], axis=1)[:, None]
    query_rows = (projected_rows[0] + per_token_scale * adapter_column_set[:, 0]).astype(
        jnp.bfloat16
    )
    key_rows = projected_rows[1].astype(jnp.bfloat16)
    value_row_block = (projected_rows[2] + per_token_scale * adapter_column_set[:, 1]).astype(
        jnp.bfloat16
    )
    owner_column = last_page_holder[:, 0]
    owner_table = owner_column.reshape(req_devices, req_per_dev)
    slot_table = holder_page_slot.reshape(req_devices, req_per_dev)
    owned = (owner_table == req_index).astype(jnp.int32)
    owned_rank = jnp.cumsum(owned, axis=1) - 1
    picked = owned[:, None, :] * (
        owned_rank[:, None, :] == jnp.arange(cap_slots, dtype=jnp.int32)[None, :, None]
    ).astype(jnp.int32)
    send_slot = jnp.sum(picked * slot_table[:, None, :], axis=2)
    fill_table = page_filled_rows.reshape(req_devices, req_per_dev)
    send_fill = jnp.sum(picked * fill_table[:, None, :], axis=2)
    my_owner = lax.dynamic_slice_in_dim(owner_column, req_index * req_per_dev, req_per_dev, 0)
    order_ids = jnp.arange(req_per_dev, dtype=jnp.int32)
    earlier = (my_owner[:, None] == my_owner[None, :]) & (order_ids[:, None] > order_ids[None, :])
    flat_pick = my_owner * cap_slots + jnp.sum(earlier.astype(jnp.int32), axis=1)
    page_inner = prefix_cache_store.shape[1:3]
    page_rows = prefix_cache_store.shape[3]
    source_pages = cut_windows(
        prefix_cache_store,
        jnp.clip(send_slot.reshape(-1), 0, prefix_cache_store.shape[0] - 1),
        send_fill.reshape(-1),
    )
    source_pages = source_pages.reshape((req_devices, cap_slots, WINDOW, 2 * head_column_set))
    arrived = lax.all_to_all(source_pages, "req", split_axis=0, concat_axis=0, tiled=True)
    prefix = jnp.take(
        arrived.reshape((req_devices * cap_slots, WINDOW, 2 * head_column_set)),
        flat_pick,
        axis=0,
        mode="clip",
    )
    key_all = jnp.concatenate(
        [key_rows, prefix[:, :, :head_column_set].reshape(req_per_dev * WINDOW, head_column_set)], axis=0
    )
    value_all = jnp.concatenate(
        [value_row_block, prefix[:, :, head_column_set:].reshape(req_per_dev * WINDOW, head_column_set)], axis=0
    )
    distance = positions[:, None] - positions[None, :]
    local_ok = (request_of[:, None] == request_of[None, :]) & (distance >= 0) & (distance <= WINDOW)
    key_request = jnp.repeat(jnp.arange(req_per_dev, dtype=jnp.int32), WINDOW)
    key_offset = jnp.tile(jnp.arange(WINDOW, dtype=jnp.int32), req_per_dev)
    prefix_ok = (request_of[:, None] == key_request[None, :]) & (
        key_offset[None, :] >= relative[:, None]
    )
    allowed = jnp.concatenate([local_ok, prefix_ok], axis=1)
    query_heads = query_rows.reshape(tok_count, head_local, HEAD_SIZE)
    key_heads = key_all.reshape(-1, head_local, HEAD_SIZE)
    value_heads = value_all.reshape(-1, head_local, HEAD_SIZE)
    scores = jnp.einsum(
        "thd,shd->hts", query_heads, key_heads, preferred_element_type=jnp.float32
    ) * (1.0 / math.sqrt(HEAD_SIZE))
    masked = jnp.where(allowed[None], scores, -1e30)
    row_max = jnp.max(masked, axis=-1, keepdims=True)
    exp_scores = jnp.exp(masked - row_max)
    weights = (exp_scores / jnp.sum(exp_scores, axis=-1, keepdims=True)).astype(jnp.bfloat16)
    mixed = (
        jnp.einsum("hts,shd->thd", weights, value_heads, preferred_element_type=jnp.float32)
        .astype(jnp.bfloat16)
        .reshape(tok_count, head_column_set)
    )
    attn_part = (
        jnp.dot(mixed, head_output_weight, preferred_element_type=jnp.float32)
        .astype(jnp.bfloat16)
        .astype(jnp.float32)
    )
    gain_wide = feedforward_norm_gain.astype(jnp.float32)[None, :]
    attn_full = lax.psum(attn_part.astype(jnp.bfloat16), "mdl").astype(jnp.float32)
    resid_full = (stream.astype(jnp.float32) + attn_full).astype(jnp.bfloat16)
    resid_wide = resid_full.astype(jnp.float32)
    mean_sq = jnp.mean(resid_wide * resid_wide, axis=1, keepdims=True)
    normed = (resid_wide * lax.rsqrt(mean_sq + 1e-06) * gain_wide).astype(jnp.bfloat16)
    resid_mine = lax.dynamic_slice_in_dim(resid_full, mdl_index * row_share, row_share, 0)
    full_mlp = lax.all_gather(feedforward_weight, "req", axis=1, tiled=True)
    gate_part = jnp.dot(normed, full_mlp[0], preferred_element_type=jnp.float32)
    up_part = jnp.dot(normed, full_mlp[1], preferred_element_type=jnp.float32)
    hidden = (jax.nn.silu(gate_part) * up_part).astype(jnp.bfloat16)
    mlp_part = (
        jnp.einsum("tf,df->td", hidden, full_mlp[2], preferred_element_type=jnp.float32)
        .astype(jnp.bfloat16)
        .astype(jnp.float32)
    )
    mlp_mine = lax.psum_scatter(
        mlp_part.astype(jnp.bfloat16), "mdl", scatter_dimension=0, tiled=True
    ).astype(jnp.float32)
    return (resid_mine.astype(jnp.float32) + mlp_mine).astype(jnp.bfloat16)


def solution(mesh):
    return jax.shard_map(
        per_device,
        mesh=mesh,
        in_specs=(
            P("req", None),
            P(None, "mdl", None),
            P("mdl", None),
            P("mdl", None, None),
            P(None, "mdl", None),
            P(),
            P(),
            P(None, "req", "mdl"),
            P("req", None, "mdl", None),
            P("req"),
            P("req", None),
            P("req"),
            P(),
            P(),
            P(),
        ),
        out_specs=P(("req", "mdl"), None),
        check_vma=False,
    )
```
